256 devices in a mesh: seq: 16 (over y_hi, z), tp: 16 (over x, y_lo, core).
Axes of the slice: x: 4, y: 4 (y_hi: 2, y_lo: 2; y = y_hi * 2 + y_lo), z: 8, core: 2. Of those that a mesh axis runs over, the one named last changes fastest.
Arguments:
- tokens: bfloat16 [65536, 1024], P(('seq', 'tp')), may hold values from -6 to 6
- fine_gain: float32 [1024], replicated, may hold values from 0.1 to 1.9
- fine_query: bfloat16 [1024, 1024], replicated, may hold values from -2.0625 to 2.0625
- fine_keyval: bfloat16 [1024, 2048], replicated, may hold values from -0.125 to 0.125
- fine_out: bfloat16 [1024, 1024], replicated, may hold values from -0.1875 to 0.1875
- down_weight: bfloat16 [1024, 4096], P(None, 'tp'), may hold values from -0.1875 to 0.1875
- coarse_gain: float32 [4096], replicated, may hold values from 0.1 to 1.9
- coarse_query: bfloat16 [4096, 4096], P('seq', 'tp'), may hold values from -1.03125 to 1.03125
- coarse_keyval: bfloat16 [4096, 2, 4096], P('seq', None, 'tp'), may hold values from -0.0625 to 0.0625
- coarse_out: bfloat16 [4096, 4096], P('tp'), may hold values from -0.09375 to 0.09375
- up_weight: bfloat16 [4096, 1024], P('tp'), may hold values from -0.09375 to 0.09375
Outputs:
- result: bfloat16 [65536, 1024], P(('seq', 'tp'))
The draws below stay inside these ranges and needn't reach their ends.
All inputs are finite; a program needn't handle non-finite values.
Results may differ from the reference program's by a relative error of at most 0.02.
Values may be sent and summed in bfloat16 or wider, within the bound.
No kernel may reach another device: no remote copies, remote signals or barrier semaphores. Data moves between devices by JAX's collectives and lax.ppermute only.
A program may use at most 192 MiB of HBM per device.

```python
import math
import jax
import jax.numpy as jnp
from jax import lax

D_FINE = 1024
D_COARSE = 4096
HEAD = 128
WINDOW = 256
SHORT = 8
TOKENS = 65536


def paired_weights(key, marker, rows, cols, spread):
    base = jax.random.fold_in(key, marker)
    first, second, third = jax.random.split(base, 3)
    root = jnp.sqrt(jnp.float32(rows))
    key_part = jax.random.truncated_normal(first, -4.0, 4.0, (rows, cols), jnp.float32) / root
    value_part = jax.random.truncated_normal(second, -4.0, 4.0, (rows, cols), jnp.float32) / root
    query_part = jax.random.truncated_normal(third, -4.0, 4.0, (rows, cols), jnp.float32) / root
    query_part = spread * query_part
    return (query_part, key_part, value_part)


def draw_fine_query(key, part):
    return paired_weights(key, 11, D_FINE, D_FINE, 1.0)[0].astype(jnp.bfloat16)


def draw_fine_keyval(key, part):
    drawn = paired_weights(key, 11, D_FINE, D_FINE, 1.0)
    return jnp.concatenate([drawn[1], drawn[2]], 1).astype(jnp.bfloat16)


def draw_coarse_query(key, part):
    return paired_weights(key, 23, D_COARSE, D_COARSE, 3.0)[0].astype(jnp.bfloat16)


def draw_coarse_keyval(key, part):
    drawn = paired_weights(key, 23, D_COARSE, D_COARSE, 3.0)
    return jnp.stack([drawn[1], drawn[2]], 1).astype(jnp.bfloat16)


def level_of(key, extent, cuts, smallest, high):
    gain, own = 1.0, jax.random.fold_in(key, 6)
    for dim, parts in cuts:
        draws = jnp.exp(jax.random.uniform(jax.random.fold_in(own, dim), (parts,), jnp.float32, smallest / len(cuts), high / len(cuts)))
        gain = gain * jnp.repeat(draws, extent[dim] // parts).reshape([-1 if axis == dim else 1 for axis in range(len(extent))])
    return gain


def noise(rng, dims, deviation, bound, cuts=(), kind=jnp.bfloat16):
    factor_of = level_of(rng, dims, cuts, -0.22, 0.18) if cuts else 1.0
    values = jax.random.normal(rng, dims, jnp.float32) * deviation * factor_of
    return jnp.minimum(jnp.maximum(values, -bound), bound).astype(kind)


def setup_inputs(seed: int = 0) -> dict:
    key_list = jax.random.split(jax.random.key(seed), 12)
    tokens = noise(key_list[0], (TOKENS, D_FINE), 1.0, 6.0, ((0, 256),))
    fine_gain = jnp.clip(1.0 + 0.18 * jax.random.normal(key_list[1], (D_FINE,), jnp.float32), 0.1, 1.9)
    fine_query = draw_fine_query(jax.random.fold_in(key_list[11], 71), 0)
    fine_keyval = draw_fine_keyval(jax.random.fold_in(key_list[11], 71), 0)
    fine_out = noise(key_list[4], (D_FINE, D_FINE), D_FINE ** -0.5, 0.1875)
    down_weight = noise(key_list[5], (D_FINE, D_COARSE), D_FINE ** -0.5, 0.1875, ((1, 16),))
    coarse_gain = jnp.clip(1.0 + 0.18 * jax.random.normal(key_list[6], (D_COARSE,), jnp.float32), 0.1, 1.9)
    coarse_query = draw_coarse_query(jax.random.fold_in(key_list[11], 71), 0)
    coarse_keyval = draw_coarse_keyval(jax.random.fold_in(key_list[11], 71), 0)
    coarse_out = noise(key_list[9], (D_COARSE, D_COARSE), D_COARSE ** -0.5, 0.09375, ((0, 16),))
    up_weight = noise(key_list[10], (D_COARSE, D_FINE), D_COARSE ** -0.5, 0.09375, ((0, 16),))
    return dict(tokens=tokens, fine_gain=fine_gain, fine_query=fine_query, fine_keyval=fine_keyval, fine_out=fine_out, down_weight=down_weight, coarse_gain=coarse_gain, coarse_query=coarse_query, coarse_keyval=coarse_keyval, coarse_out=coarse_out, up_weight=up_weight)


epsilon = 1e-06
big_negative = -1e+30

def normalize(values, scale_gain):
    mean_square = lax.optimization_barrier(jnp.mean(values * values, axis=-1, keepdims=True))
    return values * lax.rsqrt(mean_square + epsilon) * scale_gain

def fine_attention(queries, keyvals):
    total_rows = queries.shape[0]
    heads = D_FINE // HEAD
    scale = 1.0 / math.sqrt(HEAD)
    query_heads = queries.reshape(total_rows, heads, HEAD)
    padded = jnp.concatenate([jnp.zeros((WINDOW, 2 * D_FINE), jnp.bfloat16), keyvals], 0)

    def block_step(block):
        first = block * WINDOW
        query_block = lax.dynamic_slice_in_dim(query_heads, first, WINDOW, 0)
        key_block = lax.dynamic_slice_in_dim(padded, first, 2 * WINDOW, 0)
        key_heads = key_block[:, :D_FINE].reshape(2 * WINDOW, heads, HEAD)
        value_heads = key_block[:, D_FINE:].reshape(2 * WINDOW, heads, HEAD)
        scores = jnp.einsum('qhd,khd->hqk', query_block.astype(jnp.float32), key_heads.astype(jnp.float32)) * scale
        row_index = jnp.arange(WINDOW, dtype=jnp.int32)[:, None]
        col_index = jnp.arange(2 * WINDOW, dtype=jnp.int32)[None, :]
        offset = row_index + WINDOW - col_index
        allowed = (offset >= 0) & (offset < WINDOW) & (first - WINDOW + col_index >= 0)
        scores = jnp.where(allowed[None], scores, big_negative)
        peak = lax.optimization_barrier(jnp.max(scores, axis=-1, keepdims=True))
        terms = jnp.where(allowed[None], jnp.exp(scores - peak), 0.0)
        denom = lax.optimization_barrier(jnp.sum(terms, axis=-1))
        weights = terms.astype(jnp.bfloat16).astype(jnp.float32)
        mixed = jnp.einsum('hqk,khd->hqd', weights, value_heads.astype(jnp.float32)) / denom[..., None]
        return jnp.transpose(mixed, (1, 0, 2)).reshape(WINDOW, D_FINE).astype(jnp.bfloat16)
    blocks = lax.map(block_step, jnp.arange(total_rows // WINDOW, dtype=jnp.int32))
    return blocks.reshape(total_rows, D_FINE)

def coarse_attention(queries, keyvals):
    count = queries.shape[0]
    heads = D_COARSE // HEAD
    scale = 1.0 / math.sqrt(HEAD)
    block = 1024 if count % 1024 == 0 else count

    def head_step(head):
        query_head = lax.dynamic_slice_in_dim(queries, head * HEAD, HEAD, 1).astype(jnp.float32)
        key_head = lax.dynamic_slice_in_dim(keyvals, head * HEAD, HEAD, 1).astype(jnp.float32)
        value_head = lax.dynamic_slice_in_dim(keyvals, D_COARSE + head * HEAD, HEAD, 1).astype(jnp.float32)

        def query_step(index):
            first = index * block
            query_block = lax.dynamic_slice_in_dim(query_head, first, block, 0)
            scores = jnp.dot(query_block, key_head.T) * scale
            row_index = first + jnp.arange(block, dtype=jnp.int32)[:, None]
            col_index = jnp.arange(count, dtype=jnp.int32)[None, :]
            allowed = col_index <= row_index
            scores = jnp.where(allowed, scores, big_negative)
            peak = lax.optimization_barrier(jnp.max(scores, axis=-1, keepdims=True))
            terms = jnp.where(allowed, jnp.exp(scores - peak), 0.0)
            denom = lax.optimization_barrier(jnp.sum(terms, axis=-1, keepdims=True))
            weights = terms.astype(jnp.bfloat16).astype(jnp.float32)
            return (jnp.dot(weights, value_head) / denom).astype(jnp.bfloat16)
        outputs = lax.map(query_step, jnp.arange(count // block, dtype=jnp.int32))
        return outputs.reshape(count, HEAD)
    per_head = lax.map(head_step, jnp.arange(heads, dtype=jnp.int32))
    return jnp.transpose(per_head, (1, 0, 2)).reshape(count, D_COARSE)

def reference(tokens, fine_gain, fine_query, fine_keyval, fine_out, down_weight, coarse_gain, coarse_query, coarse_keyval, coarse_out, up_weight):
    inputs = tokens.astype(jnp.float32)
    normed = normalize(inputs, fine_gain).astype(jnp.bfloat16)
    queries = jnp.dot(normed, fine_query, preferred_element_type=jnp.float32).astype(jnp.bfloat16)
    keyvals = jnp.dot(normed, fine_keyval, preferred_element_type=jnp.float32).astype(jnp.bfloat16)
    local = fine_attention(queries, keyvals)
    fine_state = (inputs + jnp.dot(local, fine_out, preferred_element_type=jnp.float32)).astype(jnp.bfloat16)
    count = fine_state.shape[0] // SHORT
    pooled = lax.optimization_barrier(jnp.mean(fine_state.astype(jnp.float32).reshape(count, SHORT, D_FINE), axis=1)).astype(jnp.bfloat16)
    shortened = jnp.dot(pooled, down_weight, preferred_element_type=jnp.float32).astype(jnp.bfloat16)
    coarse_normed = normalize(shortened.astype(jnp.float32), coarse_gain).astype(jnp.bfloat16)
    coarse_queries = jnp.dot(coarse_normed, coarse_query, preferred_element_type=jnp.float32).astype(jnp.bfloat16)
    coarse_kv = jnp.dot(coarse_normed, coarse_keyval.reshape(D_COARSE, 2 * D_COARSE), preferred_element_type=jnp.float32).astype(jnp.bfloat16)
    coarse_heads = coarse_attention(coarse_queries, coarse_kv)
    coarse_state = (shortened.astype(jnp.float32) + jnp.dot(coarse_heads, coarse_out, preferred_element_type=jnp.float32)).astype(jnp.bfloat16)
    delayed = jnp.concatenate([jnp.zeros((1, D_COARSE), jnp.bfloat16), coarse_state[:-1]], 0)
    lifted = jnp.dot(delayed, up_weight, preferred_element_type=jnp.float32)
    result = fine_state.astype(jnp.float32) + jnp.repeat(lifted, SHORT, axis=0)
    return result.astype(jnp.bfloat16)
```

```python
import functools
import math

import jax
import jax.numpy as jnp
from jax import lax
from jax.experimental import pallas as pl
from jax.experimental.pallas import tpu as pltpu
from jax.sharding import Mesh, PartitionSpec as P

HEAD = 128
WINDOW = 256
SHORT = 8

epsilon = 1e-06
big_negative = -1e30

ALL = ("yh", "z", "x", "yl", "c")
SEQ = ("yh", "z")
TP = ("x", "yl", "c")
f32 = jnp.float32
bf16 = jnp.bfloat16


def from_behind(array, axis, by):
    size = lax.axis_size(axis)
    pairs = [(i, i + by) for i in range(size) if 0 <= i + by < size]
    return lax.ppermute(array, axis, pairs)


def rotated(array, axis, by):
    size = lax.axis_size(axis)
    return lax.ppermute(array, axis, [(i, (i + by) % size) for i in range(size)])


def gathered(array, axes):
    copies = jnp.broadcast_to(array, (lax.axis_size(axes), *array.shape))
    return lax.all_to_all(copies, axes, split_axis=0, concat_axis=0, tiled=True)


def exchanged(pieces, axes):
    return lax.all_to_all(pieces, axes, split_axis=0, concat_axis=0, tiled=True)


def normalize(values, scale_gain):
    mean_square = jnp.mean(values * values, axis=-1, keepdims=True)
    return values * lax.rsqrt(mean_square + epsilon) * scale_gain


def dot(a, b):
    return jnp.dot(a, b, preferred_element_type=f32)


def fine_layer(tokens, fine_gain, fine_query, fine_keyval, fine_out):
    tok_rows, width = tokens.shape
    fine_heads = width // HEAD
    scale = 1.0 / math.sqrt(HEAD)
    start_row = lax.axis_index(ALL) * tok_rows
    inputs = tokens.astype(f32)
    normed = normalize(inputs, fine_gain).astype(bf16)
    queries = dot(normed, fine_query).astype(bf16)
    keyvals = dot(normed, fine_keyval).astype(bf16)
    earlier_rows = from_behind(normed, ALL, 1)
    earlier = dot(earlier_rows, fine_keyval).astype(bf16)
    key_rows = jnp.concatenate([earlier, keyvals], 0)
    span = key_rows.shape[0]
    key_heads = key_rows[:, :width].reshape(span, fine_heads, HEAD)
    value_heads = key_rows[:, width:].reshape(span, fine_heads, HEAD)
    query_heads = queries.reshape(tok_rows, fine_heads, HEAD)
    scores = jnp.einsum("qhd,khd->hqk", query_heads, key_heads, preferred_element_type=f32) * scale
    row_index = jnp.arange(tok_rows, dtype=jnp.int32)[:, None]
    col_index = jnp.arange(span, dtype=jnp.int32)[None, :]
    offset = row_index + WINDOW - col_index
    allowed = (offset >= 0) & (offset < WINDOW) & (start_row - WINDOW + col_index >= 0)
    scores = jnp.where(allowed[None], scores, big_negative)
    peak = jnp.max(scores, axis=-1, keepdims=True)
    terms = jnp.where(allowed[None], jnp.exp(scores - peak), 0.0)
    denom = jnp.sum(terms, axis=-1)
    mixed = jnp.einsum("hqk,khd->qhd", terms.astype(bf16), value_heads, preferred_element_type=f32)
    local = (mixed / jnp.transpose(denom)[..., None]).reshape(tok_rows, width).astype(bf16)
    return (inputs + dot(local, fine_out)).astype(bf16)


def attention_kernel(place_ref, q_ref, *refs):
    chunks, out_ref = refs[:-1], refs[-1]
    tile = q_ref.shape[0]
    step = pl.program_id(0)
    q = q_ref[...]
    row = step * tile + lax.broadcasted_iota(jnp.int32, (tile, tile), 0)
    col = step * tile + lax.broadcasted_iota(jnp.int32, (tile, tile), 1)

    def position(index):
        return (index >> 6) * 512 + ((index >> 5) & 1) * 64 + (index & 31)

    ahead = position(row) - position(col)

    def update(state, kt, masked):
        peak, total, acc = state
        rows = pl.ds(pl.multiple_of(kt * tile, tile), tile)
        scores = []
        for j, chunk in enumerate(chunks):
            s = lax.dot_general(
                q, chunk[rows, :HEAD], (((1,), (1,)), ((), ())), preferred_element_type=f32
            )
            if masked:
                s = jnp.where(ahead > place_ref[j], s, big_negative)
            scores.append(s)
        top = functools.reduce(jnp.maximum, scores)
        new_peak = jnp.maximum(peak, jnp.max(top, axis=-1, keepdims=True))
        fade = jnp.exp2(peak - new_peak)
        acc = acc * fade
        sums = None
        for j, chunk in enumerate(chunks):
            p = jnp.exp2(scores[j] - new_peak)
            if masked:
                p = jnp.where(ahead > place_ref[j], p, 0.0)
            sums = p if sums is None else sums + p
            acc = acc + dot(p.astype(bf16), chunk[rows, HEAD:])
        total = total * fade + jnp.sum(sums, axis=-1, keepdims=True)
        return new_peak, total, acc

    state = (
        jnp.full((tile, 1), big_negative, f32),
        jnp.zeros((tile, 1), f32),
        jnp.zeros((tile, HEAD), f32),
    )
    state = lax.fori_loop(0, step, lambda kt, st: update(st, kt, False), state)
    _, total, acc = update(state, step, True)
    out_ref[...] = (acc / jnp.where(total > 0.0, total, 1.0)).astype(bf16)


def coarse_attention(q, chunks, places, tile=256):
    rows = q.shape[0]
    whole = pl.BlockSpec(chunks[0].shape, lambda i, place: (0, 0))
    return pl.pallas_call(
        attention_kernel,
        out_shape=jax.ShapeDtypeStruct((rows, HEAD), bf16),
        grid_spec=pltpu.PrefetchScalarGridSpec(
            num_scalar_prefetch=1,
            grid=(rows // tile,),
            in_specs=[pl.BlockSpec((tile, HEAD), lambda i, place: (i, 0))] + [whole] * len(chunks),
            out_specs=pl.BlockSpec((tile, HEAD), lambda i, place: (i, 0)),
        ),
        compiler_params=pltpu.CompilerParams(vmem_limit_bytes=48 << 20),
    )(places, q, *chunks)


def in_lanes(array):
    rows, cols = array.shape
    return jnp.transpose(array.reshape(rows, cols // 128, 128), (1, 0, 2)).reshape(-1, 128)


def out_of_lanes(array, rows):
    n = array.shape[-2] // rows
    parts = array.reshape(*array.shape[:-2], n, rows, 128)
    parts = jnp.swapaxes(parts, -3, -2)
    return parts.reshape(*array.shape[:-2], rows, n * 128)


def summed_piece(partial):
    core = lax.axis_index("c")
    heads, rows, _ = partial.shape
    parts = partial.reshape(heads, 2, 4, rows // 8, 128)
    keep = lax.dynamic_index_in_dim(parts, core, 1, keepdims=False)
    give = lax.dynamic_index_in_dim(parts, 1 - core, 1, keepdims=False)
    got = rotated(give.astype(bf16), "c", 1)
    both = (keep + got.astype(f32)).astype(bf16)
    pieces = jnp.swapaxes(both, 0, 1).reshape(8, rows // 8, 128)
    pieces = exchanged(pieces, ("x", "yl"))
    return jnp.sum(pieces.astype(f32), axis=0).astype(bf16)


def body(
    tokens,
    fine_gain,
    fine_query,
    fine_keyval,
    fine_out,
    down_weight,
    coarse_gain,
    coarse_query,
    coarse_keyval,
    coarse_out,
    up_weight,
):
    width = tokens.shape[1]
    wide = coarse_gain.shape[0]
    cols = coarse_query.shape[1]
    yh, z, x, yl, c = (lax.axis_index(a) for a in ALL)
    s, t = lax.axis_index(SEQ), lax.axis_index(TP)
    n_seq, n_tp = lax.axis_size(SEQ), lax.axis_size(TP)
    swap = [(b * n_tp + a, a * n_tp + b) for a in range(n_seq) for b in range(n_tp)]

    with jax.named_scope("weights"):
        rows_sent = jnp.concatenate([coarse_query, coarse_keyval[:, 0], coarse_keyval[:, 1]], 1)
        rows_here = lax.ppermute(rows_sent, ALL, swap)
        out_sent = lax.dynamic_slice(coarse_out, (0, s * cols), (cols, cols))
        out_here = lax.ppermute(out_sent, ALL, swap)

    fine_state = fine_layer(tokens, fine_gain, fine_query, fine_keyval, fine_out)
    run_count = tokens.shape[0] // SHORT
    pooled = jnp.mean(fine_state.astype(f32).reshape(run_count, SHORT, width), axis=1).astype(bf16)

    with jax.named_scope("gather_rows"):
        row_before = from_behind(pooled[run_count - 1 :], ALL, 1)
        z_rows = gathered(pooled, ("z",))
        z_before = gathered(row_before, ("z",))
        all_rows = gathered(z_rows, ("yh", "yl")).reshape(-1, width)
        all_before = gathered(z_before, ("yh", "yl")).reshape(-1, width)

    with jax.named_scope("weights"):
        gain = lax.dynamic_slice(coarse_gain, (t * cols,), (cols,))
        scaled = (rows_here.astype(f32) * gain[:, None]).astype(bf16)
        part = dot(down_weight, scaled)
        slot_rows = lax.dynamic_slice(down_weight, (128 * z + 64 * yh, 0), (64, cols))
        gram = lax.dot_general(
            slot_rows, down_weight, (((1,), (1,)), ((), ())), preferred_element_type=f32
        )
        first = jnp.stack(
            [
                jnp.concatenate(
                    [part[:, j * cols + k * HEAD : j * cols + (k + 1) * HEAD] for j in range(3)]
                    + [in_lanes(gram[32 * k : 32 * k + 32])],
                    0,
                )
                for k in range(2)
            ]
        )
        first = gathered(summed_piece(first), ("x", "c"))
        first = jnp.swapaxes(first.reshape(4, 2, -1, 128), 0, 1).reshape(-1, 128)
        proj = out_of_lanes(first[: 3 * width], width)
        gram_slot = out_of_lanes(first[3 * width :], 32)
        after = dot(out_here, up_weight)
        direct = dot(slot_rows, up_weight)
        second = jnp.stack(
            [
                jnp.concatenate(
                    [
                        in_lanes(after[HEAD * k : HEAD * (k + 1)]),
                        in_lanes(direct[32 * k : 32 * k + 32]),
                    ],
                    0,
                )
                for k in range(2)
            ]
        )
        second = gathered(summed_piece(second), ("yh", "yl", "x", "c"))
        second = jnp.swapaxes(second.reshape(4, 4, 2, -1, 128), 1, 2).reshape(4, -1, 128)
        after_all = out_of_lanes(second[:, :width], HEAD).reshape(4 * HEAD, width)
        direct_all = out_of_lanes(second[:, width:], 32).reshape(HEAD, width)

    with jax.named_scope("project"):
        y = yh * 2 + yl
        rows_slot = lax.dynamic_slice(all_rows, (0, 128 * z + 32 * y), (all_rows.shape[0], 32))
        before_slot = lax.dynamic_slice(
            all_before, (0, 128 * z + 32 * y), (all_before.shape[0], 32)
        )

        def square_part(rows, slot):
            product = lax.dot_general(
                rows, gram_slot, (((1,), (1,)), ((), ())), preferred_element_type=f32
            )
            return jnp.sum(product * slot.astype(f32), axis=-1)

        squares = jnp.concatenate(
            [square_part(all_rows, rows_slot), square_part(all_before, before_slot)]
        )
        squares = jnp.sum(gathered(squares[None], ("yh", "yl", "z")), axis=(0, 1))
        inverse = lax.rsqrt(jnp.maximum(squares, 0.0) / wide + epsilon)[:, None]
        n = all_rows.shape[0]
        qkv = dot(all_rows, proj)
        q_before = dot(all_before, proj[:, :HEAD])
        factor = math.log2(math.e) / math.sqrt(HEAD)

        def by_row(values):
            parts = values.reshape(2, 2, 8, run_count, values.shape[-1])
            return jnp.swapaxes(parts, 1, 2).reshape(n, values.shape[-1])

        kv = by_row((qkv[:, HEAD:] * inverse[:n]).astype(bf16))
        q = (qkv[:, :HEAD] * (inverse[:n] * factor)).reshape(-1, run_count, HEAD)
        q_before = (q_before * (inverse[n:] * factor)).reshape(-1, 1, HEAD)
        q = jnp.concatenate([q_before, q[:, : run_count - 1]], 1).astype(bf16).reshape(n, HEAD)
        q = by_row(q)

    with jax.named_scope("attention"):
        chunks, places = [], []
        for by in (0, 1, 3, 2):
            mine = kv if by == 0 else rotated(kv, "x", by)
            other = rotated(mine, "c", 1)
            shift = 128 * ((x + 4 - by) % 4 - x)
            chunks += [mine, other]
            places += [shift, shift + 32 * (1 - 2 * c)]
        heads = coarse_attention(q, chunks, jnp.stack(places).astype(jnp.int32))

    with jax.named_scope("lift"):
        heads = jnp.swapaxes(heads.reshape(2, 8, 2, run_count, HEAD), 1, 2)
        heads = exchanged(heads.reshape(4, 8 * run_count, HEAD), ("yh", "yl"))
        heads = jnp.swapaxes(heads, 0, 1).reshape(8 * run_count, 4 * HEAD)
        shifted = jnp.concatenate(
            [z_before.reshape(8, 1, width), z_rows.reshape(8, run_count, width)[:, : run_count - 1]],
            1,
        ).reshape(8 * run_count, width)
        shifted = lax.dynamic_slice(shifted, (0, 128 * z), (8 * run_count, HEAD))
        lifted = (dot(heads, after_all) + dot(shifted, direct_all)).astype(bf16)
        lifted = exchanged(lifted.reshape(8, run_count, width), ("z",))
        lifted = jnp.sum(lifted.astype(f32), axis=0)
        result = fine_state.astype(f32) + jnp.repeat(lifted, SHORT, axis=0)
    return result.astype(bf16)


def solution(mesh):
    fine = Mesh(mesh.devices.reshape(2, 8, 4, 2, 2), ALL)
    return jax.shard_map(
        body,
        mesh=fine,
        in_specs=(
            P(ALL, None),
            P(),
            P(),
            P(),
            P(),
            P(None, TP),
            P(),
            P(SEQ, TP),
            P(SEQ, None, TP),
            P(TP, None),
            P(TP, None),
        ),
        out_specs=P(ALL, None),
        check_vma=False,
    )
```

```python
import functools
import math

import jax
import jax.numpy as jnp
from jax import lax
from jax.experimental import pallas as pl
from jax.experimental.pallas import tpu as pltpu
from jax.sharding import Mesh, PartitionSpec as P

HEAD = 128
WINDOW = 256
SHORT = 8

epsilon = 1e-06
big_negative = -1e30

ALL = ("yh", "z", "x", "yl", "c")
SEQ = ("yh", "z")
TP = ("x", "yl", "c")
f32 = jnp.float32
bf16 = jnp.bfloat16


def from_behind(array, axis, by):
    size = lax.axis_size(axis)
    pairs = [(i, i + by) for i in range(size) if 0 <= i + by < size]
    return lax.ppermute(array, axis, pairs)


def rotated(array, axis, by):
    size = lax.axis_size(axis)
    return lax.ppermute(array, axis, [(i, (i + by) % size) for i in range(size)])


def gathered(array, axes):
    copies = jnp.broadcast_to(array, (lax.axis_size(axes), *array.shape))
    return lax.all_to_all(copies, axes, split_axis=0, concat_axis=0, tiled=True)


def exchanged(pieces, axes):
    return lax.all_to_all(pieces, axes, split_axis=0, concat_axis=0, tiled=True)


def normalize(values, scale_gain):
    mean_square = jnp.mean(values * values, axis=-1, keepdims=True)
    return values * lax.rsqrt(mean_square + epsilon) * scale_gain


def dot(a, b):
    return jnp.dot(a, b, preferred_element_type=f32)


def fine_layer(tokens, fine_gain, fine_query, fine_keyval, fine_out):
    tok_rows, width = tokens.shape
    fine_heads = width // HEAD
    scale = 1.0 / math.sqrt(HEAD)
    start_row = lax.axis_index(ALL) * tok_rows
    inputs = tokens.astype(f32)
    normed = normalize(inputs, fine_gain).astype(bf16)
    queries = dot(normed, fine_query).astype(bf16)
    keyvals = dot(normed, fine_keyval).astype(bf16)
    earlier_rows = from_behind(normed, ALL, 1)
    earlier = dot(earlier_rows, fine_keyval).astype(bf16)
    key_rows = jnp.concatenate([earlier, keyvals], 0)
    span = key_rows.shape[0]
    key_heads = key_rows[:, :width].reshape(span, fine_heads, HEAD)
    value_heads = key_rows[:, width:].reshape(span, fine_heads, HEAD)
    query_heads = queries.reshape(tok_rows, fine_heads, HEAD)
    scores = jnp.einsum("qhd,khd->hqk", query_heads, key_heads, preferred_element_type=f32) * scale
    row_index = jnp.arange(tok_rows, dtype=jnp.int32)[:, None]
    col_index = jnp.arange(span, dtype=jnp.int32)[None, :]
    offset = row_index + WINDOW - col_index
    allowed = (offset >= 0) & (offset < WINDOW) & (start_row - WINDOW + col_index >= 0)
    scores = jnp.where(allowed[None], scores, big_negative)
    peak = jnp.max(scores, axis=-1, keepdims=True)
    terms = jnp.where(allowed[None], jnp.exp(scores - peak), 0.0)
    denom = jnp.sum(terms, axis=-1)
    mixed = jnp.einsum("hqk,khd->qhd", terms.astype(bf16), value_heads, preferred_element_type=f32)
    local = (mixed / jnp.transpose(denom)[..., None]).reshape(tok_rows, width).astype(bf16)
    return (inputs + dot(local, fine_out)).astype(bf16)


def attention_kernel(place_ref, q_ref, *refs):
    chunks, out_ref = refs[:-1], refs[-1]
    tile = q_ref.shape[0]
    step = pl.program_id(0)
    q = q_ref[...]
    row = step * tile + lax.broadcasted_iota(jnp.int32, (tile, tile), 0)
    col = step * tile + lax.broadcasted_iota(jnp.int32, (tile, tile), 1)

    def position(index):
        return (index >> 6) * 512 + ((index >> 5) & 1) * 64 + (index & 31)

    ahead = position(row) - position(col)

    def update(state, kt, masked):
        peak, total, acc = state
        rows = pl.ds(pl.multiple_of(kt * tile, tile), tile)
        scores = []
        for j, chunk in enumerate(chunks):
            s = lax.dot_general(
                q, chunk[rows, :HEAD], (((1,), (1,)), ((), ())), preferred_element_type=f32
            )
            if masked:
                s = jnp.where(ahead >= place_ref[j], s, big_negative)
            scores.append(s)
        top = functools.reduce(jnp.maximum, scores)
        new_peak = jnp.maximum(peak, jnp.max(top, axis=-1, keepdims=True))
        fade = jnp.exp2(peak - new_peak)
        acc = acc * fade
        sums = None
        for j, chunk in enumerate(chunks):
            p = jnp.exp2(scores[j] - new_peak)
            if masked:
                p = jnp.where(ahead >= place_ref[j], p, 0.0)
            sums = p if sums is None else sums + p
            acc = acc + dot(p.astype(bf16), chunk[rows, HEAD:])
        total = total * fade + jnp.sum(sums, axis=-1, keepdims=True)
        return new_peak, total, acc

    state = (
        jnp.full((tile, 1), big_negative, f32),
        jnp.zeros((tile, 1), f32),
        jnp.zeros((tile, HEAD), f32),
    )
    state = lax.fori_loop(0, step, lambda kt, st: update(st, kt, False), state)
    _, total, acc = update(state, step, True)
    out_ref[...] = (acc / total).astype(bf16)


def coarse_attention(q, chunks, places, tile=256):
    rows = q.shape[0]
    whole = pl.BlockSpec(chunks[0].shape, lambda i, place: (0, 0))
    return pl.pallas_call(
        attention_kernel,
        out_shape=jax.ShapeDtypeStruct((rows, HEAD), bf16),
        grid_spec=pltpu.PrefetchScalarGridSpec(
            num_scalar_prefetch=1,
            grid=(rows // tile,),
            in_specs=[pl.BlockSpec((tile, HEAD), lambda i, place: (i, 0))] + [whole] * len(chunks),
            out_specs=pl.BlockSpec((tile, HEAD), lambda i, place: (i, 0)),
        ),
        compiler_params=pltpu.CompilerParams(vmem_limit_bytes=48 << 20),
    )(places, q, *chunks)


def gate(array, earlier):
    return lax.optimization_barrier((array, earlier))[0]


def summed_piece(left, right, pieces):
    core = lax.axis_index("c")
    half = left.shape[0] // 2
    mine = lax.dynamic_slice(left, (core * half, 0), (half, left.shape[1]))
    other = lax.dynamic_slice(left, ((1 - core) * half, 0), (half, left.shape[1]))
    got = rotated(dot(other, right).astype(bf16), "c", 1)
    both = (dot(mine, right) + got.astype(f32)).astype(bf16)
    return jnp.sum(exchanged(pieces(both), ("x", "yl")).astype(f32), axis=0).astype(bf16)


def body(
    tokens,
    fine_gain,
    fine_query,
    fine_keyval,
    fine_out,
    down_weight,
    coarse_gain,
    coarse_query,
    coarse_keyval,
    coarse_out,
    up_weight,
):
    width = tokens.shape[1]
    wide = coarse_gain.shape[0]
    cols = coarse_query.shape[1]
    yh, z, x, yl, c = (lax.axis_index(a) for a in ALL)
    y = yh * 2 + yl
    s, t = lax.axis_index(SEQ), lax.axis_index(TP)
    n_seq, n_tp = lax.axis_size(SEQ), lax.axis_size(TP)
    swap = [(b * n_tp + a, a * n_tp + b) for a in range(n_seq) for b in range(n_tp)]

    with jax.named_scope("weights"):
        three = (coarse_query, coarse_keyval[:, 0], coarse_keyval[:, 1])
        sent = [w[:, k * HEAD : (k + 1) * HEAD] for k in range(2) for w in three]
        rows_here = lax.ppermute(jnp.concatenate(sent, 1), ALL, swap)

    fine_state = fine_layer(tokens, fine_gain, fine_query, fine_keyval, fine_out)
    run_count = tokens.shape[0] // SHORT
    pooled = jnp.mean(fine_state.astype(f32).reshape(run_count, SHORT, width), axis=1).astype(bf16)

    with jax.named_scope("gather_rows"):
        z_rows = gathered(pooled, ("z",)).reshape(-1, width)
        z_count = z_rows.shape[0]
        y_rows = [z_rows] + [rotated(z_rows, ("yh", "yl"), by) for by in (3, 2, 1)]
        all_rows = jnp.concatenate(y_rows, 0)
        n = all_rows.shape[0]

    with jax.named_scope("weights"):
        rows_here = gate(rows_here, pooled)
        gain = lax.dynamic_slice(coarse_gain, (t * cols,), (cols,))
        scaled = (rows_here.astype(f32) * gain[:, None]).astype(bf16)
        gram_rows = jnp.transpose(lax.dynamic_slice(down_weight, (128 * z, 0), (128, cols)))
        half = 3 * HEAD
        right = jnp.concatenate([scaled[:, :half], gram_rows, scaled[:, half:], gram_rows], 1)
        first = summed_piece(
            down_weight,
            right,
            lambda v: jnp.swapaxes(v.reshape(4, 128, 2, 512), 1, 2).reshape(8, 128, 512),
        )
        proj = gathered(first, ("c", "x")).reshape(width, 512)

        out_sent = lax.dynamic_slice(gate(coarse_out, pooled), (0, s * cols), (cols, cols))
        out_here = lax.ppermute(out_sent, ALL, swap)
        slot_rows = lax.dynamic_slice(down_weight, (128 * z + 64 * yh, 0), (64, cols))
        left = jnp.concatenate([out_here[:HEAD], slot_rows[:32], out_here[HEAD:], slot_rows[32:]], 0)
        left = gate(left, first)
        flipped = jnp.transpose(up_weight)
        second = summed_piece(
            flipped,
            jnp.transpose(left),
            lambda v: jnp.swapaxes(v.reshape(4, 128, 2, 160), 1, 2).reshape(8, 128, 160),
        )
        second = gathered(second, ("c", "x")).reshape(width, 160)
        second = lax.all_gather(jnp.transpose(second), ("yh", "yl"), axis=0)

    with jax.named_scope("project"):
        qkv = dot(all_rows, proj)
        slot = lax.dynamic_slice(all_rows, (0, 128 * z), (n, 128))
        squares = jnp.sum(qkv[:, half:] * slot.astype(f32), axis=-1)
        squares = jnp.sum(gathered(squares[None], ("z",)), axis=(0, 1))
        inverse = lax.rsqrt(jnp.maximum(squares, 0.0) / wide + epsilon)

        def by_row(values):
            parts = values.reshape(4, 8, run_count, -1)
            twice = jnp.concatenate([parts, parts[:3]], 0)
            parts = lax.dynamic_slice_in_dim(twice, (4 - y) % 4, 4, 0)
            return jnp.swapaxes(parts.reshape(2, 2, 8, run_count, -1), 1, 2).reshape(n, -1)

        kv = by_row(qkv[:, HEAD:half].astype(bf16))
        inverse = by_row(inverse)
        factor = math.log2(math.e) / math.sqrt(HEAD)
        q = (by_row(qkv[:, :HEAD]) * (inverse * factor)).astype(bf16)
        every_inverse = gathered(inverse.reshape(1, n), ("x", "c")).reshape(4, 2, n, 1)

    with jax.named_scope("attention"):
        chunks, places = [], []
        for by in (0, 1, 3, 2):
            mine = kv if by == 0 else rotated(kv, "x", by)
            other = rotated(mine, "c", 1)
            source = (x + 4 - by) % 4
            shift = 128 * (source - x)
            for chunk, core, place in ((mine, c, shift), (other, 1 - c, shift + 32 * (1 - 2 * c))):
                scale = lax.dynamic_slice(every_inverse, (source, core, 0, 0), (1, 1, n, 1))
                chunks.append((chunk.astype(f32) * scale.reshape(n, 1)).astype(bf16))
                places.append(place)
        heads = coarse_attention(q, chunks, jnp.stack(places).astype(jnp.int32))

    with jax.named_scope("lift"):
        heads = jnp.swapaxes(heads.reshape(2, 8, 2, run_count, HEAD), 1, 2)
        heads = heads.reshape(4, z_count, HEAD)
        total = None
        for by in range(4):
            part = lax.dynamic_index_in_dim(heads, (y + by) % 4, 0, keepdims=False)
            if by:
                part = rotated(part, ("yh", "yl"), by)
            matrix = lax.dynamic_index_in_dim(second, (y + 4 - by) % 4, 0, keepdims=False)
            product = dot(part, matrix[:HEAD])
            total = product if total is None else total + product
        slot = lax.dynamic_slice(z_rows, (0, 128 * z), (z_count, 128))
        total = total + dot(slot, second[:, HEAD:].reshape(128, width))
        lifted = exchanged(total.astype(bf16).reshape(8, run_count, width), ("z",))
        lifted = jnp.sum(lifted.astype(f32), axis=0)
        before = from_behind(lifted[run_count - 1 :], ALL, 1)
        lifted = jnp.concatenate([before, lifted[: run_count - 1]], 0)
        result = fine_state.astype(f32) + jnp.repeat(lifted, SHORT, axis=0)
    return result.astype(bf16)


def solution(mesh):
    fine = Mesh(mesh.devices.reshape(2, 8, 4, 2, 2), ALL)
    return jax.shard_map(
        body,
        mesh=fine,
        in_specs=(
            P(ALL, None),
            P(),
            P(),
            P(),
            P(),
            P(None, TP),
            P(),
            P(SEQ, TP),
            P(SEQ, None, TP),
            P(TP, None),
            P(TP, None),
        ),
        out_specs=P(ALL, None),
        check_vma=False,
    )
```

```python
import functools
import math

import jax
import jax.numpy as jnp
from jax import lax
from jax.experimental import pallas as pl
from jax.experimental.pallas import tpu as pltpu
from jax.sharding import Mesh, PartitionSpec as P

HEAD = 128
WINDOW = 256
SHORT = 8

epsilon = 1e-06
big_negative = -1e30

ALL = ("yh", "z", "x", "yl", "c")
SEQ = ("yh", "z")
TP = ("x", "yl", "c")
f32 = jnp.float32
bf16 = jnp.bfloat16


def from_behind(array, axis, by):
    size = lax.axis_size(axis)
    pairs = [(i, i + by) for i in range(size) if 0 <= i + by < size]
    return lax.ppermute(array, axis, pairs)


def rotated(array, axis, by):
    size = lax.axis_size(axis)
    return lax.ppermute(array, axis, [(i, (i + by) % size) for i in range(size)])


def around_four(array, axes):
    above, below = rotated(array, axes, 3), rotated(array, axes, 1)
    half = array.shape[0] // 2
    top, bottom = rotated(above[:half], axes, 3), rotated(below[half:], axes, 1)
    return [array, above, jnp.concatenate([top, bottom], 0), below]


def gathered(array, axes):
    copies = jnp.broadcast_to(array, (lax.axis_size(axes), *array.shape))
    return lax.all_to_all(copies, axes, split_axis=0, concat_axis=0, tiled=True)


def exchanged(pieces, axes):
    return lax.all_to_all(pieces, axes, split_axis=0, concat_axis=0, tiled=True)


def normalize(values, scale_gain):
    mean_square = jnp.mean(values * values, axis=-1, keepdims=True)
    return values * lax.rsqrt(mean_square + epsilon) * scale_gain


def dot(a, b):
    return jnp.dot(a, b, preferred_element_type=f32)


def fine_layer(tokens, fine_gain, fine_query, fine_keyval, fine_out):
    tok_rows, width = tokens.shape
    fine_heads = width // HEAD
    scale = 1.0 / math.sqrt(HEAD)
    start_row = lax.axis_index(ALL) * tok_rows
    inputs = tokens.astype(f32)
    normed = normalize(inputs, fine_gain).astype(bf16)
    queries = dot(normed, fine_query).astype(bf16)
    keyvals = dot(normed, fine_keyval).astype(bf16)
    earlier_rows = from_behind(normed, ALL, 1)
    earlier = dot(earlier_rows, fine_keyval).astype(bf16)
    key_rows = jnp.concatenate([earlier, keyvals], 0)
    span = key_rows.shape[0]
    key_heads = key_rows[:, :width].reshape(span, fine_heads, HEAD)
    value_heads = key_rows[:, width:].reshape(span, fine_heads, HEAD)
    query_heads = queries.reshape(tok_rows, fine_heads, HEAD)
    scores = jnp.einsum("qhd,khd->hqk", query_heads, key_heads, preferred_element_type=f32) * scale
    row_index = jnp.arange(tok_rows, dtype=jnp.int32)[:, None]
    col_index = jnp.arange(span, dtype=jnp.int32)[None, :]
    offset = row_index + WINDOW - col_index
    allowed = (offset >= 0) & (offset < WINDOW) & (start_row - WINDOW + col_index >= 0)
    scores = jnp.where(allowed[None], scores, big_negative)
    peak = jnp.max(scores, axis=-1, keepdims=True)
    terms = jnp.where(allowed[None], jnp.exp(scores - peak), 0.0)
    denom = jnp.sum(terms, axis=-1)
    mixed = jnp.einsum("hqk,khd->qhd", terms.astype(bf16), value_heads, preferred_element_type=f32)
    local = (mixed / jnp.transpose(denom)[..., None]).reshape(tok_rows, width).astype(bf16)
    return (inputs + dot(local, fine_out)).astype(bf16)


def attention_kernel(place_ref, q_ref, *refs):
    chunks, out_ref = refs[:-1], refs[-1]
    tile = q_ref.shape[0]
    step = pl.program_id(0)
    q = q_ref[...]
    row = step * tile + lax.broadcasted_iota(jnp.int32, (tile, tile), 0)
    col = step * tile + lax.broadcasted_iota(jnp.int32, (tile, tile), 1)

    def position(index):
        return (index >> 6) * 512 + ((index >> 5) & 1) * 64 + (index & 31)

    ahead = position(row) - position(col)

    def update(state, kt, masked):
        peak, total, acc = state
        rows = pl.ds(pl.multiple_of(kt * tile, tile), tile)
        scores = []
        for j, chunk in enumerate(chunks):
            s = lax.dot_general(
                q, chunk[rows, :HEAD], (((1,), (1,)), ((), ())), preferred_element_type=f32
            )
            if masked:
                s = jnp.where(ahead >= place_ref[j], s, big_negative)
            scores.append(s)
        top = functools.reduce(jnp.maximum, scores)
        new_peak = jnp.maximum(peak, jnp.max(top, axis=-1, keepdims=True))
        fade = jnp.exp2(peak - new_peak)
        acc = acc * fade
        sums = None
        for j, chunk in enumerate(chunks):
            p = jnp.exp2(scores[j] - new_peak)
            if masked:
                p = jnp.where(ahead >= place_ref[j], p, 0.0)
            sums = p if sums is None else sums + p
            acc = acc + dot(p.astype(bf16), chunk[rows, HEAD:])
        total = total * fade + jnp.sum(sums, axis=-1, keepdims=True)
        return new_peak, total, acc

    state = (
        jnp.full((tile, 1), big_negative, f32),
        jnp.zeros((tile, 1), f32),
        jnp.zeros((tile, HEAD), f32),
    )
    state = lax.fori_loop(0, step, lambda kt, st: update(st, kt, False), state)
    _, total, acc = update(state, step, True)
    out_ref[...] = (acc / total).astype(bf16)


def coarse_attention(q, chunks, places, tile=256):
    rows = q.shape[0]
    whole = pl.BlockSpec(chunks[0].shape, lambda i, place: (0, 0))
    return pl.pallas_call(
        attention_kernel,
        out_shape=jax.ShapeDtypeStruct((rows, HEAD), bf16),
        grid_spec=pltpu.PrefetchScalarGridSpec(
            num_scalar_prefetch=1,
            grid=(rows // tile,),
            in_specs=[pl.BlockSpec((tile, HEAD), lambda i, place: (i, 0))] + [whole] * len(chunks),
            out_specs=pl.BlockSpec((tile, HEAD), lambda i, place: (i, 0)),
        ),
        compiler_params=pltpu.CompilerParams(vmem_limit_bytes=48 << 20),
    )(places, q, *chunks)


def gate(array, earlier):
    return lax.optimization_barrier((array, earlier))[0]


def body(
    tokens,
    fine_gain,
    fine_query,
    fine_keyval,
    fine_out,
    down_weight,
    coarse_gain,
    coarse_query,
    coarse_keyval,
    coarse_out,
    up_weight,
):
    width = tokens.shape[1]
    wide = coarse_gain.shape[0]
    cols = coarse_query.shape[1]
    yh, z, x, yl, c = (lax.axis_index(a) for a in ALL)
    y = yh * 2 + yl
    s, t = lax.axis_index(SEQ), lax.axis_index(TP)
    n_seq, n_tp = lax.axis_size(SEQ), lax.axis_size(TP)
    swap = [(b * n_tp + a, a * n_tp + b) for a in range(n_seq) for b in range(n_tp)]

    with jax.named_scope("weights"):
        query_here = lax.ppermute(coarse_query, ALL, swap)
        keyval_here = lax.ppermute(coarse_keyval, ALL, swap)
        out_sent = lax.dynamic_slice(coarse_out, (0, s * cols), (cols, cols))
        out_here = lax.ppermute(out_sent, ALL, swap)

    fine_state = fine_layer(tokens, fine_gain, fine_query, fine_keyval, fine_out)
    run_count = tokens.shape[0] // SHORT
    pooled = jnp.mean(fine_state.astype(f32).reshape(run_count, SHORT, width), axis=1).astype(bf16)

    with jax.named_scope("gather_rows"):
        z_rows = gathered(pooled, ("z",)).reshape(-1, width)
        z_count = z_rows.shape[0]
        y_rows = around_four(z_rows, ("yh", "yl"))
        all_rows = jnp.concatenate(y_rows, 0)
        n = all_rows.shape[0]

    with jax.named_scope("weights"):
        query_here, keyval_here, out_here = gate((query_here, keyval_here, out_here), pooled)
        gain = lax.dynamic_slice(coarse_gain, (t * cols,), (cols,))[:, None]
        slot_rows = lax.dynamic_slice(down_weight, (128 * z, 0), (128, cols))
        gram_rows = jnp.transpose(slot_rows)
        half = 3 * HEAD
        from_rows, from_lift = [], []
        for k in range(2):
            for w in (query_here, keyval_here[:, 0], keyval_here[:, 1]):
                w = w[:, k * HEAD : (k + 1) * HEAD]
                from_rows.append((w.astype(f32) * gain).astype(bf16))
            from_rows.append(gram_rows)
            direct = lax.dynamic_slice(slot_rows, (64 * yh + 32 * k, 0), (32, cols))
            from_lift.append(jnp.transpose(out_here[k * HEAD : (k + 1) * HEAD]))
            from_lift.append(jnp.transpose(direct))
        from_rows = jnp.concatenate(from_rows, 1)
        from_lift = jnp.concatenate(from_lift, 1)
        down, flipped = gate((down_weight, jnp.transpose(up_weight)), z_rows)

        def products(core):
            start = core * (width // 2)
            one = lax.dynamic_slice(down, (start, 0), (width // 2, cols))
            two = lax.dynamic_slice(flipped, (start, 0), (width // 2, cols))
            return dot(one, from_rows), dot(two, from_lift)

        sent = [v.astype(bf16) for v in products(1 - c)]
        both = [v + rotated(w, "c", 1).astype(f32) for v, w in zip(products(c), sent)]
        pieces = [jnp.swapaxes(v.astype(bf16).reshape(4, 128, 2, -1), 1, 2) for v in both]
        pieces = jnp.concatenate(pieces, 3).reshape(8, 128, -1)
        piece = jnp.sum(exchanged(pieces, ("x", "yl")).astype(f32), axis=0).astype(bf16)
        piece = gate(piece, (y_rows[1], y_rows[3]))
        summed = gathered(piece, ("c", "x")).reshape(width, -1)
        proj = summed[:, : 4 * HEAD]
        second = lax.all_gather(jnp.transpose(summed[:, 4 * HEAD :]), ("yh", "yl"), axis=0)

    with jax.named_scope("project"):
        qkv = dot(all_rows, proj)
        slot = lax.dynamic_slice(all_rows, (0, 128 * z), (n, 128))
        squares = jnp.sum(qkv[:, half:] * slot.astype(f32), axis=-1)
        squares = jnp.sum(gathered(squares[None], ("z",)), axis=(0, 1))
        inverse = lax.rsqrt(jnp.maximum(squares, 0.0) / wide + epsilon)

        def by_row(values):
            parts = values.reshape(4, 8, run_count, -1)
            twice = jnp.concatenate([parts, parts[:3]], 0)
            parts = lax.dynamic_slice_in_dim(twice, (4 - y) % 4, 4, 0)
            return jnp.swapaxes(parts.reshape(2, 2, 8, run_count, -1), 1, 2).reshape(n, -1)

        kv = by_row(qkv[:, HEAD:half].astype(bf16))
        inverse = by_row(inverse)
        factor = math.log2(math.e) / math.sqrt(HEAD)
        q = (by_row(qkv[:, :HEAD]) * (inverse * factor)).astype(bf16)
        near = around_four(kv, ("x",))
        every_inverse = gate(inverse.reshape(1, n), (near[1], near[3]))
        every_inverse = gathered(every_inverse, ("x", "c")).reshape(4, 2, n, 1)

    with jax.named_scope("attention"):
        chunks, places = [], []
        for by in (0, 1, 3, 2):
            mine = near[by]
            other = rotated(mine, "c", 1)
            source = (x + by) % 4
            shift = 128 * (source - x)
            for chunk, core, place in ((mine, c, shift), (other, 1 - c, shift + 32 * (1 - 2 * c))):
                scale = lax.dynamic_slice(every_inverse, (source, core, 0, 0), (1, 1, n, 1))
                chunks.append((chunk.astype(f32) * scale.reshape(n, 1)).astype(bf16))
                places.append(place)
        heads = coarse_attention(q, chunks, jnp.stack(places).astype(jnp.int32))

    with jax.named_scope("lift"):
        heads = jnp.swapaxes(heads.reshape(2, 8, 2, run_count, HEAD), 1, 2)
        heads = heads.reshape(4, z_count, HEAD)
        total = None
        for by in range(4):
            part = lax.dynamic_index_in_dim(heads, (y + by) % 4, 0, keepdims=False)
            if by:
                part = rotated(part, ("yh", "yl"), by)
            matrix = lax.dynamic_index_in_dim(second, (y + 4 - by) % 4, 0, keepdims=False)
            product = dot(part, matrix[:HEAD])
            total = product if total is None else total + product
        slot = lax.dynamic_slice(z_rows, (0, 128 * z), (z_count, 128))
        total = total + dot(slot, second[:, HEAD:].reshape(128, width))
        lifted = exchanged(total.astype(bf16).reshape(8, run_count, width), ("z",))
        lifted = jnp.sum(lifted.astype(f32), axis=0)
        before = from_behind(lifted[run_count - 1 :], ALL, 1)
        lifted = jnp.concatenate([before, lifted[: run_count - 1]], 0)
        result = fine_state.astype(f32) + jnp.repeat(lifted, SHORT, axis=0)
    return result.astype(bf16)


def solution(mesh):
    fine = Mesh(mesh.devices.reshape(2, 8, 4, 2, 2), ALL)
    return jax.shard_map(
        body,
        mesh=fine,
        in_specs=(
            P(ALL, None),
            P(),
            P(),
            P(),
            P(),
            P(None, TP),
            P(),
            P(SEQ, TP),
            P(SEQ, None, TP),
            P(TP, None),
            P(TP, None),
        ),
        out_specs=P(ALL, None),
        check_vma=False,
    )
```

```python
import functools
import math

import jax
import jax.numpy as jnp
from jax import lax
from jax.experimental import pallas as pl
from jax.experimental.pallas import tpu as pltpu
from jax.sharding import Mesh, PartitionSpec as P

HEAD = 128
WINDOW = 256
SHORT = 8

epsilon = 1e-06
big_negative = -1e30

ALL = ("yh", "z", "x", "yl", "c")
SEQ = ("yh", "z")
TP = ("x", "yl", "c")
f32 = jnp.float32
bf16 = jnp.bfloat16


def from_behind(array, axis, by):
    size = lax.axis_size(axis)
    pairs = [(i, i + by) for i in range(size) if 0 <= i + by < size]
    return lax.ppermute(array, axis, pairs)


def rotated(array, axis, by):
    size = lax.axis_size(axis)
    return lax.ppermute(array, axis, [(i, (i + by) % size) for i in range(size)])


def around_four(array, axes):
    above, below = rotated(array, axes, 3), rotated(array, axes, 1)
    half = array.shape[0] // 2
    top, bottom = rotated(above[:half], axes, 3), rotated(below[half:], axes, 1)
    return [array, above, jnp.concatenate([top, bottom], 0), below]


def gathered(array, axes):
    copies = jnp.broadcast_to(array, (lax.axis_size(axes), *array.shape))
    return lax.all_to_all(copies, axes, split_axis=0, concat_axis=0, tiled=True)


def exchanged(pieces, axes):
    return lax.all_to_all(pieces, axes, split_axis=0, concat_axis=0, tiled=True)


def normalize(values, scale_gain):
    mean_square = jnp.mean(values * values, axis=-1, keepdims=True)
    return values * lax.rsqrt(mean_square + epsilon) * scale_gain


def dot(a, b):
    return jnp.dot(a, b, preferred_element_type=f32)


def fine_layer(tokens, fine_gain, fine_query, fine_keyval, fine_out):
    tok_rows, width = tokens.shape
    fine_heads = width // HEAD
    scale = 1.0 / math.sqrt(HEAD)
    start_row = lax.axis_index(ALL) * tok_rows
    inputs = tokens.astype(f32)
    normed = normalize(inputs, fine_gain).astype(bf16)
    queries = dot(normed, fine_query).astype(bf16)
    keyvals = dot(normed, fine_keyval).astype(bf16)
    earlier_rows = from_behind(normed, ALL, 1)
    earlier = dot(earlier_rows, fine_keyval).astype(bf16)
    key_rows = jnp.concatenate([earlier, keyvals], 0)
    span = key_rows.shape[0]
    key_heads = key_rows[:, :width].reshape(span, fine_heads, HEAD)
    value_heads = key_rows[:, width:].reshape(span, fine_heads, HEAD)
    query_heads = queries.reshape(tok_rows, fine_heads, HEAD)
    scores = jnp.einsum("qhd,khd->hqk", query_heads, key_heads, preferred_element_type=f32) * scale
    row_index = jnp.arange(tok_rows, dtype=jnp.int32)[:, None]
    col_index = jnp.arange(span, dtype=jnp.int32)[None, :]
    offset = row_index + WINDOW - col_index
    allowed = (offset >= 0) & (offset < WINDOW) & (start_row - WINDOW + col_index >= 0)
    scores = jnp.where(allowed[None], scores, big_negative)
    peak = jnp.max(scores, axis=-1, keepdims=True)
    terms = jnp.where(allowed[None], jnp.exp(scores - peak), 0.0)
    denom = jnp.sum(terms, axis=-1)
    mixed = jnp.einsum("hqk,khd->qhd", terms.astype(bf16), value_heads, preferred_element_type=f32)
    local = (mixed / jnp.transpose(denom)[..., None]).reshape(tok_rows, width).astype(bf16)
    return (inputs + dot(local, fine_out)).astype(bf16)


def attention_kernel(place_ref, q_ref, inverse_ref, *refs):
    chunks, out_ref = refs[:-1], refs[-1]
    tile = q_ref.shape[0]
    step = pl.program_id(0)
    q = q_ref[...]
    row = step * tile + lax.broadcasted_iota(jnp.int32, (tile, tile), 0)
    col = step * tile + lax.broadcasted_iota(jnp.int32, (tile, tile), 1)

    def position(index):
        return (index >> 6) * 512 + ((index >> 5) & 1) * 64 + (index & 31)

    ahead = position(row) - position(col)

    def update(state, kt, masked):
        peak, total, acc = state
        rows = pl.ds(pl.multiple_of(kt * tile, tile), tile)
        scores = []
        for j, chunk in enumerate(chunks):
            s = lax.dot_general(
                q, chunk[rows, :HEAD], (((1,), (1,)), ((), ())), preferred_element_type=f32
            )
            s = s * inverse_ref[j : j + 1, rows]
            if masked:
                s = jnp.where(ahead >= place_ref[j], s, big_negative)
            scores.append(s)
        top = functools.reduce(jnp.maximum, scores)
        new_peak = jnp.maximum(peak, jnp.max(top, axis=-1, keepdims=True))
        fade = jnp.exp2(peak - new_peak)
        acc = acc * fade
        sums = None
        for j, chunk in enumerate(chunks):
            p = jnp.exp2(scores[j] - new_peak)
            if masked:
                p = jnp.where(ahead >= place_ref[j], p, 0.0)
            sums = p if sums is None else sums + p
            p = (p * inverse_ref[j : j + 1, rows]).astype(bf16)
            acc = acc + dot(p, chunk[rows, HEAD:])
        total = total * fade + jnp.sum(sums, axis=-1, keepdims=True)
        return new_peak, total, acc

    state = (
        jnp.full((tile, 1), big_negative, f32),
        jnp.zeros((tile, 1), f32),
        jnp.zeros((tile, HEAD), f32),
    )
    state = lax.fori_loop(0, step, lambda kt, st: update(st, kt, False), state)
    _, total, acc = update(state, step, True)
    out_ref[...] = (acc / total).astype(bf16)


def coarse_attention(q, inverses, chunks, places, tile=256):
    rows = q.shape[0]
    whole = pl.BlockSpec(chunks[0].shape, lambda i, place: (0, 0))
    return pl.pallas_call(
        attention_kernel,
        out_shape=jax.ShapeDtypeStruct((rows, HEAD), bf16),
        grid_spec=pltpu.PrefetchScalarGridSpec(
            num_scalar_prefetch=1,
            grid=(rows // tile,),
            in_specs=[
                pl.BlockSpec((tile, HEAD), lambda i, place: (i, 0)),
                pl.BlockSpec(inverses.shape, lambda i, place: (0, 0)),
            ]
            + [whole] * len(chunks),
            out_specs=pl.BlockSpec((tile, HEAD), lambda i, place: (i, 0)),
        ),
        compiler_params=pltpu.CompilerParams(vmem_limit_bytes=48 << 20),
    )(places, q, inverses, *chunks)


def gate(array, earlier):
    return lax.optimization_barrier((array, earlier))[0]


def product_kernel(where_ref, down_ref, up_ref, gain_ref, pack_ref, give_ref, keep_ref):
    core, gram_at = where_ref[0], where_ref[1]
    gain = gain_ref[...]
    cols = pack_ref.shape[1]
    scaled = [
        (pack_ref[j * cols : (j + 1) * cols, :].astype(f32) * gain).astype(bf16) for j in range(3)
    ]
    gram_rows = down_ref[pl.ds(pl.multiple_of(gram_at, 128), 128), :]
    right, left = [], []
    for k in range(2):
        lanes = slice(k * HEAD, (k + 1) * HEAD)
        right.append(jnp.concatenate([w[:, lanes] for w in scaled], 1))
        direct = down_ref[pl.ds(pl.multiple_of(where_ref[2 + k], 32), 32), :]
        start = 3 * cols + k * HEAD
        left.append(jnp.concatenate([pack_ref[start : start + HEAD, :], direct], 0))
    half = down_ref.shape[0] // 2
    for out_ref, side in ((give_ref, 1 - core), (keep_ref, core)):
        rows = pl.ds(pl.multiple_of(side * half, half), half)
        one, two = down_ref[rows, :], up_ref[:, rows]
        gram = lax.dot_general(
            one, gram_rows, (((1,), (1,)), ((), ())), preferred_element_type=f32
        ).astype(bf16)
        for k in range(2):
            proj = dot(one, right[k]).astype(bf16)
            lift = dot(left[k], two).astype(bf16)
            for q in range(4):
                block = slice(q * 128, (q + 1) * 128)
                for j in range(3):
                    out_ref[q, k, j * 128 : (j + 1) * 128, :] = proj[block, j * 128 : (j + 1) * 128]
                out_ref[q, k, 3 * 128 : 4 * 128, :] = gram[block]
                out_ref[q, k, 4 * 128 :, :] = lift[:, block]


def weight_products(where, down, up, gain, pack):
    width = down.shape[0]
    out = jax.ShapeDtypeStruct((4, 2, 4 * 128 + HEAD + 32, width // 8), bf16)
    whole = pl.BlockSpec(memory_space=pltpu.VMEM)
    return pl.pallas_call(
        product_kernel,
        out_shape=(out, out),
        in_specs=[pl.BlockSpec(memory_space=pltpu.SMEM)] + [whole] * 4,
        out_specs=(whole, whole),
        compiler_params=pltpu.CompilerParams(vmem_limit_bytes=40 << 20),
    )(where, down, up, gain, pack)


def body(
    tokens,
    fine_gain,
    fine_query,
    fine_keyval,
    fine_out,
    down_weight,
    coarse_gain,
    coarse_query,
    coarse_keyval,
    coarse_out,
    up_weight,
):
    width = tokens.shape[1]
    wide = coarse_gain.shape[0]
    cols = coarse_query.shape[1]
    yh, z, x, yl, c = (lax.axis_index(a) for a in ALL)
    y = yh * 2 + yl
    s, t = lax.axis_index(SEQ), lax.axis_index(TP)
    n_seq, n_tp = lax.axis_size(SEQ), lax.axis_size(TP)
    swap = [(b * n_tp + a, a * n_tp + b) for a in range(n_seq) for b in range(n_tp)]

    with jax.named_scope("weights"):
        out_sent = lax.dynamic_slice(coarse_out, (0, s * cols), (cols, cols))
        sent = (coarse_query, coarse_keyval[:, 0], coarse_keyval[:, 1], out_sent)
        pack = lax.ppermute(jnp.concatenate(sent, 0), ALL, swap)

    fine_state = fine_layer(tokens, fine_gain, fine_query, fine_keyval, fine_out)
    run_count = tokens.shape[0] // SHORT
    pooled = jnp.mean(fine_state.astype(f32).reshape(run_count, SHORT, width), axis=1).astype(bf16)

    with jax.named_scope("weights"):
        gain = lax.dynamic_slice(coarse_gain, (t * cols,), (cols,))[:, None]
        direct_at = 512 * yh + 32 * z
        where = jnp.stack([c, 128 * z, direct_at, direct_at + 256]).astype(jnp.int32)
        give, keep = weight_products(where, down_weight, up_weight, gain, gate(pack, pooled))
        both = keep.astype(f32) + rotated(give, "c", 1).astype(f32)
        pieces = exchanged(both.astype(bf16), ("x",))
        pieces = jnp.sum(pieces.astype(f32), axis=0)
        mine = lax.dynamic_index_in_dim(pieces, yl, 0, keepdims=False)
        other = lax.dynamic_index_in_dim(pieces, 1 - yl, 0, keepdims=False).astype(bf16)
        piece = (mine + rotated(other, "yl", 1).astype(f32)).astype(bf16)

    with jax.named_scope("gather_rows"):
        z_rows = gathered(gate(pooled, other), ("z",)).reshape(-1, width)
        y_rows = around_four(z_rows, ("yh", "yl"))
        all_rows = jnp.concatenate(y_rows, 0)
        n = all_rows.shape[0]

    with jax.named_scope("weights"):
        summed = gathered(gate(piece, (y_rows[1], y_rows[3])), ("c", "x"))
        proj = summed[:, : 4 * HEAD].reshape(8, 4, HEAD, 128)
        proj = jnp.swapaxes(proj, 1, 2).reshape(width, 4 * HEAD)
        second = jnp.swapaxes(summed[:, 4 * HEAD :], 0, 1).reshape(-1, width)
        second = lax.all_gather(second, ("z",), axis=0)

    with jax.named_scope("project"):
        half = 3 * HEAD
        qkv = dot(all_rows, proj)

        def in_order(parts):
            twice = jnp.concatenate([parts, parts[:3]], 0)
            return lax.dynamic_slice_in_dim(twice, (4 - y) % 4, 4, 0)

        def by_row(values):
            parts = in_order(values.reshape(4, 8, run_count, -1))
            return jnp.swapaxes(parts.reshape(2, 2, 8, run_count, -1), 1, 2).reshape(n, -1)

        kv = by_row(qkv[:, HEAD:half].astype(bf16))
        near = [kv] + [rotated(kv, "x", by) for by in (3, 2, 1)]
        slot = lax.dynamic_slice(all_rows, (0, 128 * z), (n, 128))
        squares = jnp.sum(qkv[:, half:] * slot.astype(f32), axis=-1)
        squares = jnp.sum(gathered(squares[None], ("z",)), axis=(0, 1))
        inverse = by_row(lax.rsqrt(jnp.maximum(squares, 0.0) / wide + epsilon))
        factor = math.log2(math.e) / math.sqrt(HEAD)
        q = (by_row(qkv[:, :HEAD]) * (inverse * factor)).astype(bf16)
        every_inverse = gathered(inverse.reshape(1, n), ("x", "c")).reshape(4, 2, n)

    with jax.named_scope("attention"):
        chunks, places, scales = [], [], []
        for by in (0, 1, 3, 2):
            mine = near[by]
            other = rotated(mine, "c", 1)
            source = (x + by) % 4
            shift = 128 * (source - x)
            for chunk, core, place in ((mine, c, shift), (other, 1 - c, shift + 32 * (1 - 2 * c))):
                scales.append(lax.dynamic_slice(every_inverse, (source, core, 0), (1, 1, n))[0])
                chunks.append(chunk)
                places.append(place)
        places = jnp.stack(places).astype(jnp.int32)
        heads = coarse_attention(q, jnp.concatenate(scales, 0), chunks, places)

    with jax.named_scope("lift"):
        heads = jnp.transpose(heads.reshape(2, 8, 2, run_count, HEAD), (1, 0, 2, 3, 4))
        heads = exchanged(heads.reshape(8, 4 * run_count, HEAD), ("z",))
        heads = jnp.swapaxes(heads, 0, 1).reshape(4 * run_count, 8 * HEAD)
        rows = lax.dynamic_slice(
            all_rows.reshape(4, 8, run_count, width), (0, z, 0, 256 * y), (4, 1, run_count, 256)
        )
        rows = in_order(rows.reshape(4, run_count, 256)).reshape(4 * run_count, 256)
        after = second[:, :HEAD].reshape(8 * HEAD, width)
        direct = second[:, HEAD:].reshape(256, width)
        total = (dot(heads, after) + dot(rows, direct)).reshape(4, run_count, width)
        lifted = lax.dynamic_index_in_dim(total, y, 0, keepdims=False)
        for by in (1, 2, 3):
            part = lax.dynamic_index_in_dim(total, (y + by) % 4, 0, keepdims=False).astype(bf16)
            lifted = lifted + rotated(part, ("yh", "yl"), by).astype(f32)
        before = from_behind(lifted[run_count - 1 :], ALL, 1)
        lifted = jnp.concatenate([before, lifted[: run_count - 1]], 0)
        result = fine_state.astype(f32) + jnp.repeat(lifted, SHORT, axis=0)
    return result.astype(bf16)


def solution(mesh):
    fine = Mesh(mesh.devices.reshape(2, 8, 4, 2, 2), ALL)
    return jax.shard_map(
        body,
        mesh=fine,
        in_specs=(
            P(ALL, None),
            P(),
            P(),
            P(),
            P(),
            P(None, TP),
            P(),
            P(SEQ, TP),
            P(SEQ, None, TP),
            P(TP, None),
            P(TP, None),
        ),
        out_specs=P(ALL, None),
        check_vma=False,
    )
```

```python
import functools
import math

import jax
import jax.numpy as jnp
from jax import lax
from jax.experimental import pallas as pl
from jax.experimental.pallas import tpu as pltpu
from jax.sharding import Mesh, PartitionSpec as P

HEAD = 128
WINDOW = 256
SHORT = 8

epsilon = 1e-06
big_negative = -1e30

ALL = ("yh", "z", "x", "yl", "c")
SEQ = ("yh", "z")
TP = ("x", "yl", "c")
f32 = jnp.float32
bf16 = jnp.bfloat16


def from_behind(array, axis, by):
    size = lax.axis_size(axis)
    pairs = [(i, i + by) for i in range(size) if 0 <= i + by < size]
    return lax.ppermute(array, axis, pairs)


def rotated(array, axis, by):
    size = lax.axis_size(axis)
    return lax.ppermute(array, axis, [(i, (i + by) % size) for i in range(size)])


def around_four(array, axes):
    above, below = rotated(array, axes, 3), rotated(array, axes, 1)
    half = array.shape[0] // 2
    top, bottom = rotated(above[:half], axes, 3), rotated(below[half:], axes, 1)
    return [array, above, top, bottom, below]


def gathered(array, axes):
    copies = jnp.broadcast_to(array, (lax.axis_size(axes), *array.shape))
    return lax.all_to_all(copies, axes, split_axis=0, concat_axis=0, tiled=True)


def exchanged(pieces, axes):
    return lax.all_to_all(pieces, axes, split_axis=0, concat_axis=0, tiled=True)


def normalize(values, scale_gain):
    mean_square = jnp.mean(values * values, axis=-1, keepdims=True)
    return values * lax.rsqrt(mean_square + epsilon) * scale_gain


def dot(a, b):
    return jnp.dot(a, b, preferred_element_type=f32)


def fine_layer(tokens, fine_gain, fine_query, fine_keyval, fine_out):
    tok_rows, width = tokens.shape
    fine_heads = width // HEAD
    scale = 1.0 / math.sqrt(HEAD)
    start_row = lax.axis_index(ALL) * tok_rows
    inputs = tokens.astype(f32)
    normed = normalize(inputs, fine_gain).astype(bf16)
    queries = dot(normed, fine_query).astype(bf16)
    keyvals = dot(normed, fine_keyval).astype(bf16)
    earlier_rows = from_behind(normed, ALL, 1)
    earlier = dot(earlier_rows, fine_keyval).astype(bf16)
    key_rows = jnp.concatenate([earlier, keyvals], 0)
    span = key_rows.shape[0]
    key_heads = key_rows[:, :width].reshape(span, fine_heads, HEAD)
    value_heads = key_rows[:, width:].reshape(span, fine_heads, HEAD)
    query_heads = queries.reshape(tok_rows, fine_heads, HEAD)
    scores = jnp.einsum("qhd,khd->hqk", query_heads, key_heads, preferred_element_type=f32) * scale
    row_index = jnp.arange(tok_rows, dtype=jnp.int32)[:, None]
    col_index = jnp.arange(span, dtype=jnp.int32)[None, :]
    offset = row_index + WINDOW - col_index
    allowed = (offset >= 0) & (offset < WINDOW) & (start_row - WINDOW + col_index >= 0)
    scores = jnp.where(allowed[None], scores, big_negative)
    peak = jnp.max(scores, axis=-1, keepdims=True)
    terms = jnp.where(allowed[None], jnp.exp(scores - peak), 0.0)
    denom = jnp.sum(terms, axis=-1)
    mixed = jnp.einsum("hqk,khd->qhd", terms.astype(bf16), value_heads, preferred_element_type=f32)
    local = (mixed / jnp.transpose(denom)[..., None]).reshape(tok_rows, width).astype(bf16)
    return (inputs + dot(local, fine_out)).astype(bf16)


def attention_kernel(place_ref, q_ref, inverse_ref, *refs):
    chunks, out_ref = refs[:-1], refs[-1]
    tile = q_ref.shape[0]
    step = pl.program_id(0)
    q = q_ref[...]
    row = step * tile + lax.broadcasted_iota(jnp.int32, (tile, tile), 0)
    col = step * tile + lax.broadcasted_iota(jnp.int32, (tile, tile), 1)

    def position(index):
        return (index >> 6) * 512 + ((index >> 5) & 1) * 64 + (index & 31)

    ahead = position(row) - position(col)

    def update(state, kt, masked):
        peak, total, acc = state
        rows = pl.ds(pl.multiple_of(kt * tile, tile), tile)
        scores = []
        for j, chunk in enumerate(chunks):
            s = lax.dot_general(
                q, chunk[rows, :HEAD], (((1,), (1,)), ((), ())), preferred_element_type=f32
            )
            s = s * inverse_ref[j : j + 1, rows]
            if masked:
                s = jnp.where(ahead >= place_ref[j], s, big_negative)
            scores.append(s)
        top = functools.reduce(jnp.maximum, scores)
        new_peak = jnp.maximum(peak, jnp.max(top, axis=-1, keepdims=True))
        fade = jnp.exp2(peak - new_peak)
        acc = acc * fade
        sums = None
        for j, chunk in enumerate(chunks):
            p = jnp.exp2(scores[j] - new_peak)
            if masked:
                p = jnp.where(ahead >= place_ref[j], p, 0.0)
            sums = p if sums is None else sums + p
            p = (p * inverse_ref[j : j + 1, rows]).astype(bf16)
            acc = acc + dot(p, chunk[rows, HEAD:])
        total = total * fade + jnp.sum(sums, axis=-1, keepdims=True)
        return new_peak, total, acc

    state = (
        jnp.full((tile, 1), big_negative, f32),
        jnp.zeros((tile, 1), f32),
        jnp.zeros((tile, HEAD), f32),
    )
    state = lax.fori_loop(0, step, lambda kt, st: update(st, kt, False), state)
    _, total, acc = update(state, step, True)
    out_ref[...] = (acc / total).astype(bf16)


def coarse_attention(q, inverses, chunks, places, tile=256):
    rows = q.shape[0]
    whole = pl.BlockSpec(chunks[0].shape, lambda i, place: (0, 0))
    return pl.pallas_call(
        attention_kernel,
        out_shape=jax.ShapeDtypeStruct((rows, HEAD), bf16),
        grid_spec=pltpu.PrefetchScalarGridSpec(
            num_scalar_prefetch=1,
            grid=(rows // tile,),
            in_specs=[
                pl.BlockSpec((tile, HEAD), lambda i, place: (i, 0)),
                pl.BlockSpec(inverses.shape, lambda i, place: (0, 0)),
            ]
            + [whole] * len(chunks),
            out_specs=pl.BlockSpec((tile, HEAD), lambda i, place: (i, 0)),
        ),
        compiler_params=pltpu.CompilerParams(vmem_limit_bytes=48 << 20),
    )(places, q, inverses, *chunks)


def gate(array, earlier):
    return lax.optimization_barrier((array, earlier))[0]


def product_kernel(where_ref, down_ref, up_ref, pack_ref, give_ref, keep_ref):
    core, gram_at = where_ref[0], where_ref[1]
    cols = pack_ref.shape[1]
    scaled = [pack_ref[j * cols : (j + 1) * cols, :] for j in range(3)]
    gram_rows = down_ref[pl.ds(pl.multiple_of(gram_at, 128), 128), :]
    right, left = [], []
    for k in range(2):
        lanes = slice(k * HEAD, (k + 1) * HEAD)
        right.append(jnp.concatenate([w[:, lanes] for w in scaled], 1))
        direct = down_ref[pl.ds(pl.multiple_of(where_ref[2 + k], 32), 32), :]
        start = 3 * cols + k * HEAD
        left.append(jnp.concatenate([pack_ref[start : start + HEAD, :], direct], 0))
    half = down_ref.shape[0] // 2
    for out_ref, side in ((give_ref, 1 - core), (keep_ref, core)):
        rows = pl.ds(pl.multiple_of(side * half, half), half)
        one, two = down_ref[rows, :], up_ref[:, rows]
        gram = lax.dot_general(
            one, gram_rows, (((1,), (1,)), ((), ())), preferred_element_type=f32
        ).astype(bf16)
        for k in range(2):
            proj = dot(one, right[k]).astype(bf16)
            lift = dot(left[k], two).astype(bf16)
            for q in range(4):
                block = slice(q * 128, (q + 1) * 128)
                for j in range(3):
                    out_ref[q, k, j * 128 : (j + 1) * 128, :] = proj[block, j * 128 : (j + 1) * 128]
                out_ref[q, k, 3 * 128 : 4 * 128, :] = gram[block]
                out_ref[q, k, 4 * 128 :, :] = lift[:, block]


def weight_products(where, down, up, pack):
    width = down.shape[0]
    out = jax.ShapeDtypeStruct((4, 2, 4 * 128 + HEAD + 32, width // 8), bf16)
    whole = pl.BlockSpec(memory_space=pltpu.VMEM)
    return pl.pallas_call(
        product_kernel,
        out_shape=(out, out),
        in_specs=[pl.BlockSpec(memory_space=pltpu.SMEM)] + [whole] * 3,
        out_specs=(whole, whole),
        compiler_params=pltpu.CompilerParams(vmem_limit_bytes=40 << 20),
    )(where, down, up, pack)


def body(
    tokens,
    fine_gain,
    fine_query,
    fine_keyval,
    fine_out,
    down_weight,
    coarse_gain,
    coarse_query,
    coarse_keyval,
    coarse_out,
    up_weight,
):
    width = tokens.shape[1]
    wide = coarse_gain.shape[0]
    cols = coarse_query.shape[1]
    yh, z, x, yl, c = (lax.axis_index(a) for a in ALL)
    y = yh * 2 + yl
    s, t = lax.axis_index(SEQ), lax.axis_index(TP)
    n_seq, n_tp = lax.axis_size(SEQ), lax.axis_size(TP)
    swap = [(b * n_tp + a, a * n_tp + b) for a in range(n_seq) for b in range(n_tp)]

    with jax.named_scope("weights"):
        out_sent = lax.dynamic_slice(coarse_out, (0, s * cols), (cols, cols))
        sent = (coarse_query, coarse_keyval[:, 0], coarse_keyval[:, 1], out_sent)
        pack = lax.ppermute(jnp.concatenate(sent, 0), ALL, swap)

    fine_state = fine_layer(tokens, fine_gain, fine_query, fine_keyval, fine_out)
    run_count = tokens.shape[0] // SHORT
    pooled = jnp.mean(fine_state.astype(f32).reshape(run_count, SHORT, width), axis=1).astype(bf16)

    with jax.named_scope("gather_rows"):
        around = [pooled] + [rotated(pooled, "z", by) for by in range(7, 0, -1)]
        around = jnp.stack(around + around[:7])
        z_rows = lax.dynamic_slice_in_dim(around, (8 - z) % 8, 8, 0).reshape(-1, width)
        y_rows = around_four(z_rows, ("yh", "yl"))
        all_rows = jnp.concatenate(y_rows, 0)
        n = all_rows.shape[0]

    with jax.named_scope("weights"):
        gain = lax.dynamic_slice(coarse_gain, (t * cols,), (cols,))[:, None]
        direct_at = 512 * yh + 32 * z
        where = jnp.stack([c, 128 * z, direct_at, direct_at + 256]).astype(jnp.int32)
        ones = jnp.ones((cols, 1), f32)
        pack = gate(pack, pooled).astype(f32) * jnp.concatenate([gain] * 3 + [ones], 0)
        pack = gate(pack.astype(bf16), z_rows)
        give, keep = weight_products(where, down_weight, up_weight, pack)
        both = keep.astype(f32) + rotated(give, "c", 1).astype(f32)
        pieces = exchanged(gate(both.astype(bf16), (y_rows[1], y_rows[4])), ("x",))
        pieces = jnp.sum(pieces.astype(f32), axis=0)
        mine = lax.dynamic_index_in_dim(pieces, yl, 0, keepdims=False)
        other = lax.dynamic_index_in_dim(pieces, 1 - yl, 0, keepdims=False).astype(bf16)
        piece = (mine + rotated(other, "yl", 1).astype(f32)).astype(bf16)
        near_half = gathered(gate(piece, (y_rows[2], y_rows[3])), ("x",))
        far_half = rotated(near_half, "c", 1)
        summed = jnp.stack(
            [jnp.where(c == 0, near_half, far_half), jnp.where(c == 0, far_half, near_half)]
        ).reshape(8, *piece.shape)
        proj = summed[:, : 4 * HEAD].reshape(8, 4, HEAD, 128)
        proj = jnp.swapaxes(proj, 1, 2).reshape(width, 4 * HEAD)
        second = jnp.swapaxes(summed[:, 4 * HEAD :], 0, 1).reshape(-1, width)
        second = lax.all_gather(second, ("z",), axis=0)

    with jax.named_scope("project"):
        half = 3 * HEAD
        qkv = dot(all_rows, proj)

        def in_order(parts):
            twice = jnp.concatenate([parts, parts[:3]], 0)
            return lax.dynamic_slice_in_dim(twice, (4 - y) % 4, 4, 0)

        def by_row(values):
            parts = in_order(values.reshape(4, 8, run_count, -1))
            return jnp.swapaxes(parts.reshape(2, 2, 8, run_count, -1), 1, 2).reshape(n, -1)

        kv = by_row(qkv[:, HEAD:half].astype(bf16))
        near = [kv] + [rotated(kv, "x", by) for by in (3, 2, 1)]
        slot = lax.dynamic_slice(all_rows, (0, 128 * z), (n, 128))
        squares = jnp.sum(qkv[:, half:] * slot.astype(f32), axis=-1)
        squares = jnp.sum(gathered(squares[None], ("z",)), axis=(0, 1))
        inverse = by_row(lax.rsqrt(jnp.maximum(squares, 0.0) / wide + epsilon))
        factor = math.log2(math.e) / math.sqrt(HEAD)
        q = (by_row(qkv[:, :HEAD]) * (inverse * factor)).astype(bf16)
        every_inverse = gathered(inverse.reshape(1, n), ("x", "c")).reshape(4, 2, n)

    with jax.named_scope("attention"):
        chunks, places, scales = [], [], []
        for by in (0, 1, 3, 2):
            mine = near[by]
            other = rotated(mine, "c", 1)
            source = (x + by) % 4
            shift = 128 * (source - x)
            for chunk, core, place in ((mine, c, shift), (other, 1 - c, shift + 32 * (1 - 2 * c))):
                scales.append(lax.dynamic_slice(every_inverse, (source, core, 0), (1, 1, n))[0])
                chunks.append(chunk)
                places.append(place)
        places = jnp.stack(places).astype(jnp.int32)
        heads = coarse_attention(q, jnp.concatenate(scales, 0), chunks, places)

    with jax.named_scope("lift"):
        heads = jnp.transpose(heads.reshape(2, 8, 2, run_count, HEAD), (1, 0, 2, 3, 4))
        heads = exchanged(heads.reshape(8, 4 * run_count, HEAD), ("z",))
        heads = jnp.swapaxes(heads, 0, 1).reshape(4 * run_count, 8 * HEAD)
        rows = lax.dynamic_slice(
            all_rows.reshape(4, 8, run_count, width), (0, z, 0, 256 * y), (4, 1, run_count, 256)
        )
        rows = in_order(rows.reshape(4, run_count, 256)).reshape(4 * run_count, 256)
        after = second[:, :HEAD].reshape(8 * HEAD, width)
        direct = second[:, HEAD:].reshape(256, width)
        total = (dot(heads, after) + dot(rows, direct)).reshape(4, run_count, width)
        lifted = lax.dynamic_index_in_dim(total, y, 0, keepdims=False)
        for by in (1, 2, 3):
            part = lax.dynamic_index_in_dim(total, (y + by) % 4, 0, keepdims=False).astype(bf16)
            lifted = lifted + rotated(part, ("yh", "yl"), by).astype(f32)
        before = from_behind(lifted[run_count - 1 :], ALL, 1)
        lifted = jnp.concatenate([before, lifted[: run_count - 1]], 0)
        result = fine_state.astype(f32) + jnp.repeat(lifted, SHORT, axis=0)
    return result.astype(bf16)


def solution(mesh):
    fine = Mesh(mesh.devices.reshape(2, 8, 4, 2, 2), ALL)
    return jax.shard_map(
        body,
        mesh=fine,
        in_specs=(
            P(ALL, None),
            P(),
            P(),
            P(),
            P(),
            P(None, TP),
            P(),
            P(SEQ, TP),
            P(SEQ, None, TP),
            P(TP, None),
            P(TP, None),
        ),
        out_specs=P(ALL, None),
        check_vma=False,
    )
```

```python
import functools
import math

import jax
import jax.numpy as jnp
from jax import lax
from jax.experimental import pallas as pl
from jax.experimental.pallas import tpu as pltpu
from jax.sharding import Mesh, PartitionSpec as P

HEAD = 128
WINDOW = 256
SHORT = 8

epsilon = 1e-06
big_negative = -1e30

ALL = ("yh", "z", "x", "yl", "c")
SEQ = ("yh", "z")
TP = ("x", "yl", "c")
f32 = jnp.float32
bf16 = jnp.bfloat16


def from_behind(array, axis, by):
    size = lax.axis_size(axis)
    pairs = [(i, i + by) for i in range(size) if 0 <= i + by < size]
    return lax.ppermute(array, axis, pairs)


def rotated(array, axis, by):
    size = lax.axis_size(axis)
    return lax.ppermute(array, axis, [(i, (i + by) % size) for i in range(size)])


def around_four(array, axes):
    above, below = rotated(array, axes, 3), rotated(array, axes, 1)
    half = array.shape[0] // 2
    top, bottom = rotated(above[:half], axes, 3), rotated(below[half:], axes, 1)
    return [array, above, top, bottom, below]


def gathered(array, axes):
    copies = jnp.broadcast_to(array, (lax.axis_size(axes), *array.shape))
    return lax.all_to_all(copies, axes, split_axis=0, concat_axis=0, tiled=True)


def exchanged(pieces, axes):
    return lax.all_to_all(pieces, axes, split_axis=0, concat_axis=0, tiled=True)


def normalize(values, scale_gain):
    mean_square = jnp.mean(values * values, axis=-1, keepdims=True)
    return values * lax.rsqrt(mean_square + epsilon) * scale_gain


def dot(a, b):
    return jnp.dot(a, b, preferred_element_type=f32)


def fine_layer(tokens, normed, earlier_rows, fine_query, fine_keyval, fine_out):
    tok_rows, width = tokens.shape
    fine_heads = width // HEAD
    scale = 1.0 / math.sqrt(HEAD)
    start_row = lax.axis_index(ALL) * tok_rows
    inputs = tokens.astype(f32)
    queries = dot(normed, fine_query).astype(bf16)
    keyvals = dot(normed, fine_keyval).astype(bf16)
    earlier = dot(earlier_rows, fine_keyval).astype(bf16)
    key_rows = jnp.concatenate([earlier, keyvals], 0)
    span = key_rows.shape[0]
    key_heads = key_rows[:, :width].reshape(span, fine_heads, HEAD)
    value_heads = key_rows[:, width:].reshape(span, fine_heads, HEAD)
    query_heads = queries.reshape(tok_rows, fine_heads, HEAD)
    scores = jnp.einsum("qhd,khd->hqk", query_heads, key_heads, preferred_element_type=f32) * scale
    row_index = jnp.arange(tok_rows, dtype=jnp.int32)[:, None]
    col_index = jnp.arange(span, dtype=jnp.int32)[None, :]
    offset = row_index + WINDOW - col_index
    allowed = (offset >= 0) & (offset < WINDOW) & (start_row - WINDOW + col_index >= 0)
    scores = jnp.where(allowed[None], scores, big_negative)
    peak = jnp.max(scores, axis=-1, keepdims=True)
    terms = jnp.where(allowed[None], jnp.exp(scores - peak), 0.0)
    denom = jnp.sum(terms, axis=-1)
    mixed = jnp.einsum("hqk,khd->qhd", terms.astype(bf16), value_heads, preferred_element_type=f32)
    local = (mixed / jnp.transpose(denom)[..., None]).reshape(tok_rows, width).astype(bf16)
    return (inputs + dot(local, fine_out)).astype(bf16)


def attention_kernel(place_ref, q_ref, inverse_ref, *refs):
    chunks, out_ref = refs[:-1], refs[-1]
    tile = q_ref.shape[0]
    step = pl.program_id(0)
    q = q_ref[...]
    row = step * tile + lax.broadcasted_iota(jnp.int32, (tile, tile), 0)
    col = step * tile + lax.broadcasted_iota(jnp.int32, (tile, tile), 1)

    def position(index):
        return (index >> 6) * 512 + ((index >> 5) & 1) * 64 + (index & 31)

    ahead = position(row) - position(col)

    def update(state, kt, masked):
        peak, total, acc = state
        rows = pl.ds(pl.multiple_of(kt * tile, tile), tile)
        scores = []
        for j, chunk in enumerate(chunks):
            s = lax.dot_general(
                q, chunk[rows, :HEAD], (((1,), (1,)), ((), ())), preferred_element_type=f32
            )
            s = s * inverse_ref[j : j + 1, rows]
            if masked:
                s = jnp.where(ahead >= place_ref[j], s, big_negative)
            scores.append(s)
        top = functools.reduce(jnp.maximum, scores)
        new_peak = jnp.maximum(peak, jnp.max(top, axis=-1, keepdims=True))
        fade = jnp.exp2(peak - new_peak)
        acc = acc * fade
        sums = None
        for j, chunk in enumerate(chunks):
            p = jnp.exp2(scores[j] - new_peak)
            if masked:
                p = jnp.where(ahead >= place_ref[j], p, 0.0)
            sums = p if sums is None else sums + p
            p = (p * inverse_ref[j : j + 1, rows]).astype(bf16)
            acc = acc + dot(p, chunk[rows, HEAD:])
        total = total * fade + jnp.sum(sums, axis=-1, keepdims=True)
        return new_peak, total, acc

    state = (
        jnp.full((tile, 1), big_negative, f32),
        jnp.zeros((tile, 1), f32),
        jnp.zeros((tile, HEAD), f32),
    )
    state = lax.fori_loop(0, step, lambda kt, st: update(st, kt, False), state)
    _, total, acc = update(state, step, True)
    out_ref[...] = (acc / total).astype(bf16)


def coarse_attention(q, inverses, chunks, places, tile=256):
    rows = q.shape[0]
    whole = pl.BlockSpec(chunks[0].shape, lambda i, place: (0, 0))
    return pl.pallas_call(
        attention_kernel,
        out_shape=jax.ShapeDtypeStruct((rows, HEAD), bf16),
        grid_spec=pltpu.PrefetchScalarGridSpec(
            num_scalar_prefetch=1,
            grid=(rows // tile,),
            in_specs=[
                pl.BlockSpec((tile, HEAD), lambda i, place: (i, 0)),
                pl.BlockSpec(inverses.shape, lambda i, place: (0, 0)),
            ]
            + [whole] * len(chunks),
            out_specs=pl.BlockSpec((tile, HEAD), lambda i, place: (i, 0)),
        ),
        compiler_params=pltpu.CompilerParams(vmem_limit_bytes=48 << 20),
    )(places, q, inverses, *chunks)


def gate(array, earlier):
    return lax.optimization_barrier((array, earlier))[0]


def product_kernel(where_ref, down_ref, up_ref, pack_ref, give_ref, keep_ref):
    core, gram_at = where_ref[0], where_ref[1]
    cols = pack_ref.shape[1]
    scaled = [pack_ref[j * cols : (j + 1) * cols, :] for j in range(3)]
    gram_rows = down_ref[pl.ds(pl.multiple_of(gram_at, 128), 128), :]
    right, left = [], []
    for k in range(2):
        lanes = slice(k * HEAD, (k + 1) * HEAD)
        right.append(jnp.concatenate([w[:, lanes] for w in scaled], 1))
        direct = down_ref[pl.ds(pl.multiple_of(where_ref[2 + k], 32), 32), :]
        start = 3 * cols + k * HEAD
        left.append(jnp.concatenate([pack_ref[start : start + HEAD, :], direct], 0))
    half = down_ref.shape[0] // 2
    for out_ref, side in ((give_ref, 1 - core), (keep_ref, core)):
        rows = pl.ds(pl.multiple_of(side * half, half), half)
        one, two = down_ref[rows, :], up_ref[:, rows]
        gram = lax.dot_general(
            one, gram_rows, (((1,), (1,)), ((), ())), preferred_element_type=f32
        ).astype(bf16)
        for k in range(2):
            proj = dot(one, right[k]).astype(bf16)
            lift = dot(left[k], two).astype(bf16)
            head = (k + where_ref[5]) % 2
            for q in range(4):
                block = slice(q * 128, (q + 1) * 128)
                at = (q + 4 - where_ref[4]) % 4
                for j in range(3):
                    lanes = slice(j * 128, (j + 1) * 128)
                    out_ref[at, head, lanes, :] = proj[block, lanes]
                out_ref[at, head, 3 * 128 : 4 * 128, :] = gram[block]
                out_ref[at, head, 4 * 128 :, :] = lift[:, block]


def weight_products(where, down, up, pack):
    width = down.shape[0]
    out = jax.ShapeDtypeStruct((4, 2, 4 * 128 + HEAD + 32, width // 8), bf16)
    whole = pl.BlockSpec(memory_space=pltpu.VMEM)
    return pl.pallas_call(
        product_kernel,
        out_shape=(out, out),
        in_specs=[pl.BlockSpec(memory_space=pltpu.SMEM)] + [whole] * 3,
        out_specs=(whole, whole),
        compiler_params=pltpu.CompilerParams(vmem_limit_bytes=40 << 20),
    )(where, down, up, pack)


def body(
    tokens,
    fine_gain,
    fine_query,
    fine_keyval,
    fine_out,
    down_weight,
    coarse_gain,
    coarse_query,
    coarse_keyval,
    coarse_out,
    up_weight,
):
    width = tokens.shape[1]
    wide = coarse_gain.shape[0]
    cols = coarse_query.shape[1]
    yh, z, x, yl, c = (lax.axis_index(a) for a in ALL)
    y = yh * 2 + yl
    s, t = lax.axis_index(SEQ), lax.axis_index(TP)
    n_seq, n_tp = lax.axis_size(SEQ), lax.axis_size(TP)
    swap = [(b * n_tp + a, a * n_tp + b) for a in range(n_seq) for b in range(n_tp)]

    normed = normalize(tokens.astype(f32), fine_gain).astype(bf16)
    earlier_rows = from_behind(normed, ALL, 1)

    with jax.named_scope("weights"):
        out_sent = lax.dynamic_slice(coarse_out, (0, s * cols), (cols, cols))
        sent = (coarse_query, coarse_keyval[:, 0], coarse_keyval[:, 1], out_sent)
        sent = gate(jnp.concatenate(sent, 0), normed)
        pack = lax.ppermute(sent, ALL, swap)

    fine_state = fine_layer(tokens, normed, earlier_rows, fine_query, fine_keyval, fine_out)
    run_count = tokens.shape[0] // SHORT
    pooled = jnp.mean(fine_state.astype(f32).reshape(run_count, SHORT, width), axis=1).astype(bf16)

    with jax.named_scope("gather_rows"):
        around = [pooled] + [rotated(pooled, "z", by) for by in range(7, 0, -1)]
        around = jnp.stack(around + around[:7])
        z_rows = lax.dynamic_slice_in_dim(around, (8 - z) % 8, 8, 0).reshape(-1, width)
        y_rows = around_four(z_rows, ("yh", "yl"))
        all_rows = jnp.concatenate(y_rows, 0)
        n = all_rows.shape[0]

    with jax.named_scope("weights"):
        gain = lax.dynamic_slice(coarse_gain, (t * cols,), (cols,))[:, None]
        direct_at = 128 * z + 64 * yh
        where = [c, 128 * z, direct_at, direct_at + 32, x, yl]
        where = jnp.stack(where).astype(jnp.int32)
        ones = jnp.ones((cols, 1), f32)
        pack = gate(pack, pooled).astype(f32) * jnp.concatenate([gain] * 3 + [ones], 0)
        pack = gate(pack.astype(bf16), z_rows)
        give, keep = weight_products(where, down_weight, up_weight, pack)
        got = rotated(give, "c", 1)
        both = [keep[i].astype(f32) + got[i].astype(f32) for i in range(4)]
        total = both[0]
        for by in (1, 3, 2):
            total = total + rotated(both[by].astype(bf16), "x", by).astype(f32)
        piece = (total[0] + rotated(total[1].astype(bf16), "yl", 1).astype(f32)).astype(bf16)
        near_half = gathered(gate(piece, tuple(y_rows)), ("x",))
        far_half = rotated(near_half, "c", 1)
        summed = jnp.stack(
            [jnp.where(c == 0, near_half, far_half), jnp.where(c == 0, far_half, near_half)]
        ).reshape(8, *piece.shape)
        proj = summed[:, : 4 * HEAD].reshape(8, 4, HEAD, 128)
        proj = jnp.swapaxes(proj, 1, 2).reshape(width, 4 * HEAD)
        second = jnp.swapaxes(summed[:, 4 * HEAD :], 0, 1).reshape(-1, width)
        seconds = [second] + [rotated(second, ("yh", "yl"), by) for by in (1, 2, 3)]

    with jax.named_scope("project"):
        half = 3 * HEAD
        qkv = dot(all_rows, proj)

        def in_order(parts):
            twice = jnp.concatenate([parts, parts[:3]], 0)
            return lax.dynamic_slice_in_dim(twice, (4 - y) % 4, 4, 0)

        def by_row(values):
            parts = in_order(values.reshape(4, 8, run_count, -1))
            return jnp.swapaxes(parts.reshape(2, 2, 8, run_count, -1), 1, 2).reshape(n, -1)

        kv = by_row(qkv[:, HEAD:half].astype(bf16))
        near = [kv] + [rotated(kv, "x", by) for by in (3, 2, 1)]
        slot = lax.dynamic_slice(all_rows, (0, 128 * z), (n, 128))
        squares = jnp.sum(qkv[:, half:] * slot.astype(f32), axis=-1)
        squares = jnp.sum(gathered(squares[None], ("z",)), axis=(0, 1))
        inverse = by_row(lax.rsqrt(jnp.maximum(squares, 0.0) / wide + epsilon))
        factor = math.log2(math.e) / math.sqrt(HEAD)
        q = (by_row(qkv[:, :HEAD]) * (inverse * factor)).astype(bf16)
        every_inverse = gathered(inverse.reshape(1, n), ("x", "c")).reshape(4, 2, n)

    with jax.named_scope("attention"):
        chunks, places, scales = [], [], []
        for by in (0, 1, 3, 2):
            mine = near[by]
            other = rotated(mine, "c", 1)
            source = (x + by) % 4
            shift = 128 * (source - x)
            for chunk, core, place in ((mine, c, shift), (other, 1 - c, shift + 32 * (1 - 2 * c))):
                scales.append(lax.dynamic_slice(every_inverse, (source, core, 0), (1, 1, n))[0])
                chunks.append(chunk)
                places.append(place)
        places = jnp.stack(places).astype(jnp.int32)
        q = gate(q, tuple(seconds))
        heads = coarse_attention(q, jnp.concatenate(scales, 0), chunks, places)

    with jax.named_scope("lift"):
        heads = jnp.swapaxes(heads.reshape(2, 8, 2, run_count, HEAD), 1, 2)
        heads = heads.reshape(4, 8 * run_count, HEAD)
        direct = jnp.stack([seconds[(4 - i) % 4][HEAD:] for i in range(4)])
        slot = lax.dynamic_slice(z_rows, (0, 128 * z), (8 * run_count, 128))
        total = dot(slot, in_order(direct).reshape(128, width))
        for by in range(4):
            part = lax.dynamic_index_in_dim(heads, (y + by) % 4, 0, keepdims=False)
            if by:
                part = rotated(part, ("yh", "yl"), by)
            total = total + dot(part, seconds[by][:HEAD])
        lifted = exchanged(total.astype(bf16).reshape(8, run_count, width), ("z",))
        lifted = jnp.sum(lifted.astype(f32), axis=0)
        before = from_behind(lifted[run_count - 1 :], ALL, 1)
        lifted = jnp.concatenate([before, lifted[: run_count - 1]], 0)
        result = fine_state.astype(f32) + jnp.repeat(lifted, SHORT, axis=0)
    return result.astype(bf16)


def solution(mesh):
    fine = Mesh(mesh.devices.reshape(2, 8, 4, 2, 2), ALL)
    return jax.shard_map(
        body,
        mesh=fine,
        in_specs=(
            P(ALL, None),
            P(),
            P(),
            P(),
            P(),
            P(None, TP),
            P(),
            P(SEQ, TP),
            P(SEQ, None, TP),
            P(TP, None),
            P(TP, None),
        ),
        out_specs=P(ALL, None),
        check_vma=False,
    )
```

```python
import functools
import math

import jax
import jax.numpy as jnp
from jax import lax
from jax.experimental import pallas as pl
from jax.experimental.pallas import tpu as pltpu
from jax.sharding import Mesh, PartitionSpec as P

HEAD = 128
WINDOW = 256
SHORT = 8

epsilon = 1e-06
big_negative = -1e30

ALL = ("yh", "z", "x", "yl", "c")
SEQ = ("yh", "z")
TP = ("x", "yl", "c")
f32 = jnp.float32
bf16 = jnp.bfloat16


def from_behind(array, axis, by):
    size = lax.axis_size(axis)
    pairs = [(i, i + by) for i in range(size) if 0 <= i + by < size]
    return lax.ppermute(array, axis, pairs)


def rotated(array, axis, by):
    size = lax.axis_size(axis)
    return lax.ppermute(array, axis, [(i, (i + by) % size) for i in range(size)])


def around_four(array, axes):
    above, below = rotated(array, axes, 3), rotated(array, axes, 1)
    half = array.shape[0] // 2
    top, bottom = rotated(above[:half], axes, 3), rotated(below[half:], axes, 1)
    return [array, above, top, bottom, below]


def gathered(array, axes):
    copies = jnp.broadcast_to(array, (lax.axis_size(axes), *array.shape))
    return lax.all_to_all(copies, axes, split_axis=0, concat_axis=0, tiled=True)


def exchanged(pieces, axes):
    return lax.all_to_all(pieces, axes, split_axis=0, concat_axis=0, tiled=True)


def normalize(values, scale_gain):
    mean_square = jnp.mean(values * values, axis=-1, keepdims=True)
    return values * lax.rsqrt(mean_square + epsilon) * scale_gain


def dot(a, b):
    return jnp.dot(a, b, preferred_element_type=f32)


def fine_layer(tokens, normed, earlier_rows, fine_query, fine_keyval, fine_out):
    tok_rows, width = tokens.shape
    fine_heads = width // HEAD
    scale = 1.0 / math.sqrt(HEAD)
    start_row = lax.axis_index(ALL) * tok_rows
    inputs = tokens.astype(f32)
    queries = dot(normed, fine_query).astype(bf16)
    keyvals = dot(normed, fine_keyval).astype(bf16)
    earlier = dot(earlier_rows, fine_keyval).astype(bf16)
    key_rows = jnp.concatenate([earlier, keyvals], 0)
    span = key_rows.shape[0]
    key_heads = key_rows[:, :width].reshape(span, fine_heads, HEAD)
    value_heads = key_rows[:, width:].reshape(span, fine_heads, HEAD)
    query_heads = queries.reshape(tok_rows, fine_heads, HEAD)
    scores = jnp.einsum("qhd,khd->hqk", query_heads, key_heads, preferred_element_type=f32) * scale
    row_index = jnp.arange(tok_rows, dtype=jnp.int32)[:, None]
    col_index = jnp.arange(span, dtype=jnp.int32)[None, :]
    offset = row_index + WINDOW - col_index
    allowed = (offset >= 0) & (offset < WINDOW) & (start_row - WINDOW + col_index >= 0)
    scores = jnp.where(allowed[None], scores, big_negative)
    peak = jnp.max(scores, axis=-1, keepdims=True)
    terms = jnp.where(allowed[None], jnp.exp(scores - peak), 0.0)
    denom = jnp.sum(terms, axis=-1)
    mixed = jnp.einsum("hqk,khd->qhd", terms.astype(bf16), value_heads, preferred_element_type=f32)
    local = (mixed / jnp.transpose(denom)[..., None]).reshape(tok_rows, width).astype(bf16)
    return (inputs + dot(local, fine_out)).astype(bf16)


def attention_kernel(place_ref, q_ref, inverse_ref, *refs):
    chunks, out_ref = refs[:-1], refs[-1]
    tile = q_ref.shape[0]
    step = pl.program_id(0)
    q = q_ref[...]
    row = step * tile + lax.broadcasted_iota(jnp.int32, (tile, tile), 0)
    col = step * tile + lax.broadcasted_iota(jnp.int32, (tile, tile), 1)

    def position(index):
        return (index >> 6) * 512 + ((index >> 5) & 1) * 64 + (index & 31)

    ahead = position(row) - position(col)

    def update(state, kt, masked):
        peak, total, acc = state
        rows = pl.ds(pl.multiple_of(kt * tile, tile), tile)
        scores = []
        for j, chunk in enumerate(chunks):
            s = lax.dot_general(
                q, chunk[rows, :HEAD], (((1,), (1,)), ((), ())), preferred_element_type=f32
            )
            s = s * inverse_ref[j : j + 1, rows]
            if masked:
                s = jnp.where(ahead >= place_ref[j], s, big_negative)
            scores.append(s)
        top = functools.reduce(jnp.maximum, scores)
        new_peak = jnp.maximum(peak, jnp.max(top, axis=-1, keepdims=True))
        fade = jnp.exp2(peak - new_peak)
        acc = acc * fade
        sums = None
        for j, chunk in enumerate(chunks):
            p = jnp.exp2(scores[j] - new_peak)
            if masked:
                p = jnp.where(ahead >= place_ref[j], p, 0.0)
            sums = p if sums is None else sums + p
            p = (p * inverse_ref[j : j + 1, rows]).astype(bf16)
            acc = acc + dot(p, chunk[rows, HEAD:])
        total = total * fade + jnp.sum(sums, axis=-1, keepdims=True)
        return new_peak, total, acc

    state = (
        jnp.full((tile, 1), big_negative, f32),
        jnp.zeros((tile, 1), f32),
        jnp.zeros((tile, HEAD), f32),
    )
    state = lax.fori_loop(0, step, lambda kt, st: update(st, kt, False), state)
    _, total, acc = update(state, step, True)
    out_ref[...] = (acc / total).astype(bf16)


def coarse_attention(q, inverses, chunks, places, tile=256):
    rows = q.shape[0]
    whole = pl.BlockSpec(chunks[0].shape, lambda i, place: (0, 0))
    return pl.pallas_call(
        attention_kernel,
        out_shape=jax.ShapeDtypeStruct((rows, HEAD), bf16),
        grid_spec=pltpu.PrefetchScalarGridSpec(
            num_scalar_prefetch=1,
            grid=(rows // tile,),
            in_specs=[
                pl.BlockSpec((tile, HEAD), lambda i, place: (i, 0)),
                pl.BlockSpec(inverses.shape, lambda i, place: (0, 0)),
            ]
            + [whole] * len(chunks),
            out_specs=pl.BlockSpec((tile, HEAD), lambda i, place: (i, 0)),
        ),
        compiler_params=pltpu.CompilerParams(vmem_limit_bytes=48 << 20),
    )(places, q, inverses, *chunks)


def gate(array, earlier):
    return lax.optimization_barrier((array, earlier))[0]


def product_kernel(where_ref, down_ref, up_ref, pack_ref, give_ref, keep_ref):
    core, gram_at = where_ref[0], where_ref[1]
    cols = pack_ref.shape[1]
    scaled = [pack_ref[j * cols : (j + 1) * cols, :] for j in range(3)]
    gram_rows = down_ref[pl.ds(pl.multiple_of(gram_at, 128), 128), :]
    right, left = [], []
    for k in range(2):
        lanes = slice(k * HEAD, (k + 1) * HEAD)
        right.append(jnp.concatenate([w[:, lanes] for w in scaled], 1))
        direct = down_ref[pl.ds(pl.multiple_of(where_ref[2 + k], 32), 32), :]
        start = 3 * cols + k * HEAD
        left.append(jnp.concatenate([pack_ref[start : start + HEAD, :], direct], 0))
    half = down_ref.shape[0] // 2
    for out_ref, side in ((give_ref, 1 - core), (keep_ref, core)):
        rows = pl.ds(pl.multiple_of(side * half, half), half)
        one, two = down_ref[rows, :], up_ref[:, rows]
        gram = lax.dot_general(
            one, gram_rows, (((1,), (1,)), ((), ())), preferred_element_type=f32
        ).astype(bf16)
        for k in range(2):
            proj = dot(one, right[k]).astype(bf16)
            lift = dot(left[k], two).astype(bf16)
            head = (k + where_ref[5]) % 2
            for q in range(4):
                block = slice(q * 128, (q + 1) * 128)
                at = (q + 4 - where_ref[4]) % 4
                for j in range(3):
                    lanes = slice(j * 128, (j + 1) * 128)
                    out_ref[at, head, lanes, :] = proj[block, lanes]
                out_ref[at, head, 3 * 128 : 4 * 128, :] = gram[block]
                out_ref[at, head, 4 * 128 :, :] = lift[:, block]


def weight_products(where, down, up, pack):
    width = down.shape[0]
    out = jax.ShapeDtypeStruct((4, 2, 4 * 128 + HEAD + 32, width // 8), bf16)
    whole = pl.BlockSpec(memory_space=pltpu.VMEM)
    return pl.pallas_call(
        product_kernel,
        out_shape=(out, out),
        in_specs=[pl.BlockSpec(memory_space=pltpu.SMEM)] + [whole] * 3,
        out_specs=(whole, whole),
        compiler_params=pltpu.CompilerParams(vmem_limit_bytes=40 << 20),
    )(where, down, up, pack)


def body(
    tokens,
    fine_gain,
    fine_query,
    fine_keyval,
    fine_out,
    down_weight,
    coarse_gain,
    coarse_query,
    coarse_keyval,
    coarse_out,
    up_weight,
):
    width = tokens.shape[1]
    wide = coarse_gain.shape[0]
    cols = coarse_query.shape[1]
    yh, z, x, yl, c = (lax.axis_index(a) for a in ALL)
    y = yh * 2 + yl
    s, t = lax.axis_index(SEQ), lax.axis_index(TP)
    n_seq, n_tp = lax.axis_size(SEQ), lax.axis_size(TP)
    swap = [(b * n_tp + a, a * n_tp + b) for a in range(n_seq) for b in range(n_tp)]

    normed = normalize(tokens.astype(f32), fine_gain).astype(bf16)
    earlier_rows = from_behind(normed, ALL, 1)

    with jax.named_scope("weights"):
        out_sent = lax.dynamic_slice(coarse_out, (0, s * cols), (cols, cols))
        sent = (coarse_query, coarse_keyval[:, 0], coarse_keyval[:, 1], out_sent)
        sent = gate(jnp.concatenate(sent, 0), normed)
        pack = lax.ppermute(sent, ALL, swap)

    fine_state = fine_layer(tokens, normed, earlier_rows, fine_query, fine_keyval, fine_out)
    run_count = tokens.shape[0] // SHORT
    pooled = jnp.mean(fine_state.astype(f32).reshape(run_count, SHORT, width), axis=1).astype(bf16)

    with jax.named_scope("gather_rows"):
        across = rotated(pooled, "z", 4)
        pair = jnp.where(z < 4, jnp.stack([pooled, across]), jnp.stack([across, pooled]))
        around = [pair] + [rotated(pair, "z", by) for by in (7, 6, 1)]
        around = jnp.stack(around + around[:3])
        z_rows = lax.dynamic_slice_in_dim(around, (4 - z % 4) % 4, 4, 0).reshape(-1, width)
        y_rows = around_four(z_rows, ("yh", "yl"))
        all_rows = jnp.concatenate(y_rows, 0)
        n = all_rows.shape[0]

    with jax.named_scope("weights"):
        gain = lax.dynamic_slice(coarse_gain, (t * cols,), (cols,))[:, None]
        direct_at = 128 * z + 64 * yh
        where = [c, 128 * z, direct_at, direct_at + 32, x, yl]
        where = jnp.stack(where).astype(jnp.int32)
        ones = jnp.ones((cols, 1), f32)
        pack = gate(pack, pair).astype(f32) * jnp.concatenate([gain] * 3 + [ones], 0)
        pack = gate(pack.astype(bf16), z_rows)
        give, keep = weight_products(where, down_weight, up_weight, pack)
        got = rotated(give, "c", 1)
        both = [keep[i].astype(f32) + got[i].astype(f32) for i in range(4)]
        total = both[0]
        for by in (1, 3, 2):
            total = total + rotated(both[by].astype(bf16), "x", by).astype(f32)
        piece = (total[0] + rotated(total[1].astype(bf16), "yl", 1).astype(f32)).astype(bf16)
        near_half = gathered(gate(piece, tuple(y_rows)), ("x",))
        far_half = rotated(near_half, "c", 1)
        summed = jnp.stack(
            [jnp.where(c == 0, near_half, far_half), jnp.where(c == 0, far_half, near_half)]
        ).reshape(8, *piece.shape)
        proj = summed[:, : 4 * HEAD].reshape(8, 4, HEAD, 128)
        proj = jnp.swapaxes(proj, 1, 2).reshape(width, 4 * HEAD)
        second = jnp.swapaxes(summed[:, 4 * HEAD :], 0, 1).reshape(-1, width)
        below, above = rotated(second, ("yh", "yl"), 1), rotated(second, ("yh", "yl"), 3)
        seconds = [second, below, rotated(below, ("yh", "yl"), 1), above]

    with jax.named_scope("project"):
        half = 3 * HEAD
        qkv = dot(all_rows, proj)

        def in_order(parts):
            twice = jnp.concatenate([parts, parts[:3]], 0)
            return lax.dynamic_slice_in_dim(twice, (4 - y) % 4, 4, 0)

        def by_row(values):
            parts = in_order(values.reshape(4, 8, run_count, -1))
            parts = parts.reshape(2, 2, 4, 2, run_count, -1)
            return jnp.transpose(parts, (0, 3, 2, 1, 4, 5)).reshape(n, -1)

        kv = by_row(qkv[:, HEAD:half].astype(bf16))
        near = [kv] + [rotated(kv, "x", by) for by in (3, 2, 1)]
        slot = lax.dynamic_slice(all_rows, (0, 128 * z), (n, 128))
        squares = jnp.sum(qkv[:, half:] * slot.astype(f32), axis=-1)
        squares = jnp.sum(gathered(squares[None], ("z",)), axis=(0, 1))
        inverse = by_row(lax.rsqrt(jnp.maximum(squares, 0.0) / wide + epsilon))
        factor = math.log2(math.e) / math.sqrt(HEAD)
        q = (by_row(qkv[:, :HEAD]) * (inverse * factor)).astype(bf16)
        every_inverse = gathered(inverse.reshape(1, n), ("x", "c")).reshape(4, 2, n)

    with jax.named_scope("attention"):
        chunks, places, scales = [], [], []
        for by in (0, 1, 3, 2):
            mine = near[by]
            other = rotated(mine, "c", 1)
            source = (x + by) % 4
            shift = 128 * (source - x)
            for chunk, core, place in ((mine, c, shift), (other, 1 - c, shift + 32 * (1 - 2 * c))):
                scales.append(lax.dynamic_slice(every_inverse, (source, core, 0), (1, 1, n))[0])
                chunks.append(chunk)
                places.append(place)
        places = jnp.stack(places).astype(jnp.int32)
        q = gate(q, tuple(seconds))
        heads = coarse_attention(q, jnp.concatenate(scales, 0), chunks, places)

    with jax.named_scope("lift"):
        heads = jnp.swapaxes(heads.reshape(2, 8, 2, run_count, HEAD), 1, 2)
        heads = heads.reshape(4, 8 * run_count, HEAD)
        direct = jnp.stack([seconds[(4 - i) % 4][HEAD:] for i in range(4)])
        slot = lax.dynamic_slice(z_rows, (0, 128 * z), (8 * run_count, 128))
        slot = jnp.swapaxes(slot.reshape(4, 2, run_count, 128), 0, 1).reshape(-1, 128)
        total = dot(slot, in_order(direct).reshape(128, width))
        for by in range(4):
            part = lax.dynamic_index_in_dim(heads, (y + by) % 4, 0, keepdims=False)
            if by:
                part = rotated(part, ("yh", "yl"), by)
            total = total + dot(part, seconds[by][:HEAD])
        lifted = exchanged(total.astype(bf16).reshape(8, run_count, width), ("z",))
        lifted = jnp.sum(lifted.astype(f32), axis=0)
        before = from_behind(lifted[run_count - 1 :], ALL, 1)
        lifted = jnp.concatenate([before, lifted[: run_count - 1]], 0)
        result = fine_state.astype(f32) + jnp.repeat(lifted, SHORT, axis=0)
    return result.astype(bf16)


def solution(mesh):
    fine = Mesh(mesh.devices.reshape(2, 8, 4, 2, 2), ALL)
    return jax.shard_map(
        body,
        mesh=fine,
        in_specs=(
            P(ALL, None),
            P(),
            P(),
            P(),
            P(),
            P(None, TP),
            P(),
            P(SEQ, TP),
            P(SEQ, None, TP),
            P(TP, None),
            P(TP, None),
        ),
        out_specs=P(ALL, None),
        check_vma=False,
    )
```

```python
import functools
import math

import jax
import jax.numpy as jnp
from jax import lax
from jax.experimental import pallas as pl
from jax.experimental.pallas import tpu as pltpu
from jax.sharding import Mesh, PartitionSpec as P

HEAD = 128
WINDOW = 256
SHORT = 8

epsilon = 1e-06
big_negative = -1e30

ALL = ("yh", "z", "x", "yl", "c")
SEQ = ("yh", "z")
TP = ("x", "yl", "c")
f32 = jnp.float32
bf16 = jnp.bfloat16


def from_behind(array, axis, by):
    size = lax.axis_size(axis)
    pairs = [(i, i + by) for i in range(size) if 0 <= i + by < size]
    return lax.ppermute(array, axis, pairs)


def rotated(array, axis, by):
    size = lax.axis_size(axis)
    return lax.ppermute(array, axis, [(i, (i + by) % size) for i in range(size)])


def around_four(array, axes):
    above, below = rotated(array, axes, 3), rotated(array, axes, 1)
    half = array.shape[0] // 2
    top, bottom = rotated(above[:half], axes, 3), rotated(below[half:], axes, 1)
    return [array, above, top, bottom, below]


def gathered(array, axes):
    copies = jnp.broadcast_to(array, (lax.axis_size(axes), *array.shape))
    return lax.all_to_all(copies, axes, split_axis=0, concat_axis=0, tiled=True)


def exchanged(pieces, axes):
    return lax.all_to_all(pieces, axes, split_axis=0, concat_axis=0, tiled=True)


def normalize(values, scale_gain):
    mean_square = jnp.mean(values * values, axis=-1, keepdims=True)
    return values * lax.rsqrt(mean_square + epsilon) * scale_gain


def dot(a, b):
    return jnp.dot(a, b, preferred_element_type=f32)


def fine_kernel(
    first_ref, tokens_ref, normed_ref, before_ref, query_ref, key_ref, value_ref, out_ref,
    state_ref, pooled_ref, total_ref,
):
    rows = tokens_ref.shape[0]
    step = pl.program_id(0)

    @pl.when(step == 0)
    def _():
        total_ref[...] = tokens_ref[...].astype(f32)

    normed, before = normed_ref[...], before_ref[...]
    factor = math.log2(math.e) / math.sqrt(HEAD)
    query = dot(normed, query_ref[...]).astype(bf16)
    key, value = key_ref[...], value_ref[...]
    keys = jnp.concatenate([dot(before, key).astype(bf16), dot(normed, key).astype(bf16)], 0)
    values = jnp.concatenate([dot(before, value).astype(bf16), dot(normed, value).astype(bf16)], 0)
    row = lax.broadcasted_iota(jnp.int32, (rows, 2 * rows), 0)
    col = lax.broadcasted_iota(jnp.int32, (rows, 2 * rows), 1)
    allowed = (col > row) & (col <= row + WINDOW) & (col >= first_ref[0])
    heads = []
    for k in range(query.shape[1] // HEAD):
        lanes = slice(k * HEAD, (k + 1) * HEAD)
        scores = lax.dot_general(
            query[:, lanes], keys[:, lanes], (((1,), (1,)), ((), ())), preferred_element_type=f32
        )
        scores = jnp.where(allowed, scores * factor, big_negative)
        terms = jnp.exp2(scores - jnp.max(scores, axis=-1, keepdims=True))
        denom = jnp.sum(terms, axis=-1, keepdims=True)
        heads.append((dot(terms.astype(bf16), values[:, lanes]) / denom).astype(bf16))
    total_ref[...] += dot(jnp.concatenate(heads, 1), out_ref[...])

    @pl.when(step == pl.num_programs(0) - 1)
    def _():
        state = total_ref[...].astype(bf16)
        state_ref[...] = state
        runs = state.astype(f32).reshape(rows // SHORT, SHORT, state.shape[1])
        pooled_ref[...] = (jnp.sum(runs, axis=1) * (1.0 / SHORT)).astype(bf16)


def fine_layer(tokens, normed, before, fine_query, fine_keyval, fine_out):
    rows, width = tokens.shape
    pair = 2 * HEAD
    steps = width // pair
    whole = pl.BlockSpec((rows, width), lambda i: (0, 0))
    first = jnp.where(lax.axis_index(ALL) == 0, rows, 0).astype(jnp.int32).reshape(1)
    return pl.pallas_call(
        fine_kernel,
        out_shape=(
            jax.ShapeDtypeStruct((rows, width), bf16),
            jax.ShapeDtypeStruct((rows // SHORT, width), bf16),
        ),
        grid=(steps,),
        in_specs=[pl.BlockSpec(memory_space=pltpu.SMEM), whole, whole, whole]
        + [
            pl.BlockSpec((width, pair), lambda i: (0, i)),
            pl.BlockSpec((width, pair), lambda i: (0, i)),
            pl.BlockSpec((width, pair), lambda i: (0, steps + i)),
            pl.BlockSpec((pair, width), lambda i: (i, 0)),
        ],
        out_specs=(whole, pl.BlockSpec((rows // SHORT, width), lambda i: (0, 0))),
        scratch_shapes=[pltpu.VMEM((rows, width), f32)],
        compiler_params=pltpu.CompilerParams(vmem_limit_bytes=40 << 20),
    )(first, tokens, normed, before, fine_query, fine_keyval, fine_keyval, fine_out)


def attention_kernel(place_ref, q_ref, inverse_ref, *refs):
    chunks, out_ref = refs[:-1], refs[-1]
    tile = q_ref.shape[0]
    step = pl.program_id(0)
    q = q_ref[...]
    row = step * tile + lax.broadcasted_iota(jnp.int32, (tile, tile), 0)
    col = step * tile + lax.broadcasted_iota(jnp.int32, (tile, tile), 1)

    def position(index):
        return (index >> 6) * 512 + ((index >> 5) & 1) * 64 + (index & 31)

    ahead = position(row) - position(col)

    def update(kt, state):
        peak, total, acc = state
        rows = pl.ds(pl.multiple_of(kt * tile, tile), tile)
        inverses, scores = [], []
        for j, chunk in enumerate(chunks):
            s = lax.dot_general(
                q, chunk[rows, :HEAD], (((1,), (1,)), ((), ())), preferred_element_type=f32
            )
            inverses.append(inverse_ref[pl.ds(place_ref[len(chunks) + j], 1), rows])
            bound = jnp.where(kt < step, -(1 << 24), place_ref[j])
            scores.append(jnp.where(ahead >= bound, s * inverses[j], big_negative))
        top = functools.reduce(jnp.maximum, scores)
        new_peak = jnp.maximum(peak, jnp.max(top, axis=-1, keepdims=True))
        fade = jnp.exp2(peak - new_peak)
        acc = acc * fade
        sums = None
        for j, chunk in enumerate(chunks):
            p = jnp.exp2(scores[j] - new_peak)
            sums = p if sums is None else sums + p
            acc = acc + dot((p * inverses[j]).astype(bf16), chunk[rows, HEAD:])
        total = total * fade + jnp.sum(sums, axis=-1, keepdims=True)
        return new_peak, total, acc

    state = (
        jnp.full((tile, 1), big_negative, f32),
        jnp.zeros((tile, 1), f32),
        jnp.zeros((tile, HEAD), f32),
    )
    _, total, acc = lax.fori_loop(0, step + 1, update, state)
    out_ref[...] = (acc / total).astype(bf16)


def coarse_attention(q, inverses, chunks, places, tile=256):
    rows = q.shape[0]
    whole = pl.BlockSpec(chunks[0].shape, lambda i, place: (0, 0))
    return pl.pallas_call(
        attention_kernel,
        out_shape=jax.ShapeDtypeStruct((rows, HEAD), bf16),
        grid_spec=pltpu.PrefetchScalarGridSpec(
            num_scalar_prefetch=1,
            grid=(rows // tile,),
            in_specs=[
                pl.BlockSpec((tile, HEAD), lambda i, place: (i, 0)),
                pl.BlockSpec(inverses.shape, lambda i, place: (0, 0)),
            ]
            + [whole] * len(chunks),
            out_specs=pl.BlockSpec((tile, HEAD), lambda i, place: (i, 0)),
        ),
        compiler_params=pltpu.CompilerParams(vmem_limit_bytes=48 << 20),
    )(places, q, inverses, *chunks)


def gate(array, earlier):
    return lax.optimization_barrier((array, earlier))[0]


def product_kernel(where_ref, down_ref, up_ref, pack_ref, give_ref, keep_ref):
    core, gram_at = where_ref[0], where_ref[1]
    cols = pack_ref.shape[1]
    scaled = [pack_ref[j * cols : (j + 1) * cols, :] for j in range(3)]
    gram_rows = down_ref[pl.ds(pl.multiple_of(gram_at, 128), 128), :]
    right, left = [], []
    for k in range(2):
        lanes = slice(k * HEAD, (k + 1) * HEAD)
        right.append(jnp.concatenate([w[:, lanes] for w in scaled], 1))
        direct = down_ref[pl.ds(pl.multiple_of(where_ref[2 + k], 32), 32), :]
        start = 3 * cols + k * HEAD
        left.append(jnp.concatenate([pack_ref[start : start + HEAD, :], direct], 0))
    half = down_ref.shape[0] // 2
    for out_ref, side in ((give_ref, 1 - core), (keep_ref, core)):
        rows = pl.ds(pl.multiple_of(side * half, half), half)
        one, two = down_ref[rows, :], up_ref[:, rows]
        gram = lax.dot_general(
            one, gram_rows, (((1,), (1,)), ((), ())), preferred_element_type=f32
        ).astype(bf16)
        for k in range(2):
            proj = dot(one, right[k]).astype(bf16)
            lift = dot(left[k], two).astype(bf16)
            head = (k + where_ref[5]) % 2
            for q in range(4):
                block = slice(q * 128, (q + 1) * 128)
                at = (q + 4 - where_ref[4]) % 4
                for j in range(3):
                    lanes = slice(j * 128, (j + 1) * 128)
                    out_ref[at, head, lanes, :] = proj[block, lanes]
                out_ref[at, head, 3 * 128 : 4 * 128, :] = gram[block]
                out_ref[at, head, 4 * 128 :, :] = lift[:, block]


def weight_products(where, down, up, pack):
    width = down.shape[0]
    out = jax.ShapeDtypeStruct((4, 2, 4 * 128 + HEAD + 32, width // 8), bf16)
    whole = pl.BlockSpec(memory_space=pltpu.VMEM)
    return pl.pallas_call(
        product_kernel,
        out_shape=(out, out),
        in_specs=[pl.BlockSpec(memory_space=pltpu.SMEM)] + [whole] * 3,
        out_specs=(whole, whole),
        compiler_params=pltpu.CompilerParams(vmem_limit_bytes=40 << 20),
    )(where, down, up, pack)


def body(
    tokens,
    fine_gain,
    fine_query,
    fine_keyval,
    fine_out,
    down_weight,
    coarse_gain,
    coarse_query,
    coarse_keyval,
    coarse_out,
    up_weight,
):
    width = tokens.shape[1]
    wide = coarse_gain.shape[0]
    cols = coarse_query.shape[1]
    yh, z, x, yl, c = (lax.axis_index(a) for a in ALL)
    y = yh * 2 + yl
    s, t = lax.axis_index(SEQ), lax.axis_index(TP)
    n_seq, n_tp = lax.axis_size(SEQ), lax.axis_size(TP)
    swap = [(b * n_tp + a, a * n_tp + b) for a in range(n_seq) for b in range(n_tp)]

    normed = normalize(tokens.astype(f32), fine_gain).astype(bf16)
    earlier_rows = from_behind(normed, ALL, 1)

    with jax.named_scope("weights"):
        out_sent = lax.dynamic_slice(coarse_out, (0, s * cols), (cols, cols))
        sent = (coarse_query, coarse_keyval[:, 0], coarse_keyval[:, 1], out_sent)
        sent = gate(jnp.concatenate(sent, 0), normed)
        pack = lax.ppermute(sent, ALL, swap)

    fine_state, pooled = fine_layer(
        tokens, normed, earlier_rows, fine_query, fine_keyval, fine_out
    )
    run_count = tokens.shape[0] // SHORT

    with jax.named_scope("gather_rows"):
        across = rotated(pooled, "z", 4)
        pair = jnp.where(z < 4, jnp.stack([pooled, across]), jnp.stack([across, pooled]))
        around = [pair] + [rotated(pair, "z", by) for by in (7, 6, 1)]
        around = jnp.stack(around + around[:3])
        z_rows = lax.dynamic_slice_in_dim(around, (4 - z % 4) % 4, 4, 0).reshape(-1, width)
        y_rows = around_four(z_rows, ("yh", "yl"))
        all_rows = jnp.concatenate(y_rows, 0)
        n = all_rows.shape[0]

    with jax.named_scope("weights"):
        gain = lax.dynamic_slice(coarse_gain, (t * cols,), (cols,))[:, None]
        direct_at = 128 * z + 64 * yh
        where = [c, 128 * z, direct_at, direct_at + 32, x, yl]
        where = jnp.stack(where).astype(jnp.int32)
        ones = jnp.ones((cols, 1), f32)
        pack = gate(pack, pair).astype(f32) * jnp.concatenate([gain] * 3 + [ones], 0)
        pack = gate(pack.astype(bf16), z_rows)
        give, keep = weight_products(where, down_weight, up_weight, pack)
        got = rotated(give, "c", 1)
        both = [keep[i].astype(f32) + got[i].astype(f32) for i in range(4)]
        total = both[0]
        for by in (1, 3, 2):
            total = total + rotated(both[by].astype(bf16), "x", by).astype(f32)
        piece = (total[0] + rotated(total[1].astype(bf16), "yl", 1).astype(f32)).astype(bf16)
        near_half = gathered(gate(piece, tuple(y_rows)), ("x",))
        far_half = rotated(near_half, "c", 1)
        summed = jnp.stack(
            [jnp.where(c == 0, near_half, far_half), jnp.where(c == 0, far_half, near_half)]
        ).reshape(8, *piece.shape)
        proj = summed[:, : 4 * HEAD].reshape(8, 4, HEAD, 128)
        proj = jnp.swapaxes(proj, 1, 2).reshape(width, 4 * HEAD)
        second = jnp.swapaxes(summed[:, 4 * HEAD :], 0, 1).reshape(-1, width)
        below, above = rotated(second, ("yh", "yl"), 1), rotated(second, ("yh", "yl"), 3)
        seconds = [second, below, rotated(below, ("yh", "yl"), 1), above]

    with jax.named_scope("project"):
        half = 3 * HEAD
        qkv = dot(all_rows, proj)

        def in_order(parts):
            twice = jnp.concatenate([parts, parts[:3]], 0)
            return lax.dynamic_slice_in_dim(twice, (4 - y) % 4, 4, 0)

        def by_row(values):
            parts = in_order(values.reshape(4, 8, run_count, -1))
            parts = parts.reshape(2, 2, 4, 2, run_count, -1)
            return jnp.transpose(parts, (0, 3, 2, 1, 4, 5)).reshape(n, -1)

        kv = by_row(qkv[:, HEAD:half].astype(bf16))
        near = [kv] + [rotated(kv, "x", by) for by in (3, 2, 1)]
        slot = lax.dynamic_slice(all_rows, (0, 128 * z), (n, 128))
        squares = jnp.sum(qkv[:, half:] * slot.astype(f32), axis=-1)
        squares = jnp.sum(gathered(squares[None], ("z",)), axis=(0, 1))
        inverse = by_row(lax.rsqrt(jnp.maximum(squares, 0.0) / wide + epsilon))
        factor = math.log2(math.e) / math.sqrt(HEAD)
        q = (by_row(qkv[:, :HEAD]) * (inverse * factor)).astype(bf16)
        every_inverse = gathered(inverse.reshape(1, n), ("x", "c")).reshape(8, n)

    with jax.named_scope("attention"):
        chunks, places, sources = [], [], []
        for by in (0, 1, 3, 2):
            mine = near[by]
            other = rotated(mine, "c", 1)
            source = (x + by) % 4
            shift = 128 * (source - x)
            chunks += [mine, other]
            places += [shift, shift + 32 * (1 - 2 * c)]
            sources += [2 * source + c, 2 * source + 1 - c]
        places = jnp.stack(places + sources).astype(jnp.int32)
        q = gate(q, (below, above))
        heads = coarse_attention(q, every_inverse, chunks, places)

    with jax.named_scope("lift"):
        heads = jnp.swapaxes(heads.reshape(2, 8, 2, run_count, HEAD), 1, 2)
        heads = heads.reshape(4, 8 * run_count, HEAD)
        slot = lax.dynamic_slice(z_rows, (0, 128 * z), (8 * run_count, 128))
        slot = slot.reshape(4, 2, run_count, 4, 32)
        slots = jnp.transpose(slot, (3, 1, 0, 2, 4)).reshape(4, 8 * run_count, 32)
        total = None
        for by in range(4):
            part = lax.dynamic_index_in_dim(heads, (y + by) % 4, 0, keepdims=False)
            if by:
                part = rotated(part, ("yh", "yl"), by)
            slot = lax.dynamic_index_in_dim(slots, (y + 4 - by) % 4, 0, keepdims=False)
            product = dot(jnp.concatenate([part, slot], 1), seconds[by])
            total = product if total is None else total + product
        lifted = exchanged(total.astype(bf16).reshape(8, run_count, width), ("z",))
        lifted = jnp.sum(lifted.astype(f32), axis=0)
        before = from_behind(lifted[run_count - 1 :], ALL, 1)
        lifted = jnp.concatenate([before, lifted[: run_count - 1]], 0)
        result = fine_state.astype(f32) + jnp.repeat(lifted, SHORT, axis=0)
    return result.astype(bf16)


def solution(mesh):
    fine = Mesh(mesh.devices.reshape(2, 8, 4, 2, 2), ALL)
    return jax.shard_map(
        body,
        mesh=fine,
        in_specs=(
            P(ALL, None),
            P(),
            P(),
            P(),
            P(),
            P(None, TP),
            P(),
            P(SEQ, TP),
            P(SEQ, None, TP),
            P(TP, None),
            P(TP, None),
        ),
        out_specs=P(ALL, None),
        check_vma=False,
    )
```

```python
import functools
import math

import jax
import jax.numpy as jnp
from jax import lax
from jax.experimental import pallas as pl
from jax.experimental.pallas import tpu as pltpu
from jax.sharding import Mesh, PartitionSpec as P

HEAD = 128
WINDOW = 256
SHORT = 8

epsilon = 1e-06
big_negative = -1e30

ALL = ("yh", "z", "x", "yl", "c")
SEQ = ("yh", "z")
TP = ("x", "yl", "c")
f32 = jnp.float32
bf16 = jnp.bfloat16


def from_behind(array, axis, by):
    size = lax.axis_size(axis)
    pairs = [(i, i + by) for i in range(size) if 0 <= i + by < size]
    return lax.ppermute(array, axis, pairs)


def rotated(array, axis, by):
    size = lax.axis_size(axis)
    return lax.ppermute(array, axis, [(i, (i + by) % size) for i in range(size)])


def around_four(array, axes):
    above, below = rotated(array, axes, 3), rotated(array, axes, 1)
    half = array.shape[0] // 2
    top, bottom = rotated(above[:half], axes, 3), rotated(below[half:], axes, 1)
    return [array, above, top, bottom, below]


def gathered(array, axes):
    copies = jnp.broadcast_to(array, (lax.axis_size(axes), *array.shape))
    return lax.all_to_all(copies, axes, split_axis=0, concat_axis=0, tiled=True)


def exchanged(pieces, axes):
    return lax.all_to_all(pieces, axes, split_axis=0, concat_axis=0, tiled=True)


def normalize(values, scale_gain):
    mean_square = jnp.mean(values * values, axis=-1, keepdims=True)
    return values * lax.rsqrt(mean_square + epsilon) * scale_gain


def dot(a, b):
    return jnp.dot(a, b, preferred_element_type=f32)


def fine_kernel(
    first_ref, tokens_ref, normed_ref, before_ref, query_ref, key_ref, value_ref, out_ref,
    state_ref, pooled_ref, total_ref,
):
    rows = tokens_ref.shape[0]
    step = pl.program_id(0)

    @pl.when(step == 0)
    def _():
        total_ref[...] = tokens_ref[...].astype(f32)

    normed, before = normed_ref[...], before_ref[...]
    factor = math.log2(math.e) / math.sqrt(HEAD)
    query = dot(normed, query_ref[...]).astype(bf16)
    key, value = key_ref[...], value_ref[...]
    keys = jnp.concatenate([dot(before, key).astype(bf16), dot(normed, key).astype(bf16)], 0)
    values = jnp.concatenate([dot(before, value).astype(bf16), dot(normed, value).astype(bf16)], 0)
    row = lax.broadcasted_iota(jnp.int32, (rows, 2 * rows), 0)
    col = lax.broadcasted_iota(jnp.int32, (rows, 2 * rows), 1)
    allowed = (col > row) & (col <= row + WINDOW) & (col >= first_ref[0])
    heads = []
    for k in range(query.shape[1] // HEAD):
        lanes = slice(k * HEAD, (k + 1) * HEAD)
        scores = lax.dot_general(
            query[:, lanes], keys[:, lanes], (((1,), (1,)), ((), ())), preferred_element_type=f32
        )
        scores = jnp.where(allowed, scores * factor, big_negative)
        terms = jnp.exp2(scores - jnp.max(scores, axis=-1, keepdims=True))
        denom = jnp.sum(terms, axis=-1, keepdims=True)
        heads.append((dot(terms.astype(bf16), values[:, lanes]) / denom).astype(bf16))
    total_ref[...] += dot(jnp.concatenate(heads, 1), out_ref[...])

    @pl.when(step == pl.num_programs(0) - 1)
    def _():
        state = total_ref[...].astype(bf16)
        state_ref[...] = state
        runs = state.astype(f32).reshape(rows // SHORT, SHORT, state.shape[1])
        pooled_ref[...] = (jnp.sum(runs, axis=1) * (1.0 / SHORT)).astype(bf16)


def in_hbm(array):
    return pltpu.with_memory_space_constraint(array, pltpu.MemorySpace.HBM)


def fine_layer(tokens, normed, before, fine_query, fine_keyval, fine_out):
    rows, width = tokens.shape
    pair = 2 * HEAD
    steps = width // pair
    whole = pl.BlockSpec((rows, width), lambda i: (0, 0))
    first = jnp.where(lax.axis_index(ALL) == 0, rows, 0).astype(jnp.int32).reshape(1)
    return pl.pallas_call(
        fine_kernel,
        out_shape=(
            jax.ShapeDtypeStruct((rows, width), bf16),
            jax.ShapeDtypeStruct((rows // SHORT, width), bf16),
        ),
        grid=(steps,),
        in_specs=[pl.BlockSpec(memory_space=pltpu.SMEM), whole, whole, whole]
        + [
            pl.BlockSpec((width, pair), lambda i: (0, i)),
            pl.BlockSpec((width, pair), lambda i: (0, i)),
            pl.BlockSpec((width, pair), lambda i: (0, steps + i)),
            pl.BlockSpec((pair, width), lambda i: (i, 0)),
        ],
        out_specs=(whole, pl.BlockSpec((rows // SHORT, width), lambda i: (0, 0))),
        scratch_shapes=[pltpu.VMEM((rows, width), f32)],
        compiler_params=pltpu.CompilerParams(vmem_limit_bytes=40 << 20),
    )(first, tokens, normed, before, *[in_hbm(w) for w in (fine_query, fine_keyval, fine_keyval, fine_out)])


def attention_kernel(place_ref, q_ref, inverse_ref, *refs):
    chunks, out_ref = refs[:-1], refs[-1]
    tile = q_ref.shape[0]
    step = pl.program_id(0)
    q = q_ref[...]
    row = step * tile + lax.broadcasted_iota(jnp.int32, (tile, tile), 0)
    col = step * tile + lax.broadcasted_iota(jnp.int32, (tile, tile), 1)

    def position(index):
        return (index >> 6) * 512 + ((index >> 5) & 1) * 64 + (index & 31)

    ahead = position(row) - position(col)

    def update(kt, state, masked):
        peak, total, acc = state
        rows = pl.ds(pl.multiple_of(kt * tile, tile), tile)
        inverses, scores = [], []
        for j, chunk in enumerate(chunks):
            s = lax.dot_general(
                q, chunk[rows, :HEAD], (((1,), (1,)), ((), ())), preferred_element_type=f32
            )
            inverses.append(inverse_ref[pl.ds(place_ref[len(chunks) + j], 1), rows])
            s = s * inverses[j]
            scores.append(jnp.where(ahead >= place_ref[j], s, big_negative) if masked else s)
        top = functools.reduce(jnp.maximum, scores)
        new_peak = jnp.maximum(peak, jnp.max(top, axis=-1, keepdims=True))
        fade = jnp.exp2(peak - new_peak)
        acc = acc * fade
        sums = None
        for j, chunk in enumerate(chunks):
            p = jnp.exp2(scores[j] - new_peak)
            sums = p if sums is None else sums + p
            acc = acc + dot((p * inverses[j]).astype(bf16), chunk[rows, HEAD:])
        total = total * fade + jnp.sum(sums, axis=-1, keepdims=True)
        return new_peak, total, acc

    state = (
        jnp.full((tile, 1), big_negative, f32),
        jnp.zeros((tile, 1), f32),
        jnp.zeros((tile, HEAD), f32),
    )
    state = lax.fori_loop(0, step, lambda kt, st: update(kt, st, False), state)
    _, total, acc = update(step, state, True)
    out_ref[...] = (acc / total).astype(bf16)


def coarse_attention(q, inverses, chunks, places, tile=256):
    rows = q.shape[0]
    whole = pl.BlockSpec(chunks[0].shape, lambda i, place: (0, 0))
    return pl.pallas_call(
        attention_kernel,
        out_shape=jax.ShapeDtypeStruct((rows, HEAD), bf16),
        grid_spec=pltpu.PrefetchScalarGridSpec(
            num_scalar_prefetch=1,
            grid=(rows // tile,),
            in_specs=[
                pl.BlockSpec((tile, HEAD), lambda i, place: (i, 0)),
                pl.BlockSpec(inverses.shape, lambda i, place: (0, 0)),
            ]
            + [whole] * len(chunks),
            out_specs=pl.BlockSpec((tile, HEAD), lambda i, place: (i, 0)),
        ),
        compiler_params=pltpu.CompilerParams(vmem_limit_bytes=48 << 20),
    )(places, q, inverses, *chunks)


def gate(array, earlier):
    return lax.optimization_barrier((array, earlier))[0]


def product_kernel(where_ref, down_ref, up_ref, pack_ref, give_ref, keep_ref):
    core, gram_at = where_ref[0], where_ref[1]
    cols = pack_ref.shape[1]
    scaled = [pack_ref[j * cols : (j + 1) * cols, :] for j in range(3)]
    gram_rows = down_ref[pl.ds(pl.multiple_of(gram_at, 128), 128), :]
    right, left = [], []
    for k in range(2):
        lanes = slice(k * HEAD, (k + 1) * HEAD)
        right.append(jnp.concatenate([w[:, lanes] for w in scaled], 1))
        direct = down_ref[pl.ds(pl.multiple_of(where_ref[2 + k], 32), 32), :]
        start = 3 * cols + k * HEAD
        left.append(jnp.concatenate([pack_ref[start : start + HEAD, :], direct], 0))
    half = down_ref.shape[0] // 2
    for out_ref, side in ((give_ref, 1 - core), (keep_ref, core)):
        rows = pl.ds(pl.multiple_of(side * half, half), half)
        one, two = down_ref[rows, :], up_ref[:, rows]
        gram = lax.dot_general(
            one, gram_rows, (((1,), (1,)), ((), ())), preferred_element_type=f32
        ).astype(bf16)
        for k in range(2):
            proj = dot(one, right[k]).astype(bf16)
            lift = dot(left[k], two).astype(bf16)
            head = (k + where_ref[5]) % 2
            for q in range(4):
                block = slice(q * 128, (q + 1) * 128)
                at = (q + 4 - where_ref[4]) % 4
                for j in range(3):
                    lanes = slice(j * 128, (j + 1) * 128)
                    out_ref[at, head, lanes, :] = proj[block, lanes]
                out_ref[at, head, 3 * 128 : 4 * 128, :] = gram[block]
                out_ref[at, head, 4 * 128 :, :] = lift[:, block]


def weight_products(where, down, up, pack):
    width = down.shape[0]
    out = jax.ShapeDtypeStruct((4, 2, 4 * 128 + HEAD + 32, width // 8), bf16)
    whole = pl.BlockSpec(memory_space=pltpu.VMEM)
    return pl.pallas_call(
        product_kernel,
        out_shape=(out, out),
        in_specs=[pl.BlockSpec(memory_space=pltpu.SMEM)] + [whole] * 3,
        out_specs=(whole, whole),
        compiler_params=pltpu.CompilerParams(vmem_limit_bytes=40 << 20),
    )(where, down, up, pack)


def project_kernel(
    where_ref, own_ref, above_ref, top_ref, bottom_ref, below_ref, near_ref, far_ref,
    kv_ref, q_ref, squares_ref, weight_ref,
):
    core, slot_at, y = where_ref[0], where_ref[1], where_ref[2]
    half = weight_ref.shape[0] // 2
    for side, piece_ref in ((core, near_ref), (1 - core, far_ref)):
        for x in range(4):
            rows = pl.ds(pl.multiple_of(side * half + x * 128, 128), 128)
            for j in range(4):
                lanes = slice(j * 128, (j + 1) * 128)
                weight_ref[rows, lanes] = piece_ref[x, lanes, :]
    weight = weight_ref[...]
    ones = jnp.ones((8, 128), f32)
    opposite = jnp.concatenate([top_ref[...], bottom_ref[...]], 0)
    lanes = pl.ds(pl.multiple_of(slot_at, 128), 128)
    opposite_slot = jnp.concatenate([top_ref[:, lanes], bottom_ref[:, lanes]], 0)
    groups = (
        (own_ref[...], own_ref[:, lanes]),
        (above_ref[...], above_ref[:, lanes]),
        (opposite, opposite_slot),
        (below_ref[...], below_ref[:, lanes]),
    )
    for i, (rows, slot) in enumerate(groups):
        product = dot(rows, weight)
        squares = product[:, 3 * HEAD :] * slot.astype(f32)
        squares_ref[i] = lax.dot_general(
            ones,
            squares,
            (((1,), (1,)), ((), ())),
            precision=lax.Precision.HIGHEST,
            preferred_element_type=f32,
        )
        kv = product[:, HEAD : 3 * HEAD].astype(bf16)
        source = (y + i) % 4
        start = (source // 2) * 512 + (source % 2) * 32
        for a in range(4):
            for h in range(2):
                at = pl.ds(pl.multiple_of(start + (h * 4 + a) * 64, 32), 32)
                part = slice((a * 2 + h) * 32, (a * 2 + h) * 32 + 32)
                kv_ref[at, :] = kv[part]
                q_ref[at, :] = product[part, :HEAD]


def projected(where, rows, near, far):
    width = rows[0].shape[1]
    n = 4 * rows[0].shape[0]
    whole = pl.BlockSpec(memory_space=pltpu.VMEM)
    return pl.pallas_call(
        project_kernel,
        out_shape=(
            jax.ShapeDtypeStruct((n, 2 * HEAD), bf16),
            jax.ShapeDtypeStruct((n, HEAD), f32),
            jax.ShapeDtypeStruct((4, 8, n // 4), f32),
        ),
        in_specs=[pl.BlockSpec(memory_space=pltpu.SMEM)] + [whole] * 7,
        out_specs=(whole, whole, whole),
        scratch_shapes=[pltpu.VMEM((width, 4 * HEAD), bf16)],
        compiler_params=pltpu.CompilerParams(vmem_limit_bytes=40 << 20),
    )(where, *rows, near, far)


def body(
    tokens,
    fine_gain,
    fine_query,
    fine_keyval,
    fine_out,
    down_weight,
    coarse_gain,
    coarse_query,
    coarse_keyval,
    coarse_out,
    up_weight,
):
    width = tokens.shape[1]
    wide = coarse_gain.shape[0]
    cols = coarse_query.shape[1]
    yh, z, x, yl, c = (lax.axis_index(a) for a in ALL)
    y = yh * 2 + yl
    s, t = lax.axis_index(SEQ), lax.axis_index(TP)
    n_seq, n_tp = lax.axis_size(SEQ), lax.axis_size(TP)
    swap = [(b * n_tp + a, a * n_tp + b) for a in range(n_seq) for b in range(n_tp)]

    normed = normalize(tokens.astype(f32), fine_gain).astype(bf16)
    earlier_rows = from_behind(normed, ALL, 1)

    with jax.named_scope("weights"):
        out_sent = lax.dynamic_slice(coarse_out, (0, s * cols), (cols, cols))
        sent = (coarse_query, coarse_keyval[:, 0], coarse_keyval[:, 1], out_sent)
        sent = gate(jnp.concatenate(sent, 0), normed)
        pack = lax.ppermute(sent, ALL, swap)

    fine_state, pooled = fine_layer(
        tokens, normed, earlier_rows, fine_query, fine_keyval, fine_out
    )
    run_count = tokens.shape[0] // SHORT

    with jax.named_scope("gather_rows"):
        across = rotated(pooled, "z", 4)
        pair = jnp.where(z < 4, jnp.stack([pooled, across]), jnp.stack([across, pooled]))
        around = [pair] + [rotated(pair, "z", by) for by in (7, 6, 1)]
        around = jnp.stack(around + around[:3])
        z_rows = lax.dynamic_slice_in_dim(around, (4 - z % 4) % 4, 4, 0).reshape(-1, width)
        y_rows = around_four(z_rows, ("yh", "yl"))

    with jax.named_scope("weights"):
        gain = lax.dynamic_slice(coarse_gain, (t * cols,), (cols,))[:, None]
        direct_at = 128 * z + 64 * yh
        where = [c, 128 * z, direct_at, direct_at + 32, x, yl]
        where = jnp.stack(where).astype(jnp.int32)
        ones = jnp.ones((cols, 1), f32)
        pack = gate(pack, pair).astype(f32) * jnp.concatenate([gain] * 3 + [ones], 0)
        pack = gate(pack.astype(bf16), z_rows)
        give, keep = weight_products(where, down_weight, up_weight, pack)
        got = rotated(give, "c", 1)
        both = [keep[i].astype(f32) + got[i].astype(f32) for i in range(4)]
        total = both[0]
        for by in (1, 3, 2):
            total = total + rotated(both[by].astype(bf16), "x", by).astype(f32)
        piece = (total[0] + rotated(total[1].astype(bf16), "yl", 1).astype(f32)).astype(bf16)
        near_half = gathered(gate(piece, tuple(y_rows)), ("x",))
        far_half = rotated(near_half, "c", 1)
        lifts = near_half[:, 4 * HEAD :], far_half[:, 4 * HEAD :]
        summed = jnp.concatenate(
            [jnp.where(c == 0, lifts[0], lifts[1]), jnp.where(c == 0, lifts[1], lifts[0])], 0
        )
        second = jnp.swapaxes(summed, 0, 1).reshape(-1, width)
        below, above = rotated(second, ("yh", "yl"), 1), rotated(second, ("yh", "yl"), 3)
        seconds = [second, below, rotated(below, ("yh", "yl"), 1), above]

    with jax.named_scope("project"):
        where = jnp.stack([c, 128 * z, y]).astype(jnp.int32)
        kv, q, squares = projected(where, y_rows, near_half, far_half)
        n = kv.shape[0]

        def in_order(parts):
            twice = jnp.concatenate([parts, parts[:3]], 0)
            return lax.dynamic_slice_in_dim(twice, (4 - y) % 4, 4, 0)

        def by_row(values):
            parts = in_order(values.reshape(4, 8, run_count, -1))
            parts = parts.reshape(2, 2, 4, 2, run_count, -1)
            return jnp.transpose(parts, (0, 3, 2, 1, 4, 5)).reshape(n, -1)

        near = [kv] + [rotated(kv, "x", by) for by in (3, 2, 1)]
        squares = squares[:, 0].reshape(n)
        squares = jnp.sum(gathered(squares[None], ("z",)), axis=(0, 1))
        inverse = by_row(lax.rsqrt(jnp.maximum(squares, 0.0) / wide + epsilon))
        factor = math.log2(math.e) / math.sqrt(HEAD)
        q = (q * (inverse * factor)).astype(bf16)
        every_inverse = gathered(inverse.reshape(1, n), ("x", "c")).reshape(8, n)

    with jax.named_scope("attention"):
        chunks, places, sources = [], [], []
        for by in (0, 1, 3, 2):
            mine = near[by]
            other = rotated(mine, "c", 1)
            source = (x + by) % 4
            shift = 128 * (source - x)
            chunks += [mine, other]
            places += [shift, shift + 32 * (1 - 2 * c)]
            sources += [2 * source + c, 2 * source + 1 - c]
        places = jnp.stack(places + sources).astype(jnp.int32)
        q = gate(q, (below, above))
        heads = coarse_attention(q, every_inverse, chunks, places)

    with jax.named_scope("lift"):
        heads = jnp.swapaxes(heads.reshape(2, 8, 2, run_count, HEAD), 1, 2)
        heads = heads.reshape(4, 8 * run_count, HEAD)
        slot = lax.dynamic_slice(z_rows, (0, 128 * z), (8 * run_count, 128))
        slot = slot.reshape(4, 2, run_count, 4, 32)
        slots = jnp.transpose(slot, (3, 1, 0, 2, 4)).reshape(4, 8 * run_count, 32)
        total = None
        for by in range(4):
            part = lax.dynamic_index_in_dim(heads, (y + by) % 4, 0, keepdims=False)
            if by:
                part = rotated(part, ("yh", "yl"), by)
            slot = lax.dynamic_index_in_dim(slots, (y + 4 - by) % 4, 0, keepdims=False)
            product = dot(jnp.concatenate([part, slot], 1), seconds[by])
            total = product if total is None else total + product
        lifted = exchanged(total.astype(bf16).reshape(8, run_count, width), ("z",))
        lifted = jnp.sum(lifted.astype(f32), axis=0)
        before = from_behind(lifted[run_count - 1 :], ALL, 1)
        lifted = jnp.concatenate([before, lifted[: run_count - 1]], 0)
        result = fine_state.astype(f32) + jnp.repeat(lifted, SHORT, axis=0)
    return result.astype(bf16)


def solution(mesh):
    fine = Mesh(mesh.devices.reshape(2, 8, 4, 2, 2), ALL)
    return jax.shard_map(
        body,
        mesh=fine,
        in_specs=(
            P(ALL, None),
            P(),
            P(),
            P(),
            P(),
            P(None, TP),
            P(),
            P(SEQ, TP),
            P(SEQ, None, TP),
            P(TP, None),
            P(TP, None),
        ),
        out_specs=P(ALL, None),
        check_vma=False,
    )
```

```python
import functools
import math

import jax
import jax.numpy as jnp
from jax import lax
from jax.experimental import pallas as pl
from jax.experimental.pallas import tpu as pltpu
from jax.sharding import Mesh, PartitionSpec as P

HEAD = 128
WINDOW = 256
SHORT = 8

epsilon = 1e-06
big_negative = -1e30

ALL = ("yh", "z", "x", "yl", "c")
SEQ = ("yh", "z")
TP = ("x", "yl", "c")
f32 = jnp.float32
bf16 = jnp.bfloat16


def from_behind(array, axis, by):
    size = lax.axis_size(axis)
    pairs = [(i, i + by) for i in range(size) if 0 <= i + by < size]
    return lax.ppermute(array, axis, pairs)


def rotated(array, axis, by):
    size = lax.axis_size(axis)
    return lax.ppermute(array, axis, [(i, (i + by) % size) for i in range(size)])


def around_four(array, axes):
    above, below = rotated(array, axes, 3), rotated(array, axes, 1)
    half = array.shape[0] // 2
    top, bottom = rotated(above[:half], axes, 3), rotated(below[half:], axes, 1)
    return [array, above, top, bottom, below]


def gathered(array, axes):
    copies = jnp.broadcast_to(array, (lax.axis_size(axes), *array.shape))
    return lax.all_to_all(copies, axes, split_axis=0, concat_axis=0, tiled=True)


def exchanged(pieces, axes):
    return lax.all_to_all(pieces, axes, split_axis=0, concat_axis=0, tiled=True)


def normalize(values, scale_gain):
    mean_square = jnp.mean(values * values, axis=-1, keepdims=True)
    return values * lax.rsqrt(mean_square + epsilon) * scale_gain


def dot(a, b):
    return jnp.dot(a, b, preferred_element_type=f32)


def fine_kernel(
    first_ref, tokens_ref, normed_ref, before_ref, query_ref, key_ref, value_ref, out_ref,
    state_ref, pooled_ref, total_ref,
):
    rows = tokens_ref.shape[0]
    step = pl.program_id(0)

    @pl.when(step == 0)
    def _():
        total_ref[...] = tokens_ref[...].astype(f32)

    normed, before = normed_ref[...], before_ref[...]
    factor = math.log2(math.e) / math.sqrt(HEAD)
    query = dot(normed, query_ref[...]).astype(bf16)
    key, value = key_ref[...], value_ref[...]
    keys = jnp.concatenate([dot(before, key).astype(bf16), dot(normed, key).astype(bf16)], 0)
    values = jnp.concatenate([dot(before, value).astype(bf16), dot(normed, value).astype(bf16)], 0)
    row = lax.broadcasted_iota(jnp.int32, (rows, 2 * rows), 0)
    col = lax.broadcasted_iota(jnp.int32, (rows, 2 * rows), 1)
    allowed = (col > row) & (col <= row + WINDOW) & (col >= first_ref[0])
    heads = []
    for k in range(query.shape[1] // HEAD):
        lanes = slice(k * HEAD, (k + 1) * HEAD)
        scores = lax.dot_general(
            query[:, lanes], keys[:, lanes], (((1,), (1,)), ((), ())), preferred_element_type=f32
        )
        scores = jnp.where(allowed, scores * factor, big_negative)
        terms = jnp.exp2(scores - jnp.max(scores, axis=-1, keepdims=True))
        denom = jnp.sum(terms, axis=-1, keepdims=True)
        heads.append((dot(terms.astype(bf16), values[:, lanes]) / denom).astype(bf16))
    total_ref[...] += dot(jnp.concatenate(heads, 1), out_ref[...])

    @pl.when(step == pl.num_programs(0) - 1)
    def _():
        state = total_ref[...].astype(bf16)
        state_ref[...] = state
        runs = state.astype(f32).reshape(rows // SHORT, SHORT, state.shape[1])
        pooled_ref[...] = (jnp.sum(runs, axis=1) * (1.0 / SHORT)).astype(bf16)


def in_hbm(array):
    return pltpu.with_memory_space_constraint(array, pltpu.MemorySpace.HBM)


def fine_layer(tokens, normed, before, fine_query, fine_keyval, fine_out):
    rows, width = tokens.shape
    pair = 2 * HEAD
    steps = width // pair
    whole = pl.BlockSpec((rows, width), lambda i: (0, 0))
    first = jnp.where(lax.axis_index(ALL) == 0, rows, 0).astype(jnp.int32).reshape(1)
    return pl.pallas_call(
        fine_kernel,
        out_shape=(
            jax.ShapeDtypeStruct((rows, width), bf16),
            jax.ShapeDtypeStruct((rows // SHORT, width), bf16),
        ),
        grid=(steps,),
        in_specs=[pl.BlockSpec(memory_space=pltpu.SMEM), whole, whole, whole]
        + [
            pl.BlockSpec((width, pair), lambda i: (0, i)),
            pl.BlockSpec((width, pair), lambda i: (0, i)),
            pl.BlockSpec((width, pair), lambda i: (0, steps + i)),
            pl.BlockSpec((pair, width), lambda i: (i, 0)),
        ],
        out_specs=(whole, pl.BlockSpec((rows // SHORT, width), lambda i: (0, 0))),
        scratch_shapes=[pltpu.VMEM((rows, width), f32)],
        compiler_params=pltpu.CompilerParams(vmem_limit_bytes=40 << 20),
    )(first, tokens, normed, before, *[in_hbm(w) for w in (fine_query, fine_keyval, fine_keyval, fine_out)])


def attention_kernel(place_ref, q_ref, inverse_ref, *refs):
    chunks, out_ref = refs[:-1], refs[-1]
    tile = q_ref.shape[0]
    step = pl.program_id(0)
    q = q_ref[...]
    row = step * tile + lax.broadcasted_iota(jnp.int32, (tile, tile), 0)
    col = step * tile + lax.broadcasted_iota(jnp.int32, (tile, tile), 1)

    def position(index):
        return (index >> 6) * 512 + ((index >> 5) & 1) * 64 + (index & 31)

    ahead = position(row) - position(col)

    def update(kt, state, masked):
        peak, total, acc = state
        rows = pl.ds(pl.multiple_of(kt * tile, tile), tile)
        inverses, scores = [], []
        for j, chunk in enumerate(chunks):
            s = lax.dot_general(
                q, chunk[rows, :HEAD], (((1,), (1,)), ((), ())), preferred_element_type=f32
            )
            inverses.append(inverse_ref[pl.ds(place_ref[len(chunks) + j], 1), rows])
            s = s * inverses[j]
            scores.append(jnp.where(ahead >= place_ref[j], s, big_negative) if masked else s)
        top = functools.reduce(jnp.maximum, scores)
        new_peak = jnp.maximum(peak, jnp.max(top, axis=-1, keepdims=True))
        fade = jnp.exp2(peak - new_peak)
        acc = acc * fade
        sums = None
        for j, chunk in enumerate(chunks):
            p = jnp.exp2(scores[j] - new_peak)
            sums = p if sums is None else sums + p
            acc = acc + dot((p * inverses[j]).astype(bf16), chunk[rows, HEAD:])
        total = total * fade + jnp.sum(sums, axis=-1, keepdims=True)
        return new_peak, total, acc

    state = (
        jnp.full((tile, 1), big_negative, f32),
        jnp.zeros((tile, 1), f32),
        jnp.zeros((tile, HEAD), f32),
    )
    state = lax.fori_loop(0, step, lambda kt, st: update(kt, st, False), state)
    _, total, acc = update(step, state, True)
    out_ref[...] = (acc / total).astype(bf16)


def coarse_attention(q, inverses, chunks, places, tile=256):
    rows = q.shape[0]
    whole = pl.BlockSpec(chunks[0].shape, lambda i, place: (0, 0))
    return pl.pallas_call(
        attention_kernel,
        out_shape=jax.ShapeDtypeStruct((rows, HEAD), bf16),
        grid_spec=pltpu.PrefetchScalarGridSpec(
            num_scalar_prefetch=1,
            grid=(rows // tile,),
            in_specs=[
                pl.BlockSpec((tile, HEAD), lambda i, place: (i, 0)),
                pl.BlockSpec(inverses.shape, lambda i, place: (0, 0)),
            ]
            + [whole] * len(chunks),
            out_specs=pl.BlockSpec((tile, HEAD), lambda i, place: (i, 0)),
        ),
        compiler_params=pltpu.CompilerParams(vmem_limit_bytes=48 << 20),
    )(places, q, inverses, *chunks)


def gate(array, earlier):
    return lax.optimization_barrier((array, earlier))[0]


def product_kernel(where_ref, down_ref, up_ref, pack_ref, give_ref, keep_ref):
    core, gram_at = where_ref[0], where_ref[1]
    cols = pack_ref.shape[1]
    scaled = [pack_ref[j * cols : (j + 1) * cols, :] for j in range(3)]
    gram_rows = down_ref[pl.ds(pl.multiple_of(gram_at, 128), 128), :]
    right, left = [], []
    for k in range(2):
        lanes = slice(k * HEAD, (k + 1) * HEAD)
        right.append(jnp.concatenate([w[:, lanes] for w in scaled], 1))
        direct = down_ref[pl.ds(pl.multiple_of(where_ref[2 + k], 32), 32), :]
        start = 3 * cols + k * HEAD
        left.append(jnp.concatenate([pack_ref[start : start + HEAD, :], direct], 0))
    half = down_ref.shape[0] // 2
    for out_ref, side in ((give_ref, 1 - core), (keep_ref, core)):
        rows = pl.ds(pl.multiple_of(side * half, half), half)
        one, two = down_ref[rows, :], up_ref[:, rows]
        gram = lax.dot_general(
            one, gram_rows, (((1,), (1,)), ((), ())), preferred_element_type=f32
        ).astype(bf16)
        for k in range(2):
            proj = dot(one, right[k]).astype(bf16)
            lift = dot(left[k], two).astype(bf16)
            head = (k + where_ref[5]) % 2
            for q in range(4):
                block = slice(q * 128, (q + 1) * 128)
                at = (q + 4 - where_ref[4]) % 4
                for j in range(3):
                    lanes = slice(j * 128, (j + 1) * 128)
                    out_ref[at, head, lanes, :] = proj[block, lanes]
                out_ref[at, head, 3 * 128 : 4 * 128, :] = gram[block]
                out_ref[at, head, 4 * 128 :, :] = lift[:, block]


def weight_products(where, down, up, pack):
    width = down.shape[0]
    out = jax.ShapeDtypeStruct((4, 2, 4 * 128 + HEAD + 32, width // 8), bf16)
    whole = pl.BlockSpec(memory_space=pltpu.VMEM)
    return pl.pallas_call(
        product_kernel,
        out_shape=(out, out),
        in_specs=[pl.BlockSpec(memory_space=pltpu.SMEM)] + [whole] * 3,
        out_specs=(whole, whole),
        compiler_params=pltpu.CompilerParams(vmem_limit_bytes=40 << 20),
    )(where, down, up, pack)


def project_kernel(
    where_ref, own_ref, above_ref, top_ref, bottom_ref, below_ref, near_ref, far_ref,
    kv_ref, q_ref, squares_ref, weight_ref,
):
    core, slot_at, y = where_ref[0], where_ref[1], where_ref[2]
    half = weight_ref.shape[0] // 2
    for side, piece_ref in ((core, near_ref), (1 - core, far_ref)):
        for x in range(4):
            rows = pl.ds(pl.multiple_of(side * half + x * 128, 128), 128)
            for j in range(4):
                lanes = slice(j * 128, (j + 1) * 128)
                weight_ref[rows, lanes] = piece_ref[x, lanes, :]
    weight = weight_ref[...]
    ones = jnp.ones((8, 128), f32)
    opposite = jnp.concatenate([top_ref[...], bottom_ref[...]], 0)
    lanes = pl.ds(pl.multiple_of(slot_at, 128), 128)
    opposite_slot = jnp.concatenate([top_ref[:, lanes], bottom_ref[:, lanes]], 0)
    groups = (
        (own_ref[...], own_ref[:, lanes]),
        (above_ref[...], above_ref[:, lanes]),
        (opposite, opposite_slot),
        (below_ref[...], below_ref[:, lanes]),
    )
    for i, (rows, slot) in enumerate(groups):
        product = dot(rows, weight)
        squares = product[:, 3 * HEAD :] * slot.astype(f32)
        squares_ref[i] = lax.dot_general(
            ones,
            squares,
            (((1,), (1,)), ((), ())),
            precision=lax.Precision.HIGHEST,
            preferred_element_type=f32,
        )
        kv = product[:, HEAD : 3 * HEAD].astype(bf16)
        source = (y + i) % 4
        start = (source // 2) * 512 + (source % 2) * 32
        for a in range(4):
            for h in range(2):
                at = pl.ds(pl.multiple_of(start + (h * 4 + a) * 64, 32), 32)
                part = slice((a * 2 + h) * 32, (a * 2 + h) * 32 + 32)
                kv_ref[at, :] = kv[part]
                q_ref[at, :] = product[part, :HEAD]


def projected(where, rows, near, far):
    width = rows[0].shape[1]
    n = 4 * rows[0].shape[0]
    whole = pl.BlockSpec(memory_space=pltpu.VMEM)
    return pl.pallas_call(
        project_kernel,
        out_shape=(
            jax.ShapeDtypeStruct((n, 2 * HEAD), bf16),
            jax.ShapeDtypeStruct((n, HEAD), f32),
            jax.ShapeDtypeStruct((4, 8, n // 4), f32),
        ),
        in_specs=[pl.BlockSpec(memory_space=pltpu.SMEM)] + [whole] * 7,
        out_specs=(whole, whole, whole),
        scratch_shapes=[pltpu.VMEM((width, 4 * HEAD), bf16)],
        compiler_params=pltpu.CompilerParams(vmem_limit_bytes=40 << 20),
    )(where, *rows, near, far)


def body(
    tokens,
    fine_gain,
    fine_query,
    fine_keyval,
    fine_out,
    down_weight,
    coarse_gain,
    coarse_query,
    coarse_keyval,
    coarse_out,
    up_weight,
):
    width = tokens.shape[1]
    wide = coarse_gain.shape[0]
    cols = coarse_query.shape[1]
    yh, z, x, yl, c = (lax.axis_index(a) for a in ALL)
    y = yh * 2 + yl
    s, t = lax.axis_index(SEQ), lax.axis_index(TP)
    n_seq, n_tp = lax.axis_size(SEQ), lax.axis_size(TP)
    swap = [(b * n_tp + a, a * n_tp + b) for a in range(n_seq) for b in range(n_tp)]

    normed = normalize(tokens.astype(f32), fine_gain).astype(bf16)
    earlier_rows = from_behind(normed, ALL, 1)

    with jax.named_scope("weights"):
        out_sent = lax.dynamic_slice(coarse_out, (0, s * cols), (cols, cols))
        sent = (coarse_query, coarse_keyval[:, 0], coarse_keyval[:, 1], out_sent)
        sent = gate(jnp.concatenate(sent, 0), normed)
        pack = lax.ppermute(sent, ALL, swap)

    fine_state, pooled = fine_layer(
        tokens, normed, earlier_rows, fine_query, fine_keyval, fine_out
    )
    run_count = tokens.shape[0] // SHORT

    with jax.named_scope("gather_rows"):
        across = rotated(pooled, "z", 4)
        pair = jnp.where(z < 4, jnp.stack([pooled, across]), jnp.stack([across, pooled]))
        around = [pair] + [rotated(pair, "z", by) for by in (7, 6, 1)]
        around = jnp.stack(around + around[:3])
        z_rows = lax.dynamic_slice_in_dim(around, (4 - z % 4) % 4, 4, 0).reshape(-1, width)
        y_rows = around_four(z_rows, ("yh", "yl"))

    with jax.named_scope("weights"):
        gain = lax.dynamic_slice(coarse_gain, (t * cols,), (cols,))[:, None]
        direct_at = 128 * z + 64 * yh
        where = [c, 128 * z, direct_at, direct_at + 32, x, yl]
        where = jnp.stack(where).astype(jnp.int32)
        ones = jnp.ones((cols, 1), f32)
        pack = gate(pack, pair).astype(f32) * jnp.concatenate([gain] * 3 + [ones], 0)
        pack = gate(pack.astype(bf16), z_rows)
        give, keep = weight_products(where, down_weight, up_weight, pack)
        got = rotated(give, "c", 1)
        both = [keep[i].astype(f32) + got[i].astype(f32) for i in range(4)]
        total = both[0]
        for by in (1, 3, 2):
            total = total + rotated(both[by].astype(bf16), "x", by).astype(f32)
        piece = (total[0] + rotated(total[1].astype(bf16), "yl", 1).astype(f32)).astype(bf16)
        near_half = gathered(gate(piece, tuple(y_rows)), ("x",))
        far_half = rotated(near_half, "c", 1)
        lifts = near_half[:, 4 * HEAD :], far_half[:, 4 * HEAD :]
        summed = jnp.concatenate(
            [jnp.where(c == 0, lifts[0], lifts[1]), jnp.where(c == 0, lifts[1], lifts[0])], 0
        )
        second = jnp.swapaxes(summed, 0, 1).reshape(-1, width)
        below, above = rotated(second, ("yh", "yl"), 1), rotated(second, ("yh", "yl"), 3)
        seconds = [second, below, rotated(below, ("yh", "yl"), 1), above]

    with jax.named_scope("project"):
        where = jnp.stack([c, 128 * z, y]).astype(jnp.int32)
        kv, q, squares = projected(where, y_rows, near_half, far_half)
        n = kv.shape[0]

        def in_order(parts):
            twice = jnp.concatenate([parts, parts[:3]], 0)
            return lax.dynamic_slice_in_dim(twice, (4 - y) % 4, 4, 0)

        def by_row(values):
            parts = in_order(values.reshape(4, 8, run_count, -1))
            parts = parts.reshape(2, 2, 4, 2, run_count, -1)
            return jnp.transpose(parts, (0, 3, 2, 1, 4, 5)).reshape(n, -1)

        near = [kv] + [rotated(kv, "x", by) for by in (3, 2, 1)]
        squares = squares[:, 0].reshape(n)
        squares = jnp.sum(gathered(squares[None], ("z",)), axis=(0, 1))
        inverse = by_row(lax.rsqrt(jnp.maximum(squares, 0.0) / wide + epsilon))
        factor = math.log2(math.e) / math.sqrt(HEAD)
        q = (q * (inverse * factor)).astype(bf16)
        every_inverse = gathered(gate(inverse, below).reshape(1, n), ("x", "c")).reshape(8, n)

    with jax.named_scope("attention"):
        chunks, places, sources = [], [], []
        for by in (0, 1, 3, 2):
            mine = near[by] if by == 0 else gate(near[by], every_inverse)
            other = rotated(mine, "c", 1)
            source = (x + by) % 4
            shift = 128 * (source - x)
            chunks += [mine, other]
            places += [shift, shift + 32 * (1 - 2 * c)]
            sources += [2 * source + c, 2 * source + 1 - c]
        places = jnp.stack(places + sources).astype(jnp.int32)
        heads = coarse_attention(q, every_inverse, chunks, places)

    with jax.named_scope("lift"):
        heads = jnp.swapaxes(heads.reshape(2, 8, 2, run_count, HEAD), 1, 2)
        heads = heads.reshape(4, 8 * run_count, HEAD)
        slot = lax.dynamic_slice(gate(z_rows, kv), (0, 128 * z), (8 * run_count, 128))
        slot = slot.reshape(4, 2, run_count, 4, 32)
        slots = jnp.transpose(slot, (3, 1, 0, 2, 4)).reshape(4, 8 * run_count, 32)
        total = None
        for by in range(4):
            part = lax.dynamic_index_in_dim(heads, (y + by) % 4, 0, keepdims=False)
            if by:
                part = rotated(part, ("yh", "yl"), by)
            slot = lax.dynamic_index_in_dim(slots, (y + 4 - by) % 4, 0, keepdims=False)
            product = dot(jnp.concatenate([part, slot], 1), seconds[by])
            total = product if total is None else total + product
        lifted = exchanged(total.astype(bf16).reshape(8, run_count, width), ("z",))
        lifted = jnp.sum(lifted.astype(f32), axis=0)
        before = from_behind(lifted[run_count - 1 :], ALL, 1)
        lifted = jnp.concatenate([before, lifted[: run_count - 1]], 0)
        result = fine_state.astype(f32) + jnp.repeat(lifted, SHORT, axis=0)
    return result.astype(bf16)


def solution(mesh):
    fine = Mesh(mesh.devices.reshape(2, 8, 4, 2, 2), ALL)
    return jax.shard_map(
        body,
        mesh=fine,
        in_specs=(
            P(ALL, None),
            P(),
            P(),
            P(),
            P(),
            P(None, TP),
            P(),
            P(SEQ, TP),
            P(SEQ, None, TP),
            P(TP, None),
            P(TP, None),
        ),
        out_specs=P(ALL, None),
        check_vma=False,
    )
```

```python
import functools
import math

import jax
import jax.numpy as jnp
from jax import lax
from jax.experimental import pallas as pl
from jax.experimental.pallas import tpu as pltpu
from jax.sharding import Mesh, PartitionSpec as P

HEAD = 128
WINDOW = 256
SHORT = 8

epsilon = 1e-06
big_negative = -1e30

ALL = ("yh", "z", "x", "yl", "c")
SEQ = ("yh", "z")
TP = ("x", "yl", "c")
f32 = jnp.float32
bf16 = jnp.bfloat16


def from_behind(array, axis, by):
    size = lax.axis_size(axis)
    pairs = [(i, i + by) for i in range(size) if 0 <= i + by < size]
    return lax.ppermute(array, axis, pairs)


def rotated(array, axis, by):
    size = lax.axis_size(axis)
    return lax.ppermute(array, axis, [(i, (i + by) % size) for i in range(size)])


def around_four(array, axes):
    above, below = rotated(array, axes, 3), rotated(array, axes, 1)
    half = array.shape[0] // 2
    top, bottom = rotated(above[:half], axes, 3), rotated(below[half:], axes, 1)
    return [array, above, top, bottom, below]


def gathered(array, axes):
    copies = jnp.broadcast_to(array, (lax.axis_size(axes), *array.shape))
    return lax.all_to_all(copies, axes, split_axis=0, concat_axis=0, tiled=True)


def exchanged(pieces, axes):
    return lax.all_to_all(pieces, axes, split_axis=0, concat_axis=0, tiled=True)


def normalize(values, scale_gain):
    mean_square = jnp.mean(values * values, axis=-1, keepdims=True)
    return values * lax.rsqrt(mean_square + epsilon) * scale_gain


def dot(a, b):
    return jnp.dot(a, b, preferred_element_type=f32)


def fine_kernel(
    first_ref, tokens_ref, normed_ref, before_ref, query_ref, key_ref, value_ref, out_ref,
    state_ref, pooled_ref, total_ref,
):
    rows = tokens_ref.shape[0]
    step = pl.program_id(0)

    @pl.when(step == 0)
    def _():
        total_ref[...] = tokens_ref[...].astype(f32)

    normed, before = normed_ref[...], before_ref[...]
    factor = math.log2(math.e) / math.sqrt(HEAD)
    query = dot(normed, query_ref[...]).astype(bf16)
    key, value = key_ref[...], value_ref[...]
    keys = jnp.concatenate([dot(before, key).astype(bf16), dot(normed, key).astype(bf16)], 0)
    values = jnp.concatenate([dot(before, value).astype(bf16), dot(normed, value).astype(bf16)], 0)
    row = lax.broadcasted_iota(jnp.int32, (rows, 2 * rows), 0)
    col = lax.broadcasted_iota(jnp.int32, (rows, 2 * rows), 1)
    allowed = (col > row) & (col <= row + WINDOW) & (col >= first_ref[0])
    heads = []
    for k in range(query.shape[1] // HEAD):
        lanes = slice(k * HEAD, (k + 1) * HEAD)
        scores = lax.dot_general(
            query[:, lanes], keys[:, lanes], (((1,), (1,)), ((), ())), preferred_element_type=f32
        )
        scores = jnp.where(allowed, scores * factor, big_negative)
        terms = jnp.exp2(scores - jnp.max(scores, axis=-1, keepdims=True))
        denom = jnp.sum(terms, axis=-1, keepdims=True)
        heads.append((dot(terms.astype(bf16), values[:, lanes]) / denom).astype(bf16))
    total_ref[...] += dot(jnp.concatenate(heads, 1), out_ref[...])

    @pl.when(step == pl.num_programs(0) - 1)
    def _():
        state = total_ref[...].astype(bf16)
        state_ref[...] = state
        runs = state.astype(f32).reshape(rows // SHORT, SHORT, state.shape[1])
        pooled_ref[...] = (jnp.sum(runs, axis=1) * (1.0 / SHORT)).astype(bf16)


def in_hbm(array):
    return pltpu.with_memory_space_constraint(array, pltpu.MemorySpace.HBM)


def fine_layer(tokens, normed, before, fine_query, fine_keyval, fine_out):
    rows, width = tokens.shape
    pair = 2 * HEAD
    steps = width // pair
    whole = pl.BlockSpec((rows, width), lambda i: (0, 0))
    first = jnp.where(lax.axis_index(ALL) == 0, rows, 0).astype(jnp.int32).reshape(1)
    return pl.pallas_call(
        fine_kernel,
        out_shape=(
            jax.ShapeDtypeStruct((rows, width), bf16),
            jax.ShapeDtypeStruct((rows // SHORT, width), bf16),
        ),
        grid=(steps,),
        in_specs=[pl.BlockSpec(memory_space=pltpu.SMEM), whole, whole, whole]
        + [
            pl.BlockSpec((width, pair), lambda i: (0, i)),
            pl.BlockSpec((width, pair), lambda i: (0, i)),
            pl.BlockSpec((width, pair), lambda i: (0, steps + i)),
            pl.BlockSpec((pair, width), lambda i: (i, 0)),
        ],
        out_specs=(whole, pl.BlockSpec((rows // SHORT, width), lambda i: (0, 0))),
        scratch_shapes=[pltpu.VMEM((rows, width), f32)],
        compiler_params=pltpu.CompilerParams(vmem_limit_bytes=40 << 20),
    )(first, tokens, normed, before, *[in_hbm(w) for w in (fine_query, fine_keyval, fine_keyval, fine_out)])


def attention_kernel(place_ref, q_ref, inverse_ref, *refs):
    chunks, out_ref = refs[:-1], refs[-1]
    tile = q_ref.shape[0]
    step = pl.program_id(0)
    q = q_ref[...]
    row = step * tile + lax.broadcasted_iota(jnp.int32, (tile, tile), 0)
    col = step * tile + lax.broadcasted_iota(jnp.int32, (tile, tile), 1)

    def position(index):
        return (index >> 6) * 512 + ((index >> 5) & 1) * 64 + (index & 31)

    ahead = position(row) - position(col)

    def update(kt, state, masked):
        peak, total, acc = state
        rows = pl.ds(pl.multiple_of(kt * tile, tile), tile)
        inverses, scores = [], []
        for j, chunk in enumerate(chunks):
            s = lax.dot_general(
                q, chunk[rows, :HEAD], (((1,), (1,)), ((), ())), preferred_element_type=f32
            )
            inverses.append(inverse_ref[pl.ds(place_ref[len(chunks) + j], 1), rows])
            s = s * inverses[j]
            scores.append(jnp.where(ahead >= place_ref[j], s, big_negative) if masked else s)
        top = functools.reduce(jnp.maximum, scores)
        new_peak = jnp.maximum(peak, jnp.max(top, axis=-1, keepdims=True))
        fade = jnp.exp2(peak - new_peak)
        acc = acc * fade
        sums = None
        for j, chunk in enumerate(chunks):
            p = jnp.exp2(scores[j] - new_peak)
            sums = p if sums is None else sums + p
            acc = acc + dot((p * inverses[j]).astype(bf16), chunk[rows, HEAD:])
        total = total * fade + jnp.sum(sums, axis=-1, keepdims=True)
        return new_peak, total, acc

    state = (
        jnp.full((tile, 1), big_negative, f32),
        jnp.zeros((tile, 1), f32),
        jnp.zeros((tile, HEAD), f32),
    )
    state = lax.fori_loop(0, step, lambda kt, st: update(kt, st, False), state)
    _, total, acc = update(step, state, True)
    out_ref[...] = (acc / total).astype(bf16)


def coarse_attention(q, inverses, chunks, places, tile=256):
    rows = q.shape[0]
    whole = pl.BlockSpec(chunks[0].shape, lambda i, place: (0, 0))
    return pl.pallas_call(
        attention_kernel,
        out_shape=jax.ShapeDtypeStruct((rows, HEAD), bf16),
        grid_spec=pltpu.PrefetchScalarGridSpec(
            num_scalar_prefetch=1,
            grid=(rows // tile,),
            in_specs=[
                pl.BlockSpec((tile, HEAD), lambda i, place: (i, 0)),
                pl.BlockSpec(inverses.shape, lambda i, place: (0, 0)),
            ]
            + [whole] * len(chunks),
            out_specs=pl.BlockSpec((tile, HEAD), lambda i, place: (i, 0)),
        ),
        compiler_params=pltpu.CompilerParams(vmem_limit_bytes=48 << 20),
    )(places, q, inverses, *chunks)


def gate(array, earlier):
    return lax.optimization_barrier((array, earlier))[0]


def product_kernel(where_ref, down_ref, up_ref, pack_ref, give_ref, keep_ref):
    core, gram_at = where_ref[0], where_ref[1]
    cols = pack_ref.shape[1]
    scaled = [pack_ref[j * cols : (j + 1) * cols, :] for j in range(3)]
    gram_rows = down_ref[pl.ds(pl.multiple_of(gram_at, 128), 128), :]
    right, left = [], []
    for k in range(2):
        lanes = slice(k * HEAD, (k + 1) * HEAD)
        right.append(jnp.concatenate([w[:, lanes] for w in scaled], 1))
        direct = down_ref[pl.ds(pl.multiple_of(where_ref[2 + k], 32), 32), :]
        start = 3 * cols + k * HEAD
        left.append(jnp.concatenate([pack_ref[start : start + HEAD, :], direct], 0))
    half = down_ref.shape[0] // 2
    for out_ref, side in ((give_ref, 1 - core), (keep_ref, core)):
        rows = pl.ds(pl.multiple_of(side * half, half), half)
        one, two = down_ref[rows, :], up_ref[:, rows]
        gram = lax.dot_general(
            one, gram_rows, (((1,), (1,)), ((), ())), preferred_element_type=f32
        ).astype(bf16)
        for k in range(2):
            proj = dot(one, right[k]).astype(bf16)
            lift = dot(left[k], two).astype(bf16)
            head = (k + where_ref[5]) % 2
            for q in range(4):
                block = slice(q * 128, (q + 1) * 128)
                at = (q + 4 - where_ref[4]) % 4
                for j in range(3):
                    lanes = slice(j * 128, (j + 1) * 128)
                    out_ref[at, head, lanes, :] = proj[block, lanes]
                out_ref[at, head, 3 * 128 : 4 * 128, :] = gram[block]
                out_ref[at, head, 4 * 128 :, :] = lift[:, block]


def weight_products(where, down, up, pack):
    width = down.shape[0]
    out = jax.ShapeDtypeStruct((4, 2, 4 * 128 + HEAD + 32, width // 8), bf16)
    whole = pl.BlockSpec(memory_space=pltpu.VMEM)
    return pl.pallas_call(
        product_kernel,
        out_shape=(out, out),
        in_specs=[pl.BlockSpec(memory_space=pltpu.SMEM)] + [whole] * 3,
        out_specs=(whole, whole),
        compiler_params=pltpu.CompilerParams(vmem_limit_bytes=40 << 20),
    )(where, down, up, pack)


def project_kernel(
    where_ref, own_ref, above_ref, top_ref, bottom_ref, below_ref, near_ref, far_ref,
    kv_ref, q_ref, squares_ref, slots_ref, weight_ref,
):
    core, slot_at, y = where_ref[0], where_ref[1], where_ref[2]
    half = weight_ref.shape[0] // 2
    for side, piece_ref in ((core, near_ref), (1 - core, far_ref)):
        for x in range(4):
            rows = pl.ds(pl.multiple_of(side * half + x * 128, 128), 128)
            for j in range(4):
                lanes = slice(j * 128, (j + 1) * 128)
                weight_ref[rows, lanes] = piece_ref[x, lanes, :]
    weight = weight_ref[...]
    ones = jnp.ones((8, 128), f32)
    opposite = jnp.concatenate([top_ref[...], bottom_ref[...]], 0)
    lanes = pl.ds(pl.multiple_of(slot_at, 128), 128)
    opposite_slot = jnp.concatenate([top_ref[:, lanes], bottom_ref[:, lanes]], 0)
    groups = (
        (own_ref[...], own_ref[:, lanes]),
        (above_ref[...], above_ref[:, lanes]),
        (opposite, opposite_slot),
        (below_ref[...], below_ref[:, lanes]),
    )
    own_slot = own_ref[:, lanes]
    for k in range(4):
        for a in range(4):
            for h in range(2):
                at = slice((h * 4 + a) * 32, (h * 4 + a) * 32 + 32)
                part = slice((a * 2 + h) * 32, (a * 2 + h) * 32 + 32)
                slots_ref[(y + 4 - k) % 4, at, :] = own_slot[part, 32 * k : 32 * k + 32]
    for i, (rows, slot) in enumerate(groups):
        product = dot(rows, weight)
        squares = product[:, 3 * HEAD :] * slot.astype(f32)
        squares_ref[i] = lax.dot_general(
            ones,
            squares,
            (((1,), (1,)), ((), ())),
            precision=lax.Precision.HIGHEST,
            preferred_element_type=f32,
        )
        kv = product[:, HEAD : 3 * HEAD].astype(bf16)
        source = (y + i) % 4
        start = (source // 2) * 512 + (source % 2) * 32
        for a in range(4):
            for h in range(2):
                at = pl.ds(pl.multiple_of(start + (h * 4 + a) * 64, 32), 32)
                part = slice((a * 2 + h) * 32, (a * 2 + h) * 32 + 32)
                kv_ref[at, :] = kv[part]
                q_ref[at, :] = product[part, :HEAD]


def projected(where, rows, near, far):
    width = rows[0].shape[1]
    n = 4 * rows[0].shape[0]
    whole = pl.BlockSpec(memory_space=pltpu.VMEM)
    return pl.pallas_call(
        project_kernel,
        out_shape=(
            jax.ShapeDtypeStruct((n, 2 * HEAD), bf16),
            jax.ShapeDtypeStruct((n, HEAD), f32),
            jax.ShapeDtypeStruct((4, 8, n // 4), f32),
            jax.ShapeDtypeStruct((4, n // 4, 32), bf16),
        ),
        in_specs=[pl.BlockSpec(memory_space=pltpu.SMEM)] + [whole] * 7,
        out_specs=(whole, whole, whole, whole),
        scratch_shapes=[pltpu.VMEM((width, 4 * HEAD), bf16)],
        compiler_params=pltpu.CompilerParams(vmem_limit_bytes=40 << 20),
    )(where, *rows, near, far)


def body(
    tokens,
    fine_gain,
    fine_query,
    fine_keyval,
    fine_out,
    down_weight,
    coarse_gain,
    coarse_query,
    coarse_keyval,
    coarse_out,
    up_weight,
):
    width = tokens.shape[1]
    wide = coarse_gain.shape[0]
    cols = coarse_query.shape[1]
    yh, z, x, yl, c = (lax.axis_index(a) for a in ALL)
    y = yh * 2 + yl
    s, t = lax.axis_index(SEQ), lax.axis_index(TP)
    n_seq, n_tp = lax.axis_size(SEQ), lax.axis_size(TP)
    swap = [(b * n_tp + a, a * n_tp + b) for a in range(n_seq) for b in range(n_tp)]

    normed = normalize(tokens.astype(f32), fine_gain).astype(bf16)
    earlier_rows = from_behind(normed, ALL, 1)

    with jax.named_scope("weights"):
        out_sent = lax.dynamic_slice(coarse_out, (0, s * cols), (cols, cols))
        sent = (coarse_query, coarse_keyval[:, 0], coarse_keyval[:, 1], out_sent)
        sent = gate(jnp.concatenate(sent, 0), normed)
        pack = lax.ppermute(sent, ALL, swap)

    fine_state, pooled = fine_layer(
        tokens, normed, earlier_rows, fine_query, fine_keyval, fine_out
    )
    run_count = tokens.shape[0] // SHORT

    with jax.named_scope("gather_rows"):
        across = rotated(pooled, "z", 4)
        pair = jnp.where(z < 4, jnp.stack([pooled, across]), jnp.stack([across, pooled]))
        around = [pair] + [rotated(pair, "z", by) for by in (7, 6, 1)]
        around = jnp.stack(around + around[:3])
        z_rows = lax.dynamic_slice_in_dim(around, (4 - z % 4) % 4, 4, 0).reshape(-1, width)
        y_rows = around_four(z_rows, ("yh", "yl"))

    with jax.named_scope("weights"):
        gain = lax.dynamic_slice(coarse_gain, (t * cols,), (cols,))[:, None]
        direct_at = 128 * z + 64 * yh
        where = [c, 128 * z, direct_at, direct_at + 32, x, yl]
        where = jnp.stack(where).astype(jnp.int32)
        ones = jnp.ones((cols, 1), f32)
        pack = gate(pack, pair).astype(f32) * jnp.concatenate([gain] * 3 + [ones], 0)
        pack = gate(pack.astype(bf16), z_rows)
        give, keep = weight_products(where, down_weight, up_weight, pack)
        got = rotated(give, "c", 1)
        both = [keep[i].astype(f32) + got[i].astype(f32) for i in range(4)]
        total = both[0]
        for by in (1, 3, 2):
            total = total + rotated(both[by].astype(bf16), "x", by).astype(f32)
        piece = (total[0] + rotated(total[1].astype(bf16), "yl", 1).astype(f32)).astype(bf16)
        near_half = gathered(gate(piece, tuple(y_rows)), ("x",))
        far_half = rotated(near_half, "c", 1)
        lifts = near_half[:, 4 * HEAD :], far_half[:, 4 * HEAD :]
        summed = jnp.concatenate(
            [jnp.where(c == 0, lifts[0], lifts[1]), jnp.where(c == 0, lifts[1], lifts[0])], 0
        )
        second = jnp.swapaxes(summed, 0, 1).reshape(-1, width)
        below, above = rotated(second, ("yh", "yl"), 1), rotated(second, ("yh", "yl"), 3)
        seconds = [second, below, rotated(below, ("yh", "yl"), 1), above]

    with jax.named_scope("project"):
        where = jnp.stack([c, 128 * z, y]).astype(jnp.int32)
        kv, q, squares, slots = projected(where, y_rows, near_half, far_half)
        n = kv.shape[0]

        def in_order(parts):
            twice = jnp.concatenate([parts, parts[:3]], 0)
            return lax.dynamic_slice_in_dim(twice, (4 - y) % 4, 4, 0)

        def by_row(values):
            parts = in_order(values.reshape(4, 8, run_count, -1))
            parts = parts.reshape(2, 2, 4, 2, run_count, -1)
            return jnp.transpose(parts, (0, 3, 2, 1, 4, 5)).reshape(n, -1)

        near = [kv] + [rotated(kv, "x", by) for by in (3, 2, 1)]
        squares = squares[:, 0].reshape(n)
        squares = jnp.sum(gathered(squares[None], ("z",)), axis=(0, 1))
        inverse = by_row(lax.rsqrt(jnp.maximum(squares, 0.0) / wide + epsilon))
        factor = math.log2(math.e) / math.sqrt(HEAD)
        q = (q * (inverse * factor)).astype(bf16)
        every_inverse = gathered(gate(inverse, (below, q)).reshape(1, n), ("x", "c")).reshape(8, n)

    with jax.named_scope("attention"):
        chunks, places, sources = [], [], []
        for by in (0, 1, 3, 2):
            mine = near[by] if by == 0 else gate(near[by], every_inverse)
            other = rotated(mine, "c", 1)
            source = (x + by) % 4
            shift = 128 * (source - x)
            chunks += [mine, other]
            places += [shift, shift + 32 * (1 - 2 * c)]
            sources += [2 * source + c, 2 * source + 1 - c]
        places = jnp.stack(places + sources).astype(jnp.int32)
        heads = coarse_attention(q, every_inverse, chunks, places)

    with jax.named_scope("lift"):
        heads = jnp.swapaxes(heads.reshape(2, 8, 2, run_count, HEAD), 1, 2)
        heads = heads.reshape(4, 8 * run_count, HEAD)
        total = None
        for by in range(4):
            part = lax.dynamic_index_in_dim(heads, (y + by) % 4, 0, keepdims=False)
            if by:
                part = rotated(part, ("yh", "yl"), by)
            product = dot(jnp.concatenate([part, slots[by]], 1), seconds[by])
            total = product if total is None else total + product
        lifted = exchanged(total.astype(bf16).reshape(8, run_count, width), ("z",))
        lifted = jnp.sum(lifted.astype(f32), axis=0)
        before = from_behind(lifted[run_count - 1 :], ALL, 1)
        lifted = jnp.concatenate([before, lifted[: run_count - 1]], 0)
        result = fine_state.astype(f32) + jnp.repeat(lifted, SHORT, axis=0)
    return result.astype(bf16)


def solution(mesh):
    fine = Mesh(mesh.devices.reshape(2, 8, 4, 2, 2), ALL)
    return jax.shard_map(
        body,
        mesh=fine,
        in_specs=(
            P(ALL, None),
            P(),
            P(),
            P(),
            P(),
            P(None, TP),
            P(),
            P(SEQ, TP),
            P(SEQ, None, TP),
            P(TP, None),
            P(TP, None),
        ),
        out_specs=P(ALL, None),
        check_vma=False,
    )
```

```python
import functools
import math

import jax
import jax.numpy as jnp
from jax import lax
from jax.experimental import pallas as pl
from jax.experimental.pallas import tpu as pltpu
from jax.sharding import Mesh, PartitionSpec as P

HEAD = 128
WINDOW = 256
SHORT = 8

epsilon = 1e-06
big_negative = -1e30

ALL = ("yh", "z", "x", "yl", "c")
SEQ = ("yh", "z")
TP = ("x", "yl", "c")
f32 = jnp.float32
bf16 = jnp.bfloat16


def from_behind(array, axis, by):
    size = lax.axis_size(axis)
    pairs = [(i, i + by) for i in range(size) if 0 <= i + by < size]
    return lax.ppermute(array, axis, pairs)


def rotated(array, axis, by):
    size = lax.axis_size(axis)
    return lax.ppermute(array, axis, [(i, (i + by) % size) for i in range(size)])


def around_four(array, axes):
    above, below = rotated(array, axes, 3), rotated(array, axes, 1)
    half = array.shape[0] // 2
    top, bottom = rotated(above[:half], axes, 3), rotated(below[half:], axes, 1)
    return [array, above, top, bottom, below]


def gathered(array, axes):
    copies = jnp.broadcast_to(array, (lax.axis_size(axes), *array.shape))
    return lax.all_to_all(copies, axes, split_axis=0, concat_axis=0, tiled=True)


def exchanged(pieces, axes):
    return lax.all_to_all(pieces, axes, split_axis=0, concat_axis=0, tiled=True)


def normalize(values, scale_gain):
    mean_square = jnp.mean(values * values, axis=-1, keepdims=True)
    return values * lax.rsqrt(mean_square + epsilon) * scale_gain


def dot(a, b):
    return jnp.dot(a, b, preferred_element_type=f32)


def fine_kernel(
    first_ref, tokens_ref, normed_ref, before_ref, query_ref, key_ref, value_ref, out_ref,
    state_ref, pooled_ref, total_ref,
):
    rows = tokens_ref.shape[0]
    step = pl.program_id(0)

    @pl.when(step == 0)
    def _():
        total_ref[...] = tokens_ref[...].astype(f32)

    normed, before = normed_ref[...], before_ref[...]
    factor = math.log2(math.e) / math.sqrt(HEAD)
    query = dot(normed, query_ref[...]).astype(bf16)
    key, value = key_ref[...], value_ref[...]
    keys = jnp.concatenate([dot(before, key).astype(bf16), dot(normed, key).astype(bf16)], 0)
    values = jnp.concatenate([dot(before, value).astype(bf16), dot(normed, value).astype(bf16)], 0)
    row = lax.broadcasted_iota(jnp.int32, (rows, 2 * rows), 0)
    col = lax.broadcasted_iota(jnp.int32, (rows, 2 * rows), 1)
    allowed = (col > row) & (col <= row + WINDOW) & (col >= first_ref[0])
    heads = []
    for k in range(query.shape[1] // HEAD):
        lanes = slice(k * HEAD, (k + 1) * HEAD)
        scores = lax.dot_general(
            query[:, lanes], keys[:, lanes], (((1,), (1,)), ((), ())), preferred_element_type=f32
        )
        scores = jnp.where(allowed, scores * factor, big_negative)
        terms = jnp.exp2(scores - jnp.max(scores, axis=-1, keepdims=True))
        denom = jnp.sum(terms, axis=-1, keepdims=True)
        heads.append((dot(terms.astype(bf16), values[:, lanes]) / denom).astype(bf16))
    total_ref[...] += dot(jnp.concatenate(heads, 1), out_ref[...])

    @pl.when(step == pl.num_programs(0) - 1)
    def _():
        state = total_ref[...].astype(bf16)
        state_ref[...] = state
        runs = state.astype(f32).reshape(rows // SHORT, SHORT, state.shape[1])
        pooled_ref[...] = (jnp.sum(runs, axis=1) * (1.0 / SHORT)).astype(bf16)


def in_hbm(array):
    return pltpu.with_memory_space_constraint(array, pltpu.MemorySpace.HBM)


def fine_layer(tokens, normed, before, fine_query, fine_keyval, fine_out):
    rows, width = tokens.shape
    pair = 2 * HEAD
    steps = width // pair
    whole = pl.BlockSpec((rows, width), lambda i: (0, 0))
    first = jnp.where(lax.axis_index(ALL) == 0, rows, 0).astype(jnp.int32).reshape(1)
    return pl.pallas_call(
        fine_kernel,
        out_shape=(
            jax.ShapeDtypeStruct((rows, width), bf16),
            jax.ShapeDtypeStruct((rows // SHORT, width), bf16),
        ),
        grid=(steps,),
        in_specs=[pl.BlockSpec(memory_space=pltpu.SMEM), whole, whole, whole]
        + [
            pl.BlockSpec((width, pair), lambda i: (0, i)),
            pl.BlockSpec((width, pair), lambda i: (0, i)),
            pl.BlockSpec((width, pair), lambda i: (0, steps + i)),
            pl.BlockSpec((pair, width), lambda i: (i, 0)),
        ],
        out_specs=(whole, pl.BlockSpec((rows // SHORT, width), lambda i: (0, 0))),
        scratch_shapes=[pltpu.VMEM((rows, width), f32)],
        compiler_params=pltpu.CompilerParams(vmem_limit_bytes=40 << 20),
    )(first, tokens, normed, before, *[in_hbm(w) for w in (fine_query, fine_keyval, fine_keyval, fine_out)])


def attention_kernel(place_ref, q_ref, inverse_ref, *refs):
    chunks, out_ref = refs[:-1], refs[-1]
    tile = q_ref.shape[0]
    step = pl.program_id(0)
    q = q_ref[...]
    row = step * tile + lax.broadcasted_iota(jnp.int32, (tile, tile), 0)
    col = step * tile + lax.broadcasted_iota(jnp.int32, (tile, tile), 1)

    def position(index):
        return (index >> 6) * 512 + ((index >> 5) & 1) * 64 + (index & 31)

    ahead = position(row) - position(col)

    def update(kt, state, masked):
        peak, total, acc = state
        rows = pl.ds(pl.multiple_of(kt * tile, tile), tile)
        inverses, scores = [], []
        for j, chunk in enumerate(chunks):
            s = lax.dot_general(
                q, chunk[rows, :HEAD], (((1,), (1,)), ((), ())), preferred_element_type=f32
            )
            inverses.append(inverse_ref[pl.ds(place_ref[len(chunks) + j], 1), rows])
            s = s * inverses[j]
            scores.append(jnp.where(ahead >= place_ref[j], s, big_negative) if masked else s)
        top = functools.reduce(jnp.maximum, scores)
        new_peak = jnp.maximum(peak, jnp.max(top, axis=-1, keepdims=True))
        fade = jnp.exp2(peak - new_peak)
        acc = acc * fade
        sums = None
        for j, chunk in enumerate(chunks):
            p = jnp.exp2(scores[j] - new_peak)
            sums = p if sums is None else sums + p
            acc = acc + dot((p * inverses[j]).astype(bf16), chunk[rows, HEAD:])
        total = total * fade + jnp.sum(sums, axis=-1, keepdims=True)
        return new_peak, total, acc

    state = (
        jnp.full((tile, 1), big_negative, f32),
        jnp.zeros((tile, 1), f32),
        jnp.zeros((tile, HEAD), f32),
    )
    state = lax.fori_loop(0, step, lambda kt, st: update(kt, st, False), state)
    _, total, acc = update(step, state, True)
    out_ref[...] = (acc / total).astype(bf16)


def coarse_attention(q, inverses, chunks, places, tile=256):
    rows = q.shape[0]
    whole = pl.BlockSpec(chunks[0].shape, lambda i, place: (0, 0))
    return pl.pallas_call(
        attention_kernel,
        out_shape=jax.ShapeDtypeStruct((rows, HEAD), bf16),
        grid_spec=pltpu.PrefetchScalarGridSpec(
            num_scalar_prefetch=1,
            grid=(rows // tile,),
            in_specs=[
                pl.BlockSpec((tile, HEAD), lambda i, place: (i, 0)),
                pl.BlockSpec(inverses.shape, lambda i, place: (0, 0)),
            ]
            + [whole] * len(chunks),
            out_specs=pl.BlockSpec((tile, HEAD), lambda i, place: (i, 0)),
        ),
        compiler_params=pltpu.CompilerParams(vmem_limit_bytes=48 << 20),
    )(places, q, inverses, *chunks)


def gate(array, earlier):
    return lax.optimization_barrier((array, earlier))[0]


def product_kernel(where_ref, down_ref, up_ref, pack_ref, give_ref, keep_ref):
    core, gram_at = where_ref[0], where_ref[1]
    cols = pack_ref.shape[1]
    scaled = [pack_ref[j * cols : (j + 1) * cols, :] for j in range(3)]
    gram_rows = down_ref[pl.ds(pl.multiple_of(gram_at, 128), 128), :]
    right, left = [], []
    for k in range(2):
        lanes = slice(k * HEAD, (k + 1) * HEAD)
        right.append(jnp.concatenate([w[:, lanes] for w in scaled], 1))
        direct = down_ref[pl.ds(pl.multiple_of(where_ref[2 + k], 32), 32), :]
        start = 3 * cols + k * HEAD
        left.append(jnp.concatenate([pack_ref[start : start + HEAD, :], direct], 0))
    half = down_ref.shape[0] // 2
    for out_ref, side in ((give_ref, 1 - core), (keep_ref, core)):
        rows = pl.ds(pl.multiple_of(side * half, half), half)
        one, two = down_ref[rows, :], up_ref[:, rows]
        gram = lax.dot_general(
            one, gram_rows, (((1,), (1,)), ((), ())), preferred_element_type=f32
        ).astype(bf16)
        for k in range(2):
            proj = dot(one, right[k]).astype(bf16)
            lift = dot(left[k], two).astype(bf16)
            head = (k + where_ref[5]) % 2
            for q in range(4):
                block = slice(q * 128, (q + 1) * 128)
                at = (q + 4 - where_ref[4]) % 4
                for j in range(3):
                    lanes = slice(j * 128, (j + 1) * 128)
                    out_ref[at, head, lanes, :] = proj[block, lanes]
                out_ref[at, head, 3 * 128 : 4 * 128, :] = gram[block]
                out_ref[at, head, 4 * 128 :, :] = lift[:, block]


def weight_products(where, down, up, pack):
    width = down.shape[0]
    out = jax.ShapeDtypeStruct((4, 2, 4 * 128 + HEAD + 32, width // 8), bf16)
    whole = pl.BlockSpec(memory_space=pltpu.VMEM)
    return pl.pallas_call(
        product_kernel,
        out_shape=(out, out),
        in_specs=[pl.BlockSpec(memory_space=pltpu.SMEM)] + [whole] * 3,
        out_specs=(whole, whole),
        compiler_params=pltpu.CompilerParams(vmem_limit_bytes=40 << 20),
    )(where, down, up, pack)


def project_kernel(
    where_ref, own_ref, above_ref, top_ref, bottom_ref, below_ref, near_ref, far_ref,
    kv_ref, q_ref, squares_ref, slots_ref, weight_ref,
):
    core, slot_at, y = where_ref[0], where_ref[1], where_ref[2]
    half = weight_ref.shape[0] // 2
    for side, piece_ref in ((core, near_ref), (1 - core, far_ref)):
        for x in range(4):
            rows = pl.ds(pl.multiple_of(side * half + x * 128, 128), 128)
            for j in range(4):
                lanes = slice(j * 128, (j + 1) * 128)
                weight_ref[rows, lanes] = piece_ref[x, lanes, :]
    weight = weight_ref[...]
    ones = jnp.ones((8, 128), f32)
    opposite = jnp.concatenate([top_ref[...], bottom_ref[...]], 0)
    lanes = pl.ds(pl.multiple_of(slot_at, 128), 128)
    opposite_slot = jnp.concatenate([top_ref[:, lanes], bottom_ref[:, lanes]], 0)
    groups = (
        (own_ref[...], own_ref[:, lanes]),
        (above_ref[...], above_ref[:, lanes]),
        (opposite, opposite_slot),
        (below_ref[...], below_ref[:, lanes]),
    )
    own_slot = own_ref[:, lanes]
    for k in range(4):
        for a in range(4):
            for h in range(2):
                at = slice((h * 4 + a) * 32, (h * 4 + a) * 32 + 32)
                part = slice((a * 2 + h) * 32, (a * 2 + h) * 32 + 32)
                slots_ref[(y + 4 - k) % 4, at, :] = own_slot[part, 32 * k : 32 * k + 32]
    for i, (rows, slot) in enumerate(groups):
        product = dot(rows, weight)
        squares = product[:, 3 * HEAD :] * slot.astype(f32)
        squares_ref[i] = lax.dot_general(
            ones,
            squares,
            (((1,), (1,)), ((), ())),
            precision=lax.Precision.HIGHEST,
            preferred_element_type=f32,
        )
        kv = product[:, HEAD : 3 * HEAD].astype(bf16)
        source = (y + i) % 4
        start = (source // 2) * 512 + (source % 2) * 32
        for a in range(4):
            for h in range(2):
                at = pl.ds(pl.multiple_of(start + (h * 4 + a) * 64, 32), 32)
                part = slice((a * 2 + h) * 32, (a * 2 + h) * 32 + 32)
                kv_ref[at, :] = kv[part]
                q_ref[at, :] = product[part, :HEAD]


def projected(where, rows, near, far):
    width = rows[0].shape[1]
    n = 4 * rows[0].shape[0]
    whole = pl.BlockSpec(memory_space=pltpu.VMEM)
    return pl.pallas_call(
        project_kernel,
        out_shape=(
            jax.ShapeDtypeStruct((n, 2 * HEAD), bf16),
            jax.ShapeDtypeStruct((n, HEAD), f32),
            jax.ShapeDtypeStruct((4, 8, n // 4), f32),
            jax.ShapeDtypeStruct((4, n // 4, 32), bf16),
        ),
        in_specs=[pl.BlockSpec(memory_space=pltpu.SMEM)] + [whole] * 7,
        out_specs=(whole, whole, whole, whole),
        scratch_shapes=[pltpu.VMEM((width, 4 * HEAD), bf16)],
        compiler_params=pltpu.CompilerParams(vmem_limit_bytes=40 << 20),
    )(where, *[in_hbm(r) for r in rows], near, far)


def body(
    tokens,
    fine_gain,
    fine_query,
    fine_keyval,
    fine_out,
    down_weight,
    coarse_gain,
    coarse_query,
    coarse_keyval,
    coarse_out,
    up_weight,
):
    width = tokens.shape[1]
    wide = coarse_gain.shape[0]
    cols = coarse_query.shape[1]
    yh, z, x, yl, c = (lax.axis_index(a) for a in ALL)
    y = yh * 2 + yl
    s, t = lax.axis_index(SEQ), lax.axis_index(TP)
    n_seq, n_tp = lax.axis_size(SEQ), lax.axis_size(TP)
    swap = [(b * n_tp + a, a * n_tp + b) for a in range(n_seq) for b in range(n_tp)]

    normed = normalize(tokens.astype(f32), fine_gain).astype(bf16)
    earlier_rows = from_behind(normed, ALL, 1)

    with jax.named_scope("weights"):
        out_sent = lax.dynamic_slice(coarse_out, (0, s * cols), (cols, cols))
        sent = (coarse_query, coarse_keyval[:, 0], coarse_keyval[:, 1], out_sent)
        sent = gate(jnp.concatenate(sent, 0), normed)
        pack = lax.ppermute(sent, ALL, swap)

    fine_state, pooled = fine_layer(
        tokens, normed, earlier_rows, fine_query, fine_keyval, fine_out
    )
    run_count = tokens.shape[0] // SHORT

    with jax.named_scope("gather_rows"):
        across = rotated(pooled, "z", 4)
        pair = jnp.where(z < 4, jnp.stack([pooled, across]), jnp.stack([across, pooled]))
        around = [pair] + [rotated(pair, "z", by) for by in (7, 6, 1)]
        around = jnp.stack(around + around[:3])
        z_rows = lax.dynamic_slice_in_dim(around, (4 - z % 4) % 4, 4, 0).reshape(-1, width)
        y_rows = around_four(z_rows, ("yh", "yl"))

    with jax.named_scope("weights"):
        gain = lax.dynamic_slice(coarse_gain, (t * cols,), (cols,))[:, None]
        direct_at = 128 * z + 64 * yh
        where = [c, 128 * z, direct_at, direct_at + 32, x, yl]
        where = jnp.stack(where).astype(jnp.int32)
        ones = jnp.ones((cols, 1), f32)
        pack = gate(pack, pair).astype(f32) * jnp.concatenate([gain] * 3 + [ones], 0)
        pack = gate(pack.astype(bf16), z_rows)
        give, keep = weight_products(where, down_weight, up_weight, pack)
        got = rotated(give, "c", 1)
        both = [keep[i].astype(f32) + got[i].astype(f32) for i in range(4)]
        total = both[0]
        for by in (1, 3, 2):
            total = total + rotated(both[by].astype(bf16), "x", by).astype(f32)
        piece = (total[0] + rotated(total[1].astype(bf16), "yl", 1).astype(f32)).astype(bf16)
        near_half = gathered(gate(piece, tuple(y_rows)), ("x",))
        far_half = rotated(near_half, "c", 1)
        lifts = near_half[:, 4 * HEAD :], far_half[:, 4 * HEAD :]
        summed = jnp.concatenate(
            [jnp.where(c == 0, lifts[0], lifts[1]), jnp.where(c == 0, lifts[1], lifts[0])], 0
        )
        second = jnp.swapaxes(summed, 0, 1).reshape(-1, width)
        below, above = rotated(second, ("yh", "yl"), 1), rotated(second, ("yh", "yl"), 3)
        seconds = [second, below, rotated(below, ("yh", "yl"), 1), above]

    with jax.named_scope("project"):
        where = jnp.stack([c, 128 * z, y]).astype(jnp.int32)
        kv, q, squares, slots = projected(where, y_rows, near_half, far_half)
        n = kv.shape[0]

        def in_order(parts):
            twice = jnp.concatenate([parts, parts[:3]], 0)
            return lax.dynamic_slice_in_dim(twice, (4 - y) % 4, 4, 0)

        def by_row(values):
            parts = in_order(values.reshape(4, 8, run_count, -1))
            parts = parts.reshape(2, 2, 4, 2, run_count, -1)
            return jnp.transpose(parts, (0, 3, 2, 1, 4, 5)).reshape(n, -1)

        near = [kv] + [rotated(kv, "x", by) for by in (3, 2, 1)]
        squares = squares[:, 0].reshape(n)
        squares = jnp.sum(gathered(squares[None], ("z",)), axis=(0, 1))
        inverse = by_row(lax.rsqrt(jnp.maximum(squares, 0.0) / wide + epsilon))
        factor = math.log2(math.e) / math.sqrt(HEAD)
        q = (q * (inverse * factor)).astype(bf16)
        every_inverse = gathered(gate(inverse, (below, q)).reshape(1, n), ("x", "c")).reshape(8, n)

    with jax.named_scope("attention"):
        chunks, places, sources = [], [], []
        for by in (0, 1, 3, 2):
            mine = near[by] if by == 0 else gate(near[by], every_inverse)
            other = rotated(mine, "c", 1)
            source = (x + by) % 4
            shift = 128 * (source - x)
            chunks += [mine, other]
            places += [shift, shift + 32 * (1 - 2 * c)]
            sources += [2 * source + c, 2 * source + 1 - c]
        places = jnp.stack(places + sources).astype(jnp.int32)
        heads = coarse_attention(q, every_inverse, chunks, places)

    with jax.named_scope("lift"):
        heads = jnp.swapaxes(heads.reshape(2, 8, 2, run_count, HEAD), 1, 2)
        heads = heads.reshape(4, 8 * run_count, HEAD)
        total = None
        for by in range(4):
            part = lax.dynamic_index_in_dim(heads, (y + by) % 4, 0, keepdims=False)
            if by:
                part = rotated(part, ("yh", "yl"), by)
            product = dot(jnp.concatenate([part, slots[by]], 1), seconds[by])
            total = product if total is None else total + product
        lifted = exchanged(total.astype(bf16).reshape(8, run_count, width), ("z",))
        lifted = jnp.sum(lifted.astype(f32), axis=0)
        before = from_behind(lifted[run_count - 1 :], ALL, 1)
        lifted = jnp.concatenate([before, lifted[: run_count - 1]], 0)
        result = fine_state.astype(f32) + jnp.repeat(lifted, SHORT, axis=0)
    return result.astype(bf16)


def solution(mesh):
    fine = Mesh(mesh.devices.reshape(2, 8, 4, 2, 2), ALL)
    return jax.shard_map(
        body,
        mesh=fine,
        in_specs=(
            P(ALL, None),
            P(),
            P(),
            P(),
            P(),
            P(None, TP),
            P(),
            P(SEQ, TP),
            P(SEQ, None, TP),
            P(TP, None),
            P(TP, None),
        ),
        out_specs=P(ALL, None),
        check_vma=False,
    )
```
